128 devices in a mesh: lat: 8 (over x, core), lon: 16 (over y, z).
Axes of the slice: x: 4, y: 4, z: 4, core: 2. Of those that a mesh axis runs over, the one named last changes fastest.
Arguments:
- tracers: float32 [1024, 1152, 256], P(('lat', 'lon')), may hold values from 0.1 to 3
- phys_fine: bfloat16 [384, 6144, 144], P('lat', 'lon'), may hold values from -2 to 30, as said below
- mix_coarse: bfloat16 [128, 2048, 48], P('lat', 'lon'), may hold values from 0.0049743652 to 0.19921875
- surf_light: float32 [384, 6144], P('lat', 'lon'), may hold values from 0.5 to 4
- land_mask: int32 [128, 2048], P('lat', 'lon'), may hold values from 0 to 1, as said below
- owner_map: int32 [8, 128], P('lat'), may hold values from -1 to 1023, as said below
Outputs:
- tracers_out: float32 [1024, 1152, 256], P(('lat', 'lon'))
- heating: bfloat16 [48, 384, 6144], P(None, 'lat', 'lon')
The draws below stay inside these ranges and needn't reach their ends.
Inputs may be any that keep to these rules, and one draw needn't show every extreme that they name: `owner_map`: -1 marks a block whose columns are all land, any other value is the slot that holds the block. Slots are numbered band by band, 128 to a band, owner by owner within a band with 8 slots each, and a block's slot lies in its own band. Every band has a multiple of 16 wet blocks. The wet blocks of a band, taken in order of longitude, are held by the owners in turn: the next wet block after one held by owner o is held by owner o + 1 (after 16 - 1 comes 0), also from the band's last wet block to its first; the r-th wet block of a band (from 0) lies in slot r // 16 of its owner. In some band every slot holds a block. `land_mask`: 1 for an ocean column, 0 for land; every column of a block that owner_map marks -1 is land. `phys_fine`: channel c * 48 + l holds level l of: c = 0 the eastward velocity on a fine cell's east face and c = 1 the northward velocity on its north face, as fractions of a cell per step within -0.15 to 0.15; c = 2 temperature within -2 to 30.
All inputs are finite; a program needn't handle non-finite values.
Results may differ from the reference program's by a relative error of at most 0.001.
Values sent between devices are 32-bit elements; how exact they have to be, the bound alone decides.
A program may use at most 192 MiB of HBM per device.

```python
import math
from functools import partial
import jax
import jax.numpy as jnp
from jax import lax

NTR = 24
NLEV = 48
BLK = 16
CF = 3
BPD = 8
ITERS = 2
NBY = 8
NBX = 128
NYC = 128
NXC = 2048
NYF = 384
NXF = 6144
WETMAX = 128
SLOTS = 1024


def band_layout(key):
    base_key = jax.random.fold_in(key, 7)
    count_key, pick_key, turn_key, order_key, column_key = jax.random.split(base_key, 5)
    owner_count = WETMAX // BPD
    lowest = max(1, BPD - BPD // 4)
    wet_counts = owner_count * jax.random.randint(count_key, (NBY,), lowest, BPD + 1)
    full_band = jax.random.randint(pick_key, (), 0, NBY)
    wet_counts = jnp.where(jnp.arange(NBY) == full_band, WETMAX, wet_counts)
    order_keys = jax.random.split(order_key, NBY)

    def inverse_order(row_key):
        return jnp.argsort(jax.random.permutation(row_key, NBX))
    orders = jax.vmap(inverse_order)(order_keys)
    wet_blocks = orders < wet_counts[:, None]
    wet_ranks = jnp.cumsum(wet_blocks.astype(jnp.int32), axis=1) - 1
    shifts = jax.random.randint(turn_key, (NBY, 1), 0, owner_count)
    owners = (wet_ranks + shifts) % owner_count
    slot_codes = (jnp.arange(NBY)[:, None] * owner_count + owners) * BPD + wet_ranks // owner_count
    owner_table = jnp.where(wet_blocks, slot_codes, -1).astype(jnp.int32)
    column_bits = jax.random.randint(column_key, (NBY * BLK, NBX * BLK), 0, 8) < 7
    block_wet = jnp.repeat(jnp.repeat(wet_blocks, BLK, axis=0), BLK, axis=1)
    land_cells = (column_bits & block_wet).astype(jnp.int32)
    return (owner_table, land_cells)


def draw_owner_map(key, part):
    return band_layout(key)[0]


def draw_land_mask(key, part):
    return band_layout(key)[1]


def draw_phys_fine(key, part):
    sub_keys = jax.random.split(jax.random.fold_in(key, 3), 3)
    cell_shape = (NYF, NXF, NLEV)
    east_flow = jax.random.uniform(sub_keys[0], cell_shape, minval=-0.15, maxval=0.15)
    north_flow = jax.random.uniform(sub_keys[1], cell_shape, minval=-0.15, maxval=0.15)
    warmth = jax.random.uniform(sub_keys[2], cell_shape, minval=-2.0, maxval=30.0)
    return jnp.concatenate([east_flow, north_flow, warmth], axis=2).astype(jnp.bfloat16)


def level_of(key, shape, shards, low, high):
    factor_of, own = 1.0, jax.random.fold_in(key, 6)
    for dim, blocks in shards:
        steps = jnp.exp(jax.random.uniform(jax.random.fold_in(own, dim), (blocks,), jnp.float32, low / len(shards), high / len(shards)))
        factor_of = factor_of * jnp.repeat(steps, shape[dim] // blocks).reshape([-1 if axis == dim else 1 for axis in range(len(shape))])
    return factor_of


def setup_inputs(seed: int = 0) -> dict:
    arg_keys = jax.random.split(jax.random.key(seed), 7)
    tracers = jnp.clip(jnp.exp(math.log(3.0) - 3.4011974 * jax.random.uniform(arg_keys[0], (SLOTS, NTR * NLEV, BLK * BLK), jnp.float32) ** level_of(arg_keys[0], (SLOTS, NTR * NLEV, BLK * BLK), ((0, 128),), -0.2, 0.2)), 0.1, 3.0)
    phys_fine = draw_phys_fine(jax.random.fold_in(arg_keys[6], 71), 0)
    mix_coarse = jnp.clip(jnp.exp(math.log(0.19921875) - 3.6901057 * jax.random.uniform(arg_keys[2], (NYC, NXC, NLEV), jnp.float32) ** level_of(arg_keys[2], (NYC, NXC, NLEV), ((0, 8), (1, 16)), -0.2, 0.2)), 0.0049743652, 0.19921875).astype(jnp.bfloat16)
    surf_light = jnp.clip(jnp.exp(math.log(4.0) - 2.0794415 * jax.random.uniform(arg_keys[3], (NYF, NXF), jnp.float32) ** level_of(arg_keys[3], (NYF, NXF), ((0, 8), (1, 16)), -0.2, 0.2)), 0.5, 4.0)
    land_mask = draw_land_mask(jax.random.fold_in(arg_keys[6], 71), 0)
    owner_map = draw_owner_map(jax.random.fold_in(arg_keys[6], 71), 0)
    return {"tracers": tracers, "phys_fine": phys_fine, "mix_coarse": mix_coarse, "surf_light": surf_light, "land_mask": land_mask, "owner_map": owner_map}


diffuse_rate = 0.08
nano_chl_index = 10
diat_chl_index = 11


def positive(value):
    return jnp.maximum(value, 0.0)


def strict_upper(levels):
    level_ids = jnp.arange(levels)
    return (level_ids[:, None] < level_ids[None, :]).astype(jnp.float32)


def depth_sums(absorb, levels):
    flat_rows = absorb.reshape(-1, levels)
    summed = jnp.dot(flat_rows, strict_upper(levels), precision=lax.Precision.HIGHEST, preferred_element_type=jnp.float32)
    return summed.reshape(absorb.shape)


def coarsen(fine_band, light_fine, levels, factor):
    row_count = fine_band.shape[0] // factor
    col_count = fine_band.shape[1] // factor
    fine_grid = fine_band.reshape(row_count, factor, col_count, factor, 3, levels)
    east_face = jnp.mean(fine_grid[:, :, :, factor - 1, 0, :].astype(jnp.float32), axis=1)
    north_face = jnp.mean(fine_grid[:, factor - 1, :, :, 1, :].astype(jnp.float32), axis=2)
    temp_mean = jnp.mean(fine_grid[:, :, :, :, 2, :].astype(jnp.float32), axis=(1, 3))
    light_mean = jnp.mean(light_fine.reshape(row_count, factor, col_count, factor), axis=(1, 3))
    return east_face, north_face, temp_mean, light_mean


def open_faces(east_face, north_face, wet_cells, wet_north, wet_east):
    open_east = wet_cells * jnp.concatenate([wet_cells[:, 1:], wet_east[:, None]], axis=1)
    open_north = wet_cells * jnp.concatenate([wet_cells[1:], wet_north[None]], axis=0)
    flow_east = east_face * open_east[:, :, None]
    flow_north = north_face * open_north[:, :, None]
    return open_east, open_north, flow_east, flow_north


def back_faces(open_east, open_north, flow_east, flow_north, open_west_col, open_south_row, flow_west_col, flow_south_row):
    open_west = jnp.concatenate([open_west_col[:, None], open_east[:, :-1]], axis=1)
    open_south = jnp.concatenate([open_south_row[None], open_north[:-1]], axis=0)
    flow_west = jnp.concatenate([flow_west_col[:, None], flow_east[:, :-1]], axis=1)
    flow_south = jnp.concatenate([flow_south_row[None], flow_north[:-1]], axis=0)
    return open_west, open_south, flow_west, flow_south


def react(mixed_cells, temp_mean, light_top, levels):
    def tracer_at(tracer_number):
        return mixed_cells[:, :, tracer_number * levels:(tracer_number + 1) * levels]

    carbon_dis = tracer_at(0)
    alkalinity = tracer_at(1)
    oxygen = tracer_at(2)
    nitrate = tracer_at(3)
    ammonium = tracer_at(4)
    phosphate = tracer_at(5)
    silicate = tracer_at(6)
    iron_free = tracer_at(7)
    nano_carbon = tracer_at(8)
    diat_carbon = tracer_at(9)
    nano_chl = tracer_at(10)
    diat_chl = tracer_at(11)
    nano_iron = tracer_at(12)
    diat_iron = tracer_at(13)
    diat_silica = tracer_at(14)
    micro_zoo = tracer_at(15)
    meso_zoo = tracer_at(16)
    dissolved_org = tracer_at(17)
    small_part = tracer_at(18)
    big_part = tracer_at(19)
    small_iron = tracer_at(20)
    big_iron = tracer_at(21)
    big_silica = tracer_at(22)
    calcite = tracer_at(23)
    absorb = 0.04 + 0.02 * (positive(nano_chl) + positive(diat_chl))
    depth_sum = depth_sums(absorb, levels)
    par_light = light_top[:, :, None] * jnp.exp(-(depth_sum + 0.5 * absorb))
    warm_factor = jnp.exp(0.0639 * temp_mean)
    nitrogen = positive(nitrate) + positive(ammonium)
    limit_nitro = nitrogen / (0.5 + nitrogen)
    limit_phos = positive(phosphate) / (0.3 + positive(phosphate))
    limit_iron = positive(iron_free) / (0.2 + positive(iron_free))
    limit_sil = positive(silicate) / (1.0 + positive(silicate))
    nutr_nano = jnp.minimum(jnp.minimum(limit_nitro, limit_phos), limit_iron)
    nutr_diat = jnp.minimum(nutr_nano, limit_sil)
    prod_nano = 0.1 * warm_factor * par_light / (par_light + 0.5) * nutr_nano * nano_carbon
    prod_diat = 0.12 * warm_factor * par_light / (par_light + 1.0) * nutr_diat * diat_carbon
    ammon_share = (positive(ammonium) + 0.01) / (nitrogen + 0.02)
    graze_nano = 0.08 * warm_factor * micro_zoo / (1.0 + positive(nano_carbon))
    graze_diat = 0.06 * warm_factor * meso_zoo / (1.0 + positive(diat_carbon))
    loss_nano = graze_nano + 0.02
    loss_diat = graze_diat + 0.02
    eaten_nano = graze_nano * nano_carbon
    eaten_diat = graze_diat * diat_carbon
    death_micro = 0.03 * micro_zoo * positive(micro_zoo)
    death_meso = 0.03 * meso_zoo * positive(meso_zoo)
    remin_doc = 0.03 * warm_factor * dissolved_org
    remin_poc = 0.02 * warm_factor * small_part
    remin_goc = 0.01 * warm_factor * big_part
    nitrify = 0.05 * ammonium
    melt_si = 0.02 * big_silica
    melt_cal = 0.01 * calcite
    melt_sfe = 0.02 * small_iron
    melt_bfe = 0.01 * big_iron
    uptake = prod_nano + prod_diat
    remin_total = remin_doc + remin_poc + remin_goc
    calcify = 0.02 * prod_nano
    updated = [
        carbon_dis + remin_total - uptake + melt_cal - calcify,
        alkalinity + 2.0 * (melt_cal - calcify) + 0.16 * ((1.0 - ammon_share) * uptake - nitrify),
        oxygen + 1.3 * (uptake - remin_total) - 0.32 * nitrify,
        nitrate + 0.16 * (nitrify - (1.0 - ammon_share) * uptake),
        ammonium + 0.16 * (remin_total - ammon_share * uptake - nitrify),
        phosphate + 0.01 * (remin_total - uptake),
        silicate + melt_si - 0.15 * prod_diat,
        iron_free + melt_sfe + melt_bfe - 0.005 * uptake,
        nano_carbon + prod_nano - loss_nano * nano_carbon,
        diat_carbon + prod_diat - loss_diat * diat_carbon,
        nano_chl + 0.03 * prod_nano - loss_nano * nano_chl,
        diat_chl + 0.03 * prod_diat - loss_diat * diat_chl,
        nano_iron + 0.005 * prod_nano - loss_nano * nano_iron,
        diat_iron + 0.005 * prod_diat - loss_diat * diat_iron,
        diat_silica + 0.15 * prod_diat - loss_diat * diat_silica,
        micro_zoo + 0.3 * eaten_nano - death_micro,
        meso_zoo + 0.3 * eaten_diat - death_meso,
        dissolved_org + 0.3 * eaten_nano + 0.02 * nano_carbon - remin_doc,
        small_part + 0.4 * eaten_nano + death_micro - remin_poc,
        big_part + 0.4 * eaten_diat + 0.02 * diat_carbon + death_meso - remin_goc,
        small_iron + loss_nano * nano_iron - melt_sfe,
        big_iron + loss_diat * diat_iron - melt_bfe,
        big_silica + loss_diat * diat_silica - melt_si,
        calcite + calcify - melt_cal,
    ]
    return jnp.concatenate(updated, axis=2)


def advance(current, halo_sides, physics, cell_flags, levels, tracer_count):
    def widen(level_part):
        return jnp.tile(level_part, (1, 1, tracer_count))

    flow_west = widen(physics[:, :, 0:levels])
    flow_east = widen(physics[:, :, levels:2 * levels])
    flow_south = widen(physics[:, :, 2 * levels:3 * levels])
    flow_north = widen(physics[:, :, 3 * levels:4 * levels])
    temp_mean = physics[:, :, 4 * levels:5 * levels]
    mixing = widen(physics[:, :, 5 * levels:6 * levels])
    south_cell = jnp.concatenate([halo_sides[0][None], current[:-1]], axis=0)
    north_cell = jnp.concatenate([current[1:], halo_sides[1][None]], axis=0)
    west_cell = jnp.concatenate([halo_sides[2][:, None], current[:, :-1]], axis=1)
    east_cell = jnp.concatenate([current[:, 1:], halo_sides[3][:, None]], axis=1)
    flux_east = jnp.maximum(flow_east, 0.0) * current + jnp.minimum(flow_east, 0.0) * east_cell
    flux_west = jnp.maximum(flow_west, 0.0) * west_cell + jnp.minimum(flow_west, 0.0) * current
    flux_north = jnp.maximum(flow_north, 0.0) * current + jnp.minimum(flow_north, 0.0) * north_cell
    flux_south = jnp.maximum(flow_south, 0.0) * south_cell + jnp.minimum(flow_south, 0.0) * current
    spread = diffuse_rate * (cell_flags[:, :, 0:1] * (west_cell - current) + cell_flags[:, :, 1:2] * (east_cell - current) + cell_flags[:, :, 2:3] * (south_cell - current) + cell_flags[:, :, 3:4] * (north_cell - current))
    moved_cells = current - (flux_east - flux_west) - (flux_north - flux_south) + spread
    level_index = jnp.arange(moved_cells.shape[-1]) % levels
    zero_level = jnp.zeros_like(moved_cells[:, :, :1])
    deeper = jnp.concatenate([moved_cells[:, :, 1:], zero_level], axis=2)
    shallower = jnp.concatenate([zero_level, moved_cells[:, :, :-1]], axis=2)
    mixing_upper = jnp.concatenate([zero_level, mixing[:, :, :-1]], axis=2)
    flux_below = jnp.where(level_index < levels - 1, mixing * (deeper - moved_cells), 0.0)
    flux_above = jnp.where(level_index > 0, mixing_upper * (moved_cells - shallower), 0.0)
    mixed_cells = moved_cells + flux_below - flux_above
    reacted = react(mixed_cells, temp_mean, cell_flags[:, :, 4], levels)
    return reacted * cell_flags[:, :, 5:6]


def shortwave(chl_grid, light_fine, wet_cells, levels, factor):
    absorb = 0.04 + 0.02 * chl_grid
    depth_sum = depth_sums(absorb, levels)
    passed = (jnp.exp(-depth_sum) - jnp.exp(-(depth_sum + absorb))) * wet_cells[:, :, None]
    layered = jnp.transpose(passed, (2, 0, 1))
    spread_cells = jnp.repeat(jnp.repeat(layered, factor, axis=1), factor, axis=2)
    return (light_fine[None] * spread_cells).astype(jnp.bfloat16)


def reference(tracers, phys_fine, mix_coarse, surf_light, land_mask, owner_map):
    wet_all = land_mask.astype(jnp.float32)
    fine_rows = CF * BLK
    slot_ids = jnp.arange(WETMAX)
    block_ids = jnp.arange(NBX)

    def band_physics(band_index):
        fine_band = lax.dynamic_slice_in_dim(phys_fine, band_index * fine_rows, fine_rows, 0)
        light_fine = lax.dynamic_slice_in_dim(surf_light, band_index * fine_rows, fine_rows, 0)
        east_face, north_face, temp_mean, light_mean = coarsen(fine_band, light_fine, NLEV, CF)
        mix_mean = lax.dynamic_slice_in_dim(mix_coarse, band_index * BLK, BLK, 0).astype(jnp.float32)
        wet_cells = lax.dynamic_slice_in_dim(wet_all, band_index * BLK, BLK, 0)
        has_north = (band_index < NBY - 1).astype(jnp.float32)
        has_south = (band_index > 0).astype(jnp.float32)
        wet_north = lax.dynamic_index_in_dim(wet_all, jnp.minimum(band_index + 1, NBY - 1) * BLK, 0, keepdims=False) * has_north
        wet_south = lax.dynamic_index_in_dim(wet_all, jnp.maximum(band_index * BLK - 1, 0), 0, keepdims=False) * has_south
        open_east, open_north, flow_east, flow_north = open_faces(east_face, north_face, wet_cells, wet_north, wet_cells[:, 0])
        below_row = lax.dynamic_index_in_dim(phys_fine, jnp.maximum(band_index * fine_rows - 1, 0), 0, keepdims=False)
        north_below = jnp.mean(below_row[:, NLEV:2 * NLEV].reshape(NXC, CF, NLEV).astype(jnp.float32), axis=1)
        open_south_row = wet_south * wet_cells[0]
        open_west_col = wet_cells[:, -1] * wet_cells[:, 0]
        flow_south_row = north_below * open_south_row[:, None]
        open_west, open_south, flow_west, flow_south = back_faces(open_east, open_north, flow_east, flow_north, open_west_col, open_south_row, flow_east[:, -1], flow_south_row)
        physics = jnp.concatenate([flow_west, flow_east, flow_south, flow_north, temp_mean, mix_mean], axis=2)
        cell_flags = jnp.stack([open_west, open_east, open_south, open_north, light_mean, wet_cells], axis=2)
        map_row = lax.dynamic_index_in_dim(owner_map, band_index, 0, keepdims=False)
        slot_codes = band_index * WETMAX + slot_ids
        code_match = map_row[None, :] == slot_codes[:, None]
        block_of = jnp.sum(jnp.where(code_match, block_ids[None, :], 0), axis=1).astype(jnp.int32)
        filled = jnp.any(code_match, axis=1)
        phys_blocks = physics.reshape(BLK, NBX, BLK, 6 * NLEV).transpose(1, 0, 2, 3)
        flag_blocks = cell_flags.reshape(BLK, NBX, BLK, 6).transpose(1, 0, 2, 3)
        slot_phys = jnp.where(filled[:, None, None, None], phys_blocks[block_of], 0.0)
        slot_flags = jnp.where(filled[:, None, None, None], flag_blocks[block_of], 0.0)
        return slot_phys, slot_flags, block_of, filled

    band_phys, band_flags, band_blocks, band_filled = lax.map(band_physics, jnp.arange(NBY))

    def advance_one(items):
        return advance(items[0], items[1], items[2], items[3], NLEV, NTR)

    def band_step(current, items):
        band_index, slot_phys, slot_flags, block_of, filled = items
        own_slots = lax.dynamic_slice_in_dim(current, band_index * WETMAX, WETMAX, 0)
        map_row = lax.dynamic_index_in_dim(owner_map, band_index, 0, keepdims=False)
        south_map = lax.dynamic_index_in_dim(owner_map, jnp.maximum(band_index - 1, 0), 0, keepdims=False)
        north_map = lax.dynamic_index_in_dim(owner_map, jnp.minimum(band_index + 1, NBY - 1), 0, keepdims=False)
        west_slot = map_row[(block_of - 1) % NBX]
        east_slot = map_row[(block_of + 1) % NBX]
        south_slot = jnp.where(band_index > 0, south_map[block_of], -1)
        north_slot = jnp.where(band_index < NBY - 1, north_map[block_of], -1)

        def masked(edge_rows, slot_index):
            return jnp.where((slot_index >= 0)[:, None, None], edge_rows, 0.0)

        halo_south = masked(current[jnp.maximum(south_slot, 0), BLK - 1], south_slot)
        halo_north = masked(current[jnp.maximum(north_slot, 0), 0], north_slot)
        halo_west = masked(current[jnp.maximum(west_slot, 0), :, BLK - 1], west_slot)
        halo_east = masked(current[jnp.maximum(east_slot, 0), :, 0], east_slot)
        halo_sides = jnp.stack([halo_south, halo_north, halo_west, halo_east], axis=1)
        updated = lax.map(advance_one, (own_slots, halo_sides, slot_phys, slot_flags))
        return jnp.where(filled[:, None, None, None], updated, 0.0)

    current = tracers.reshape(SLOTS, NTR * NLEV, BLK, BLK).transpose(0, 2, 3, 1)
    for step_index in range(ITERS):
        stepped = lax.map(partial(band_step, current), (jnp.arange(NBY), band_phys, band_flags, band_blocks, band_filled))
        current = stepped.reshape(SLOTS, BLK, BLK, NTR * NLEV)

    chl_slots = positive(current[..., nano_chl_index * NLEV:(nano_chl_index + 1) * NLEV]) + positive(current[..., diat_chl_index * NLEV:(diat_chl_index + 1) * NLEV])

    def band_heat(band_index):
        map_row = lax.dynamic_index_in_dim(owner_map, band_index, 0, keepdims=False)
        block_chl = jnp.where((map_row >= 0)[:, None, None, None], chl_slots[jnp.maximum(map_row, 0)], 0.0)
        chl_grid = block_chl.transpose(1, 0, 2, 3).reshape(BLK, NXC, NLEV)
        wet_cells = lax.dynamic_slice_in_dim(wet_all, band_index * BLK, BLK, 0)
        light_fine = lax.dynamic_slice_in_dim(surf_light, band_index * fine_rows, fine_rows, 0)
        return shortwave(chl_grid, light_fine, wet_cells, NLEV, CF)

    heat_bands = lax.map(band_heat, jnp.arange(NBY))
    heating = heat_bands.transpose(1, 0, 2, 3).reshape(NLEV, NYF, NXF)
    tracers_out = current.transpose(0, 3, 1, 2).reshape(SLOTS, NTR * NLEV, BLK * BLK)
    return tracers_out, heating
```

```python
import functools

import jax
import jax.numpy as jnp
from jax import lax
from jax.experimental import pallas as pl
from jax.experimental.pallas import tpu as pltpu
from jax.sharding import PartitionSpec as P

NTR = 24
LEV = 48
SIDE = 16
CELLS = 256
SLOTS = 8
TILE = 8
PHYS = 224
DIFF = 0.08
VM = pltpu.VMEM
ROWS3 = 3 * LEV


def pos(v):
    return jnp.maximum(v, 0.0)


def lanes():
    return lax.broadcasted_iota(jnp.int32, (LEV, 128), 1)


def roll(x, shift):
    return pltpu.roll(x, shift, 1)


def pack_edges(c_ref, rows_ref, w_ref, e_ref, odd):
    lane = lanes()
    group = lane // SIDE
    col = lane % SIDE
    base = odd * 8
    for m in range(3):
        blank = jnp.zeros((LEV, 128), jnp.float32)
        south, north = blank, blank
        west, east = [blank, blank], [blank, blank]
        for g in range(8):
            t = 3 * g + m
            a = c_ref[0, t * LEV:(t + 1) * LEV, 0:128]
            b = c_ref[0, t * LEV:(t + 1) * LEV, 128:256]
            south = jnp.where(group == g, roll(a, 16 * g) if g else a, south)
            north = jnp.where(group == g, roll(b, (16 * g + 16) % 128), north)
            for h, v in enumerate((a, b)):
                west[h] = jnp.where(col == g, roll(v, g) if g else v, west[h])
                east[h] = jnp.where(col == g, roll(v, (g - 15) % 128), east[h])
        at = slice(m * LEV, (m + 1) * LEV)
        rows_ref[0, 0, at, :] = south
        rows_ref[0, 1, at, :] = north
        mine = (col // 8) == odd
        for h in range(2):
            hs = slice(h * 128, (h + 1) * 128)
            w_ref[0, at, hs] = jnp.where(mine, roll(west[h], base), w_ref[0, at, hs])
            e_ref[0, at, hs] = jnp.where(mine, roll(east[h], base), e_ref[0, at, hs])


def clear_first(odd, *refs):
    @pl.when(odd == 0)
    def _():
        for ref in refs:
            ref[...] = jnp.zeros_like(ref)


def pack_kernel(tab, c_ref, rows_ref, w_ref, e_ref):
    odd = pl.program_id(0) % 2
    clear_first(odd, w_ref, e_ref)
    pack_edges(c_ref, rows_ref, w_ref, e_ref, odd)


def pack(tab, tracers):
    return pl.pallas_call(
        pack_kernel,
        grid_spec=pltpu.PrefetchScalarGridSpec(
            num_scalar_prefetch=1,
            grid=(SLOTS,),
            in_specs=[pl.BlockSpec((1, NTR * LEV, CELLS), lambda j, tab: (j, 0, 0))],
            out_specs=[
                pl.BlockSpec((1, 2, ROWS3, 128), lambda j, tab: (tab[4, j], 0, 0, 0)),
                pl.BlockSpec((1, ROWS3, CELLS), lambda j, tab: (j // 2, 0, 0)),
                pl.BlockSpec((1, ROWS3, CELLS), lambda j, tab: (j // 2, 0, 0)),
            ],
        ),
        out_shape=[
            jax.ShapeDtypeStruct((16, 2, ROWS3, 128), jnp.float32),
            jax.ShapeDtypeStruct((4, ROWS3, CELLS), jnp.float32),
            jax.ShapeDtypeStruct((4, ROWS3, CELLS), jnp.float32),
        ],
        cost_estimate=pl.CostEstimate(flops=10**7, bytes_accessed=12 * 10**6, transcendentals=0),
        name="pack",
    )(tab, tracers)


def react(get, put, par, warm):
    (carbon_dis, alkalinity, oxygen, nitrate, ammonium, phosphate, silicate, iron_free,
     nano_carbon, diat_carbon, nano_chl, diat_chl, nano_iron, diat_iron, diat_silica,
     micro_zoo, meso_zoo, dissolved_org, small_part, big_part, small_iron, big_iron,
     big_silica, calcite) = [functools.partial(get, t) for t in range(NTR)]
    p_am = pos(ammonium())
    nitrogen = pos(nitrate()) + p_am
    limit_nitro = nitrogen / (0.5 + nitrogen)
    p_ph = pos(phosphate())
    p_fe = pos(iron_free())
    p_si = pos(silicate())
    nutr_nano = jnp.minimum(jnp.minimum(limit_nitro, p_ph / (0.3 + p_ph)), p_fe / (0.2 + p_fe))
    nutr_diat = jnp.minimum(nutr_nano, p_si / (1.0 + p_si))
    nc = nano_carbon()
    dc = diat_carbon()
    wp = warm * par
    prod_nano = 0.1 * wp / (par + 0.5) * nutr_nano * nc
    prod_diat = 0.12 * wp / (par + 1.0) * nutr_diat * dc
    share = (p_am + 0.01) / (nitrogen + 0.02)
    mi = micro_zoo()
    me = meso_zoo()
    graze_nano = 0.08 * warm * mi / (1.0 + pos(nc))
    graze_diat = 0.06 * warm * me / (1.0 + pos(dc))
    loss_nano = graze_nano + 0.02
    loss_diat = graze_diat + 0.02
    eaten_nano = graze_nano * nc
    eaten_diat = graze_diat * dc
    death_micro = 0.03 * mi * pos(mi)
    death_meso = 0.03 * me * pos(me)
    do = dissolved_org()
    sp = small_part()
    bp = big_part()
    remin_doc = 0.03 * warm * do
    remin_poc = 0.02 * warm * sp
    remin_goc = 0.01 * warm * bp
    am = ammonium()
    nitrify = 0.05 * am
    cal = calcite()
    melt_cal = 0.01 * cal
    uptake = prod_nano + prod_diat
    remin = remin_doc + remin_poc + remin_goc
    calcify = 0.02 * prod_nano
    shell = melt_cal - calcify
    put(0, carbon_dis() + remin - uptake + shell)
    su = share * uptake
    fresh = uptake - su
    put(1, alkalinity() + 2.0 * shell + 0.16 * (fresh - nitrify))
    put(2, oxygen() + 1.3 * (uptake - remin) - 0.32 * nitrify)
    put(3, nitrate() + 0.16 * (nitrify - fresh))
    put(4, am + 0.16 * (remin - su - nitrify))
    put(5, phosphate() + 0.01 * (remin - uptake))
    bsi = big_silica()
    melt_si = 0.02 * bsi
    put(6, silicate() + melt_si - 0.15 * prod_diat)
    sfe = small_iron()
    bfe = big_iron()
    melt_sfe = 0.02 * sfe
    melt_bfe = 0.01 * bfe
    put(7, iron_free() + melt_sfe + melt_bfe - 0.005 * uptake)
    put(8, nc + prod_nano - loss_nano * nc)
    put(9, dc + prod_diat - loss_diat * dc)
    x = nano_chl()
    put(10, x + 0.03 * prod_nano - loss_nano * x)
    x = diat_chl()
    put(11, x + 0.03 * prod_diat - loss_diat * x)
    x = nano_iron()
    lost = loss_nano * x
    put(12, x + 0.005 * prod_nano - lost)
    put(20, sfe + lost - melt_sfe)
    x = diat_iron()
    lost = loss_diat * x
    put(13, x + 0.005 * prod_diat - lost)
    put(21, bfe + lost - melt_bfe)
    x = diat_silica()
    lost = loss_diat * x
    put(14, x + 0.15 * prod_diat - lost)
    put(22, bsi + lost - melt_si)
    put(15, mi + 0.3 * eaten_nano - death_micro)
    put(16, me + 0.3 * eaten_diat - death_meso)
    put(17, do + 0.3 * eaten_nano + 0.02 * nc - remin_doc)
    put(18, sp + 0.4 * eaten_nano + death_micro - remin_poc)
    put(19, bp + 0.4 * eaten_diat + 0.02 * dc + death_meso - remin_goc)
    put(23, cal - shell)


def tri():
    i = lax.broadcasted_iota(jnp.int32, (LEV, LEV), 0)
    j = lax.broadcasted_iota(jnp.int32, (LEV, LEV), 1)
    return (j < i).astype(jnp.float32)


def depth(absorb):
    return jnp.dot(tri(), absorb, precision=lax.Precision.HIGHEST,
                   preferred_element_type=jnp.float32)


def slot_step(tab, c_ref, phys, rows, west, east, out, coef, par_ref):
    j = pl.program_id(0)
    w_odd = tab[2, j] % 2
    e_odd = tab[3, j] % 2
    lane = lanes()
    col = lane % SIDE
    at_w = col == 0
    at_e = col == SIDE - 1
    low = lane < 16
    high = lane >= 112
    H = (slice(0, 128), slice(128, 256))
    edge = jnp.concatenate([phys[0, 200:224, 0:128], phys[0, 200:224, 128:256]], axis=0)
    sel_r = lax.broadcasted_iota(jnp.int32, (128, 256), 0)
    sel_c = lax.broadcasted_iota(jnp.int32, (128, 256), 1)
    sel = ((sel_c == SIDE * sel_r) & (sel_r < SIDE)).astype(jnp.float32)
    edge_lane = jnp.where(low, edge, 0.0)
    edge_w = jnp.dot(edge_lane, sel, precision=lax.Precision.HIGHEST,
                     preferred_element_type=jnp.float32)
    edge_s = roll(edge, 112)
    fn_up = roll(phys[0, 48:96, H[0]], 16)
    level = lax.broadcasted_iota(jnp.int32, (LEV, 128), 0)
    for h in range(2):
        fe = phys[0, 0:48, H[h]]
        fn = phys[0, 48:96, H[h]]
        fw = jnp.where(at_w, edge_w[:, H[h]], roll(fe, 1))
        if h == 0:
            fs = jnp.where(low, edge_s, fn_up)
        else:
            fs = jnp.where(low, fn_up, roll(fn, 16))
        ow = DIFF * phys[0, 192:193, H[h]]
        oe = DIFF * phys[0, 193:194, H[h]]
        os = DIFF * phys[0, 194:195, H[h]]
        on = DIFF * phys[0, 195:196, H[h]]
        coef[0, :, H[h]] = (1.0 - (ow + oe + os + on)) - pos(fe) + jnp.minimum(fw, 0.0) - pos(fn) + jnp.minimum(fs, 0.0)
        coef[1, :, H[h]] = oe - jnp.minimum(fe, 0.0)
        coef[2, :, H[h]] = ow + pos(fw)
        coef[3, :, H[h]] = on - jnp.minimum(fn, 0.0)
        coef[4, :, H[h]] = os + pos(fs)
        coef[5, :, H[h]] = jnp.where(level < LEV - 1, phys[0, 144:192, H[h]], 0.0)

    def mix(moved, k):
        flux = k * (pltpu.roll(moved, LEV - 1, 0) - moved)
        return moved + flux - pltpu.roll(flux, 1, 0)

    def group(g, carry):
        for m in range(3):
            at = pl.ds(pl.multiple_of((3 * g + m) * LEV, LEV), LEV)
            hm = slice(m * LEV, (m + 1) * LEV)
            a = c_ref[0, at, H[0]]
            b = c_ref[0, at, H[1]]
            hs = roll(rows[0, 0, hm, :], (128 - 16 * g) % 128)
            hn = roll(rows[0, 1, hm, :], 112 - 16 * g)
            an, bn = roll(a, 112), roll(b, 112)
            as_, bs = roll(a, 16), roll(b, 16)
            north = (jnp.where(high, bn, an), jnp.where(high, hn, bn))
            south = (jnp.where(low, hs, as_), jnp.where(low, as_, bs))
            w_shift = (128 - (8 * w_odd + g)) % 128
            e_shift = 15 - (8 * e_odd + g)
            for h, v in enumerate((a, b)):
                vw = jnp.where(at_w, roll(west[0, hm, H[h]], w_shift), roll(v, 1))
                ve = jnp.where(at_e, roll(east[0, hm, H[h]], e_shift), roll(v, 127))
                moved = (coef[0, :, H[h]] * v + coef[1, :, H[h]] * ve + coef[2, :, H[h]] * vw
                         + coef[3, :, H[h]] * north[h] + coef[4, :, H[h]] * south[h])
                out[0, at, H[h]] = mix(moved, coef[5, :, H[h]])
        return carry

    lax.fori_loop(0, 8, group, 0)
    absorb = 0.04 + 0.02 * (pos(out[0, 480:528, :]) + pos(out[0, 528:576, :]))
    above = depth(absorb)
    par_ref[...] = phys[0, 196:197, :] * jnp.exp(-(above + 0.5 * absorb))
    for h in range(2):
        wet = jnp.broadcast_to(phys[0, 197:198, H[h]], (8, 128))

        def chunk(i, carry):
            l0 = pl.multiple_of(i * 8, 8)

            def get(t):
                return out[0, pl.ds(pl.multiple_of(t * LEV + l0, 8), 8), H[h]]

            held = [get(t) for t in range(NTR)]

            def put(t, v):
                out[0, pl.ds(pl.multiple_of(t * LEV + l0, 8), 8), H[h]] = v * wet

            warm = jnp.exp(0.0639 * phys[0, pl.ds(pl.multiple_of(96 + l0, 8), 8), H[h]])
            par = par_ref[pl.ds(l0, 8), H[h]]
            react(lambda t: held[t], put, par, warm)
            return carry

        lax.fori_loop(0, LEV // 8, chunk, 0)


def first_kernel(tab, c_ref, phys, rows, west, east, out, rows_out, w_out, e_out, coef, par_ref):
    j = pl.program_id(0)
    odd = j % 2

    @pl.when(tab[1, j] == 1)
    def _():
        slot_step(tab, c_ref, phys, rows, west, east, out, coef, par_ref)

    @pl.when(tab[1, j] == 0)
    def _():
        out[...] = jnp.zeros_like(out)

    clear_first(odd, w_out, e_out)
    pack_edges(out, rows_out, w_out, e_out, odd)


def last_kernel(tab, c_ref, phys, rows, west, east, out, light_out, coef, par_ref):
    j = pl.program_id(0)

    @pl.when(tab[1, j] == 1)
    def _():
        slot_step(tab, c_ref, phys, rows, west, east, out, coef, par_ref)
        absorb = 0.04 + 0.02 * (pos(out[0, 480:528, :]) + pos(out[0, 528:576, :]))
        above = depth(absorb)
        light_out[0] = jnp.exp(-above) - jnp.exp(-(above + absorb))

    @pl.when(tab[1, j] == 0)
    def _():
        out[...] = jnp.zeros_like(out)
        light_out[...] = jnp.zeros_like(light_out)


def step(last, tab, current, phys, rows, came_west, came_east):
    edge_spec = pl.BlockSpec((1, ROWS3, CELLS), lambda j, tab: (j // 2, 0, 0))
    edge_shape = jax.ShapeDtypeStruct((4, ROWS3, CELLS), jnp.float32)
    if last:
        outs = [pl.BlockSpec((1, LEV, CELLS), lambda j, tab: (tab[4, j], 0, 0))]
        shapes = [jax.ShapeDtypeStruct((16, LEV, CELLS), jnp.float32)]
    else:
        outs = [pl.BlockSpec((1, 2, ROWS3, 128), lambda j, tab: (tab[4, j], 0, 0, 0)), edge_spec, edge_spec]
        shapes = [jax.ShapeDtypeStruct((16, 2, ROWS3, 128), jnp.float32), edge_shape, edge_shape]
    return pl.pallas_call(
        last_kernel if last else first_kernel,
        grid_spec=pltpu.PrefetchScalarGridSpec(
            num_scalar_prefetch=1,
            grid=(SLOTS,),
            in_specs=[
                pl.BlockSpec((1, NTR * LEV, CELLS), lambda j, tab: (j, 0, 0)),
                pl.BlockSpec((1, PHYS, CELLS), lambda j, tab: (tab[0, j], 0, 0)),
                pl.BlockSpec((1, 2, ROWS3, 128), lambda j, tab: (tab[0, j], 0, 0, 0)),
                pl.BlockSpec((1, ROWS3, CELLS), lambda j, tab: (tab[2, j] // 2, 0, 0)),
                pl.BlockSpec((1, ROWS3, CELLS), lambda j, tab: (tab[3, j] // 2, 0, 0)),
            ],
            out_specs=[pl.BlockSpec((1, NTR * LEV, CELLS), lambda j, tab: (j, 0, 0))] + outs,
            scratch_shapes=[VM((6, LEV, CELLS), jnp.float32), VM((LEV, CELLS), jnp.float32)],
        ),
        out_shape=[jax.ShapeDtypeStruct((SLOTS, NTR * LEV, CELLS), jnp.float32)] + shapes,
        cost_estimate=pl.CostEstimate(flops=10**8, bytes_accessed=25 * 10**6, transcendentals=10**6),
        name="last_step" if last else "first_step",
    )(tab, current, phys, rows, came_west, came_east)


def spread_matrix(shape, lhs_wide, dtype=jnp.bfloat16):
    i = lax.broadcasted_iota(jnp.int32, shape, 0)
    j = lax.broadcasted_iota(jnp.int32, shape, 1)
    return (i // 3 == j if lhs_wide else i == j // 3).astype(dtype)


def coarse_kernel(phys, mix, flags, y_ref, col_ref):
    r = pl.program_id(0)
    i = lax.broadcasted_iota(jnp.int32, (384, 128), 0)
    j = lax.broadcasted_iota(jnp.int32, (384, 128), 1)
    every = (i // 3 == j).astype(jnp.bfloat16)
    third = (i == 3 * j + 2).astype(jnp.bfloat16)

    def dot(a, b):
        return jnp.dot(a, b, preferred_element_type=jnp.float32)

    east = (dot(phys[0, 0:48, :], third) + dot(phys[1, 0:48, :], third) + dot(phys[2, 0:48, :], third)) / 3.0
    north = dot(phys[2, 48:96, :], every) / 3.0
    temp = (dot(phys[0, 96:144, :], every) + dot(phys[1, 96:144, :], every) + dot(phys[2, 96:144, :], every)) / 9.0
    east = east * flags[0, 1:2, :]
    y_ref[0, 0:48, :] = east
    y_ref[0, 48:96, :] = north * flags[0, 3:4, :]
    y_ref[0, 96:144, :] = temp
    y_ref[0, 144:192, :] = mix[0].astype(jnp.float32)
    y_ref[0, 192:200, :] = flags[0]

    @pl.when(r == 0)
    def _():
        col_ref[...] = jnp.zeros_like(col_ref)

    col_ref[...] = jnp.where(lanes() == r, roll(east, r + 1), col_ref[...])


def coarse(phys_t, mix_t, flags):
    return pl.pallas_call(
        coarse_kernel,
        grid=(SIDE,),
        in_specs=[
            pl.BlockSpec((3, 144, 384), lambda r: (r, 0, 0)),
            pl.BlockSpec((1, LEV, 128), lambda r: (r, 0, 0)),
            pl.BlockSpec((1, 8, 128), lambda r: (r, 0, 0)),
        ],
        out_specs=[
            pl.BlockSpec((1, 200, 128), lambda r: (r, 0, 0)),
            pl.BlockSpec((LEV, 128), lambda r: (0, 0)),
        ],
        out_shape=[
            jax.ShapeDtypeStruct((SIDE, 200, 128), jnp.float32),
            jax.ShapeDtypeStruct((LEV, 128), jnp.float32),
        ],
        cost_estimate=pl.CostEstimate(flops=10**9, bytes_accessed=8 * 10**6, transcendentals=0),
        name="coarse",
    )(phys_t, mix_t, flags)


def package_kernel(tab, y_ref, col_ref, row_ref, out):
    k = pl.program_id(0)
    lane = lanes()
    group = lane // SIDE
    for f in range(5):
        n = 48 if f < 4 else 8
        at = slice(48 * f, 48 * f + n)
        for h in range(2):
            acc = jnp.zeros((n, 128), jnp.float32)
            for g in range(8):
                turned = roll(y_ref[8 * h + g, at, :], (16 * g - 16 * k + 128) % 128)
                acc = jnp.where(group[:n] == g, turned, acc)
            out[0, at, 128 * h:128 * h + 128] = acc
    west = col_ref[...]
    for r in range(SIDE):
        turned = roll(y_ref[r, 0:48, :], (r + 1 - 16 * k + 128) % 128)
        west = jnp.where((lane == r) & (k > 0), turned, west)
    edge = jnp.where(lane < 16, west, roll(row_ref[...], (16 - 16 * k + 128) % 128))
    out[0, 200:224, 0:128] = edge[0:24]
    out[0, 200:224, 128:256] = edge[24:48]


def package(tab, y, col, row):
    return pl.pallas_call(
        package_kernel,
        grid_spec=pltpu.PrefetchScalarGridSpec(
            num_scalar_prefetch=1,
            grid=(TILE,),
            in_specs=[
                pl.BlockSpec((SIDE, 200, 128), lambda k, tab: (0, 0, 0)),
                pl.BlockSpec((LEV, 128), lambda k, tab: (0, 0)),
                pl.BlockSpec((LEV, 128), lambda k, tab: (0, 0)),
            ],
            out_specs=pl.BlockSpec((1, PHYS, CELLS), lambda k, tab: (tab[6, k], 0, 0)),
        ),
        out_shape=jax.ShapeDtypeStruct((16, PHYS, CELLS), jnp.float32),
        cost_estimate=pl.CostEstimate(flops=10**7, bytes_accessed=4 * 10**6, transcendentals=0),
        name="package",
    )(tab, y, col, row)


def unpick_kernel(tab, got, south, north):
    wet = tab[5, pl.program_id(0)] == 1
    south[0] = jnp.where(wet, got[0, 0], 0.0)
    north[0] = jnp.where(wet, got[0, 1], 0.0)


def unpick(tab, got):
    one = pl.BlockSpec((1, ROWS3, 128), lambda k, tab: (k, 0, 0))
    return pl.pallas_call(
        unpick_kernel,
        grid_spec=pltpu.PrefetchScalarGridSpec(
            num_scalar_prefetch=1,
            grid=(TILE,),
            in_specs=[pl.BlockSpec((1, 2, ROWS3, 128), lambda k, tab: (tab[6, k], 0, 0, 0))],
            out_specs=[one, one],
        ),
        out_shape=[jax.ShapeDtypeStruct((TILE, ROWS3, 128), jnp.float32)] * 2,
        cost_estimate=pl.CostEstimate(flops=10**6, bytes_accessed=24 * 10**5, transcendentals=0),
        name="unpick",
    )(tab, got)


def repick_kernel(tab, south, north, out):
    out[0, 0] = south[0]
    out[0, 1] = north[0]


def repick(tab, south, north):
    one = pl.BlockSpec((1, ROWS3, 128), lambda k, tab: (k, 0, 0))
    return pl.pallas_call(
        repick_kernel,
        grid_spec=pltpu.PrefetchScalarGridSpec(
            num_scalar_prefetch=1,
            grid=(TILE,),
            in_specs=[one, one],
            out_specs=pl.BlockSpec((1, 2, ROWS3, 128), lambda k, tab: (tab[6, k], 0, 0, 0)),
        ),
        out_shape=jax.ShapeDtypeStruct((16, 2, ROWS3, 128), jnp.float32),
        cost_estimate=pl.CostEstimate(flops=10**6, bytes_accessed=24 * 10**5, transcendentals=0),
        name="repick",
    )(tab, south, north)


def heat_kernel(tab, got, wet, light, out, fine):
    lane = lanes()
    group = lane // SIDE
    for r in range(SIDE):
        half = slice(128 * (r // 8), 128 * (r // 8) + 128)
        acc = jnp.zeros((LEV, 128), jnp.float32)
        for k in range(TILE):
            acc = jnp.where(group == k, roll(got[tab[6, k], :, half], (16 * k - 16 * (r % 8)) % 128), acc)
        acc = jnp.where(wet[r:r + 1, :] > 0.0, acc, 0.0)
        for a in range(3):
            fine[pl.ds(3 * r + a, LEV, stride=LEV), :] = acc
    spread = spread_matrix((128, 384), False)
    stacked = jnp.concatenate([spread] * 3, axis=0)

    def level(l, carry):
        x = fine[pl.ds(pl.multiple_of(l * LEV, LEV), LEV), :]
        high = x.astype(jnp.bfloat16)
        rest = x - high.astype(jnp.float32)
        mid = rest.astype(jnp.bfloat16)
        low = (rest - mid.astype(jnp.float32)).astype(jnp.bfloat16)
        wide = jnp.dot(jnp.concatenate([high, mid, low], axis=1), stacked,
                       preferred_element_type=jnp.float32)
        out[l] = (light[...] * wide).astype(jnp.bfloat16)
        return carry

    lax.fori_loop(0, LEV, level, 0)


def heat(tab, got, wet, light):
    return pl.pallas_call(
        heat_kernel,
        in_specs=[pl.BlockSpec(memory_space=pltpu.SMEM)] + [pl.BlockSpec(memory_space=VM)] * 3,
        out_specs=pl.BlockSpec(memory_space=VM),
        out_shape=jax.ShapeDtypeStruct((LEV, 48, 384), jnp.bfloat16),
        scratch_shapes=[VM((LEV * LEV, 128), jnp.float32)],
        cost_estimate=pl.CostEstimate(flops=10**9, bytes_accessed=3 * 10**6, transcendentals=0),
        name="heat",
    )(tab, got, wet, light)


def tables(band, lat, lon):
    wet = band >= 0
    owner = band // SLOTS % 16
    tile = jnp.arange(128) // TILE
    slot_code = (lat * 16 + lon) * SLOTS + jnp.arange(SLOTS)
    hit = band[None, :] == slot_code[:, None]
    full = jnp.any(hit, axis=1)
    block = jnp.sum(jnp.where(hit, jnp.arange(128)[None, :], 0), axis=1)
    west = jnp.sum(jnp.where(jnp.roll(hit, -1, axis=1), band[None, :], 0), axis=1)
    east = jnp.sum(jnp.where(jnp.roll(hit, 1, axis=1), band[None, :], 0), axis=1)
    src = jnp.where(full, block // TILE, 0)
    used = jnp.any((src[None, :] == jnp.arange(16)[:, None]) & full[None, :], axis=1)
    spare = jnp.argmin(used).astype(jnp.int32)
    w_slot = jnp.where(full & (west >= 0), west % SLOTS, 0)
    e_slot = jnp.where(full & (east >= 0), east % SLOTS, 0)
    mine = lax.dynamic_slice_in_dim(band, lon * TILE, TILE)
    t_wet = mine >= 0
    t_own = mine // SLOTS % 16
    t_used = jnp.any((t_own[None, :] == jnp.arange(16)[:, None]) & t_wet[None, :], axis=1)
    t_spare = jnp.argmin(t_used).astype(jnp.int32)
    rows = [src, full, w_slot, e_slot, jnp.where(full, src, spare), t_wet, jnp.where(t_wet, t_own, t_spare), src]
    return jnp.stack([r.astype(jnp.int32) for r in rows])


def shift(x, axis, by, closed=True):
    n = lax.axis_size(axis)
    return lax.ppermute(x, axis, [(i, (i + by) % n) for i in range(n) if closed or 0 <= i + by < n])


def swap(x):
    return lax.all_to_all(x, "lon", split_axis=0, concat_axis=0, tiled=True)


def on_device(tracers, phys_fine, mix_coarse, surf_light, land_mask, owner_map):
    tab = tables(owner_map[0], lax.axis_index("lat"), lax.axis_index("lon"))
    wet = land_mask.astype(jnp.float32)
    wet_s = shift(wet[-1], "lat", 1, False)
    wet_n = shift(wet[0], "lat", -1, False)
    wet_w = shift(wet[:, -1], "lon", 1)
    wet_e = shift(wet[:, 0], "lon", -1)
    rows_out, w_out, e_out = pack(tab, tracers)
    open_e = wet * jnp.concatenate([wet[:, 1:], wet_e[:, None]], axis=1)
    open_w = wet * jnp.concatenate([wet_w[:, None], wet[:, :-1]], axis=1)
    open_n = wet * jnp.concatenate([wet[1:], wet_n[None]], axis=0)
    open_s = wet * jnp.concatenate([wet_s[None], wet[:-1]], axis=0)
    light = jnp.dot(surf_light, spread_matrix((384, 128), True, jnp.float32),
                    precision=lax.Precision.HIGHEST).reshape(SIDE, 3, 128)
    light = (light[:, 0] + light[:, 1] + light[:, 2]) / 9.0
    blank = jnp.zeros_like(wet)
    flags = jnp.stack([open_w, open_e, open_s, open_n, light, wet, blank, blank], axis=1)
    y, col = coarse(jnp.swapaxes(phys_fine, 1, 2), jnp.swapaxes(mix_coarse, 1, 2), flags)
    col = shift(col, "lon", 1)
    row = shift(y[SIDE - 1, 48:96], "lat", 1)
    phys = swap(package(tab, y, col, row))
    current = tracers
    for n in range(2):
        south, north = unpick(tab, swap(rows_out))
        rows = swap(repick(tab, shift(north, "lat", 1), shift(south, "lat", -1)))
        came_west = shift(e_out, "lon", 1)
        came_east = shift(w_out, "lon", -1)
        if n == 0:
            current, rows_out, w_out, e_out = step(False, tab, current, phys, rows, came_west, came_east)
        else:
            current, light_part = step(True, tab, current, phys, rows, came_west, came_east)
    return current, heat(tab, swap(light_part), wet, surf_light)


def solution(mesh):
    in_specs = (
        P(("lat", "lon"), None, None),
        P("lat", "lon", None),
        P("lat", "lon", None),
        P("lat", "lon"),
        P("lat", "lon"),
        P("lat", None),
    )
    out_specs = (P(("lat", "lon"), None, None), P(None, "lat", "lon"))
    return jax.shard_map(
        on_device, mesh=mesh, in_specs=in_specs, out_specs=out_specs, check_vma=False
    )
```

```python
import functools

import jax
import jax.numpy as jnp
from jax import lax
from jax.experimental import pallas as pl
from jax.experimental.pallas import tpu as pltpu
from jax.sharding import PartitionSpec as P

NTR = 24
LEV = 48
SIDE = 16
CELLS = 256
SLOTS = 8
TILE = 8
PHYS = 224
DIFF = 0.08
VM = pltpu.VMEM
ROWS3 = 3 * LEV
HALF = ROWS3 // 2


def pos(v):
    return jnp.maximum(v, 0.0)


def lanes():
    return lax.broadcasted_iota(jnp.int32, (LEV, 128), 1)


def roll(x, shift):
    return pltpu.roll(x, shift, 1)


def pack_edges(c_ref, rows_ref, w_ref, e_ref, odd):
    lane = lanes()
    group = lane // SIDE
    col = lane % SIDE
    even = lane % 2 == 0
    low = lane < SIDE
    for m in range(3):
        blank = jnp.zeros((LEV, 128), jnp.float32)
        ends = [blank, blank]
        both = [blank, blank]
        for g in range(8):
            t = 3 * g + m
            a = c_ref[0, t * LEV:(t + 1) * LEV, 0:128]
            b = c_ref[0, t * LEV:(t + 1) * LEV, 128:256]
            end = jnp.where(low, a, b)
            ends[g % 2] = jnp.where((group == g) | (group == (g + 7) % 8), roll(end, 16 * g) if g else end, ends[g % 2])
            here = (col == 2 * g) | (col == (2 * g + 15) % 16)
            for h, v in enumerate((a, b)):
                both[h] = jnp.where(here, roll(v, 2 * g) if g else v, both[h])
        flat = group % 2 == 0
        put_rows(rows_ref, 0, m, jnp.where(flat, ends[0], ends[1]))
        put_rows(rows_ref, 1, m, jnp.where(flat, ends[1], ends[0]))
        at = slice(m * LEV, (m + 1) * LEV)
        mine = (lane % 2) == odd
        for h in range(2):
            hs = slice(h * 128, (h + 1) * 128)
            turned = roll(both[h], odd)
            w_ref[0, at, hs] = jnp.where(mine, turned, w_ref[0, at, hs])
            e_ref[0, at, hs] = jnp.where(mine, e_ref[0, at, hs], turned)


def put_rows(rows_ref, d, m, x):
    lo = m * LEV
    if lo < HALF:
        n = min(LEV, HALF - lo)
        rows_ref[0, 0, d, lo:lo + n, :] = x[:n]
        if n < LEV:
            rows_ref[0, 1, d, 0:LEV - n, :] = x[n:]
    else:
        rows_ref[0, 1, d, lo - HALF:lo - HALF + LEV, :] = x


def clear_first(odd, *refs):
    @pl.when(odd == 0)
    def _():
        for ref in refs:
            ref[...] = jnp.zeros_like(ref)


def pack_kernel(tab, c_ref, rows_ref, w_ref, e_ref):
    odd = pl.program_id(0) % 2
    clear_first(odd, w_ref, e_ref)
    pack_edges(c_ref, rows_ref, w_ref, e_ref, odd)


def pack(tab, tracers):
    return pl.pallas_call(
        pack_kernel,
        grid_spec=pltpu.PrefetchScalarGridSpec(
            num_scalar_prefetch=1,
            grid=(SLOTS,),
            in_specs=[pl.BlockSpec((1, NTR * LEV, CELLS), lambda j, tab: (j, 0, 0))],
            out_specs=[
                pl.BlockSpec((1, 2, 2, HALF, 128), lambda j, tab: (tab[8, j], 0, 0, 0, 0)),
                pl.BlockSpec((1, ROWS3, CELLS), lambda j, tab: (j // 2, 0, 0)),
                pl.BlockSpec((1, ROWS3, CELLS), lambda j, tab: (j // 2, 0, 0)),
            ],
        ),
        out_shape=[
            jax.ShapeDtypeStruct((8, 2, 2, HALF, 128), jnp.float32),
            jax.ShapeDtypeStruct((4, ROWS3, CELLS), jnp.float32),
            jax.ShapeDtypeStruct((4, ROWS3, CELLS), jnp.float32),
        ],
        cost_estimate=pl.CostEstimate(flops=10**7, bytes_accessed=12 * 10**6, transcendentals=0),
        name="pack",
    )(tab, tracers)


def react(get, put, par, warm):
    (carbon_dis, alkalinity, oxygen, nitrate, ammonium, phosphate, silicate, iron_free,
     nano_carbon, diat_carbon, nano_chl, diat_chl, nano_iron, diat_iron, diat_silica,
     micro_zoo, meso_zoo, dissolved_org, small_part, big_part, small_iron, big_iron,
     big_silica, calcite) = [functools.partial(get, t) for t in range(NTR)]
    p_am = pos(ammonium())
    nitrogen = pos(nitrate()) + p_am
    limit_nitro = nitrogen / (0.5 + nitrogen)
    p_ph = pos(phosphate())
    p_fe = pos(iron_free())
    p_si = pos(silicate())
    nutr_nano = jnp.minimum(jnp.minimum(limit_nitro, p_ph / (0.3 + p_ph)), p_fe / (0.2 + p_fe))
    nutr_diat = jnp.minimum(nutr_nano, p_si / (1.0 + p_si))
    nc = nano_carbon()
    dc = diat_carbon()
    wp = warm * par
    prod_nano = 0.1 * wp / (par + 0.5) * nutr_nano * nc
    prod_diat = 0.12 * wp / (par + 1.0) * nutr_diat * dc
    share = (p_am + 0.01) / (nitrogen + 0.02)
    mi = micro_zoo()
    me = meso_zoo()
    graze_nano = 0.08 * warm * mi / (1.0 + pos(nc))
    graze_diat = 0.06 * warm * me / (1.0 + pos(dc))
    loss_nano = graze_nano + 0.02
    loss_diat = graze_diat + 0.02
    eaten_nano = graze_nano * nc
    eaten_diat = graze_diat * dc
    death_micro = 0.03 * mi * pos(mi)
    death_meso = 0.03 * me * pos(me)
    do = dissolved_org()
    sp = small_part()
    bp = big_part()
    remin_doc = 0.03 * warm * do
    remin_poc = 0.02 * warm * sp
    remin_goc = 0.01 * warm * bp
    am = ammonium()
    nitrify = 0.05 * am
    cal = calcite()
    melt_cal = 0.01 * cal
    uptake = prod_nano + prod_diat
    remin = remin_doc + remin_poc + remin_goc
    calcify = 0.02 * prod_nano
    shell = melt_cal - calcify
    put(0, carbon_dis() + remin - uptake + shell)
    su = share * uptake
    fresh = uptake - su
    put(1, alkalinity() + 2.0 * shell + 0.16 * (fresh - nitrify))
    put(2, oxygen() + 1.3 * (uptake - remin) - 0.32 * nitrify)
    put(3, nitrate() + 0.16 * (nitrify - fresh))
    put(4, am + 0.16 * (remin - su - nitrify))
    put(5, phosphate() + 0.01 * (remin - uptake))
    bsi = big_silica()
    melt_si = 0.02 * bsi
    put(6, silicate() + melt_si - 0.15 * prod_diat)
    sfe = small_iron()
    bfe = big_iron()
    melt_sfe = 0.02 * sfe
    melt_bfe = 0.01 * bfe
    put(7, iron_free() + melt_sfe + melt_bfe - 0.005 * uptake)
    put(8, nc + prod_nano - loss_nano * nc)
    put(9, dc + prod_diat - loss_diat * dc)
    x = nano_chl()
    put(10, x + 0.03 * prod_nano - loss_nano * x)
    x = diat_chl()
    put(11, x + 0.03 * prod_diat - loss_diat * x)
    x = nano_iron()
    lost = loss_nano * x
    put(12, x + 0.005 * prod_nano - lost)
    put(20, sfe + lost - melt_sfe)
    x = diat_iron()
    lost = loss_diat * x
    put(13, x + 0.005 * prod_diat - lost)
    put(21, bfe + lost - melt_bfe)
    x = diat_silica()
    lost = loss_diat * x
    put(14, x + 0.15 * prod_diat - lost)
    put(22, bsi + lost - melt_si)
    put(15, mi + 0.3 * eaten_nano - death_micro)
    put(16, me + 0.3 * eaten_diat - death_meso)
    put(17, do + 0.3 * eaten_nano + 0.02 * nc - remin_doc)
    put(18, sp + 0.4 * eaten_nano + death_micro - remin_poc)
    put(19, bp + 0.4 * eaten_diat + 0.02 * dc + death_meso - remin_goc)
    put(23, cal - shell)


def tri():
    i = lax.broadcasted_iota(jnp.int32, (LEV, LEV), 0)
    j = lax.broadcasted_iota(jnp.int32, (LEV, LEV), 1)
    return (j < i).astype(jnp.float32)


def depth(absorb):
    return jnp.dot(tri(), absorb, precision=lax.Precision.HIGHEST,
                   preferred_element_type=jnp.float32)


def slot_step(tab, c_ref, phys, rows, west, east, out, coef, par_ref, cross, along):
    j = pl.program_id(0)
    w_odd = tab[2, j] % 2
    e_odd = tab[3, j] % 2
    lane = lanes()
    col = lane % SIDE
    at_w = col == 0
    at_e = col == SIDE - 1
    low = lane < 16
    high = lane >= 112
    H = (slice(0, 128), slice(128, 256))
    edge = jnp.concatenate([phys[0, 200:224, 0:128], phys[0, 200:224, 128:256]], axis=0)
    sel_r = lax.broadcasted_iota(jnp.int32, (128, 256), 0)
    sel_c = lax.broadcasted_iota(jnp.int32, (128, 256), 1)
    sel = ((sel_c == SIDE * sel_r) & (sel_r < SIDE)).astype(jnp.float32)
    edge_lane = jnp.where(low, edge, 0.0)
    edge_w = jnp.dot(edge_lane, sel, precision=lax.Precision.HIGHEST,
                     preferred_element_type=jnp.float32)
    edge_s = roll(edge, 112)
    fn_up = roll(phys[0, 48:96, H[0]], 16)
    level = lax.broadcasted_iota(jnp.int32, (LEV, 128), 0)
    for h in range(2):
        fe = phys[0, 0:48, H[h]]
        fn = phys[0, 48:96, H[h]]
        fw = jnp.where(at_w, edge_w[:, H[h]], roll(fe, 1))
        if h == 0:
            fs = jnp.where(low, edge_s, fn_up)
        else:
            fs = jnp.where(low, fn_up, roll(fn, 16))
        ow = DIFF * phys[0, 192:193, H[h]]
        oe = DIFF * phys[0, 193:194, H[h]]
        os = DIFF * phys[0, 194:195, H[h]]
        on = DIFF * phys[0, 195:196, H[h]]
        coef[0, :, H[h]] = (1.0 - (ow + oe + os + on)) - pos(fe) + jnp.minimum(fw, 0.0) - pos(fn) + jnp.minimum(fs, 0.0)
        coef[1, :, H[h]] = oe - jnp.minimum(fe, 0.0)
        coef[2, :, H[h]] = ow + pos(fw)
        coef[3, :, H[h]] = on - jnp.minimum(fn, 0.0)
        coef[4, :, H[h]] = os + pos(fs)
        coef[5, :, H[h]] = jnp.where(level < LEV - 1, phys[0, 144:192, H[h]], 0.0)

    def mix(moved, k):
        flux = k * (pltpu.roll(moved, LEV - 1, 0) - moved)
        return moved + flux - pltpu.roll(flux, 1, 0)

    wide = lax.broadcasted_iota(jnp.int32, (HALF, 128), 1)
    flat = (wide // SIDE) % 2 == 0
    for p in range(2):
        hp = slice(p * HALF, (p + 1) * HALF)
        upper = rows[0, p, 1, :, :]
        under = roll(rows[0, p, 0, :, :], 32)
        cross[0, hp, :] = jnp.where(flat, upper, under)
        cross[1, hp, :] = jnp.where(flat, under, upper)
        for h in range(2):
            along[hp, H[h]] = jnp.where(wide % 2 == 0, roll(west[0, hp, H[h]], 128 - 15 - w_odd),
                                        roll(east[0, hp, H[h]], 15 - e_odd))

    def group(g, carry):
        for m in range(3):
            at = pl.ds(pl.multiple_of((3 * g + m) * LEV, LEV), LEV)
            hm = slice(m * LEV, (m + 1) * LEV)
            a = c_ref[0, at, H[0]]
            b = c_ref[0, at, H[1]]
            ends = roll(cross[lax.rem(g, 2), hm, :], 112 - 16 * g)
            an, bn = roll(a, 112), roll(b, 112)
            as_, bs = roll(a, 16), roll(b, 16)
            north = (jnp.where(high, bn, an), jnp.where(high, ends, bn))
            south = (jnp.where(low, ends, as_), jnp.where(low, as_, bs))
            for h, v in enumerate((a, b)):
                sides = roll(along[hm, H[h]], lax.rem(128 - 2 * g, 128))
                vw = jnp.where(at_w, sides, roll(v, 1))
                ve = jnp.where(at_e, sides, roll(v, 127))
                moved = (coef[0, :, H[h]] * v + coef[1, :, H[h]] * ve + coef[2, :, H[h]] * vw
                         + coef[3, :, H[h]] * north[h] + coef[4, :, H[h]] * south[h])
                out[0, at, H[h]] = mix(moved, coef[5, :, H[h]])
        return carry

    lax.fori_loop(0, 8, group, 0)
    absorb = 0.04 + 0.02 * (pos(out[0, 480:528, :]) + pos(out[0, 528:576, :]))
    above = depth(absorb)
    par_ref[...] = phys[0, 196:197, :] * jnp.exp(-(above + 0.5 * absorb))
    for h in range(2):
        wet = jnp.broadcast_to(phys[0, 197:198, H[h]], (8, 128))

        def chunk(i, carry):
            l0 = pl.multiple_of(i * 8, 8)

            def get(t):
                return out[0, pl.ds(pl.multiple_of(t * LEV + l0, 8), 8), H[h]]

            held = [get(t) for t in range(NTR)]

            def put(t, v):
                out[0, pl.ds(pl.multiple_of(t * LEV + l0, 8), 8), H[h]] = v * wet

            warm = jnp.exp(0.0639 * phys[0, pl.ds(pl.multiple_of(96 + l0, 8), 8), H[h]])
            par = par_ref[pl.ds(l0, 8), H[h]]
            react(lambda t: held[t], put, par, warm)
            return carry

        lax.fori_loop(0, LEV // 8, chunk, 0)


def first_kernel(tab, c_ref, phys, rows, west, east, out, rows_out, w_out, e_out, coef, par_ref, cross, along):
    j = pl.program_id(0)
    odd = j % 2

    @pl.when(tab[1, j] == 1)
    def _():
        slot_step(tab, c_ref, phys, rows, west, east, out, coef, par_ref, cross, along)

    @pl.when(tab[1, j] == 0)
    def _():
        out[...] = jnp.zeros_like(out)

    clear_first(odd, w_out, e_out)
    pack_edges(out, rows_out, w_out, e_out, odd)


def last_kernel(tab, c_ref, phys, rows, west, east, out, light_out, coef, par_ref, cross, along):
    j = pl.program_id(0)

    @pl.when(tab[1, j] == 1)
    def _():
        slot_step(tab, c_ref, phys, rows, west, east, out, coef, par_ref, cross, along)
        absorb = 0.04 + 0.02 * (pos(out[0, 480:528, :]) + pos(out[0, 528:576, :]))
        above = depth(absorb)
        light_out[0] = jnp.exp(-above) - jnp.exp(-(above + absorb))

    @pl.when(tab[1, j] == 0)
    def _():
        out[...] = jnp.zeros_like(out)
        light_out[...] = jnp.zeros_like(light_out)


def step(last, tab, current, phys, rows, came_west, came_east):
    edge_spec = pl.BlockSpec((1, ROWS3, CELLS), lambda j, tab: (j // 2, 0, 0))
    edge_shape = jax.ShapeDtypeStruct((4, ROWS3, CELLS), jnp.float32)
    if last:
        outs = [pl.BlockSpec((1, LEV, CELLS), lambda j, tab: (tab[4, j], 0, 0))]
        shapes = [jax.ShapeDtypeStruct((16, LEV, CELLS), jnp.float32)]
    else:
        outs = [pl.BlockSpec((1, 2, 2, HALF, 128), lambda j, tab: (tab[8, j], 0, 0, 0, 0)), edge_spec, edge_spec]
        shapes = [jax.ShapeDtypeStruct((8, 2, 2, HALF, 128), jnp.float32), edge_shape, edge_shape]
    return pl.pallas_call(
        last_kernel if last else first_kernel,
        grid_spec=pltpu.PrefetchScalarGridSpec(
            num_scalar_prefetch=1,
            grid=(SLOTS,),
            in_specs=[
                pl.BlockSpec((1, NTR * LEV, CELLS), lambda j, tab: (j, 0, 0)),
                pl.BlockSpec((1, PHYS, CELLS), lambda j, tab: (tab[0, j], 0, 0)),
                pl.BlockSpec((1, 2, 2, HALF, 128), lambda j, tab: (tab[7, j], 0, 0, 0, 0)),
                pl.BlockSpec((1, ROWS3, CELLS), lambda j, tab: (tab[2, j] // 2, 0, 0)),
                pl.BlockSpec((1, ROWS3, CELLS), lambda j, tab: (tab[3, j] // 2, 0, 0)),
            ],
            out_specs=[pl.BlockSpec((1, NTR * LEV, CELLS), lambda j, tab: (j, 0, 0))] + outs,
            scratch_shapes=[VM((6, LEV, CELLS), jnp.float32), VM((LEV, CELLS), jnp.float32),
                            VM((2, ROWS3, 128), jnp.float32), VM((ROWS3, CELLS), jnp.float32)],
        ),
        out_shape=[jax.ShapeDtypeStruct((SLOTS, NTR * LEV, CELLS), jnp.float32)] + shapes,
        cost_estimate=pl.CostEstimate(flops=10**8, bytes_accessed=25 * 10**6, transcendentals=10**6),
        name="last_step" if last else "first_step",
    )(tab, current, phys, rows, came_west, came_east)


def spread_matrix(shape, lhs_wide, dtype=jnp.bfloat16):
    i = lax.broadcasted_iota(jnp.int32, shape, 0)
    j = lax.broadcasted_iota(jnp.int32, shape, 1)
    return (i // 3 == j if lhs_wide else i == j // 3).astype(dtype)


def coarse_kernel(phys, mix, flags, y_ref, col_ref):
    r = pl.program_id(0)
    i = lax.broadcasted_iota(jnp.int32, (384, 128), 0)
    j = lax.broadcasted_iota(jnp.int32, (384, 128), 1)
    every = (i // 3 == j).astype(jnp.bfloat16)
    third = (i == 3 * j + 2).astype(jnp.bfloat16)

    def dot(a, b):
        return jnp.dot(a, b, preferred_element_type=jnp.float32)

    east = (dot(phys[0, 0:48, :], third) + dot(phys[1, 0:48, :], third) + dot(phys[2, 0:48, :], third)) / 3.0
    north = dot(phys[2, 48:96, :], every) / 3.0
    temp = (dot(phys[0, 96:144, :], every) + dot(phys[1, 96:144, :], every) + dot(phys[2, 96:144, :], every)) / 9.0
    east = east * flags[0, 1:2, :]
    y_ref[0, 0:48, :] = east
    y_ref[0, 48:96, :] = north * flags[0, 3:4, :]
    y_ref[0, 96:144, :] = temp
    y_ref[0, 144:192, :] = mix[0].astype(jnp.float32)
    y_ref[0, 192:200, :] = flags[0]

    @pl.when(r == 0)
    def _():
        col_ref[...] = jnp.zeros_like(col_ref)

    col_ref[...] = jnp.where(lanes() == r, roll(east, r + 1), col_ref[...])


def coarse(phys_t, mix_t, flags):
    return pl.pallas_call(
        coarse_kernel,
        grid=(SIDE,),
        in_specs=[
            pl.BlockSpec((3, 144, 384), lambda r: (r, 0, 0)),
            pl.BlockSpec((1, LEV, 128), lambda r: (r, 0, 0)),
            pl.BlockSpec((1, 8, 128), lambda r: (r, 0, 0)),
        ],
        out_specs=[
            pl.BlockSpec((1, 200, 128), lambda r: (r, 0, 0)),
            pl.BlockSpec((LEV, 128), lambda r: (0, 0)),
        ],
        out_shape=[
            jax.ShapeDtypeStruct((SIDE, 200, 128), jnp.float32),
            jax.ShapeDtypeStruct((LEV, 128), jnp.float32),
        ],
        cost_estimate=pl.CostEstimate(flops=10**9, bytes_accessed=8 * 10**6, transcendentals=0),
        name="coarse",
    )(phys_t, mix_t, flags)


def package_kernel(tab, y_ref, col_ref, row_ref, out):
    k = pl.program_id(0)
    lane = lanes()
    group = lane // SIDE
    for f in range(5):
        n = 48 if f < 4 else 8
        at = slice(48 * f, 48 * f + n)
        for h in range(2):
            acc = jnp.zeros((n, 128), jnp.float32)
            for g in range(8):
                turned = roll(y_ref[8 * h + g, at, :], (16 * g - 16 * k + 128) % 128)
                acc = jnp.where(group[:n] == g, turned, acc)
            out[0, at, 128 * h:128 * h + 128] = acc
    west = col_ref[...]
    for r in range(SIDE):
        turned = roll(y_ref[r, 0:48, :], (r + 1 - 16 * k + 128) % 128)
        west = jnp.where((lane == r) & (k > 0), turned, west)
    edge = jnp.where(lane < 16, west, roll(row_ref[...], (16 - 16 * k + 128) % 128))
    out[0, 200:224, 0:128] = edge[0:24]
    out[0, 200:224, 128:256] = edge[24:48]


def package(tab, y, col, row):
    return pl.pallas_call(
        package_kernel,
        grid_spec=pltpu.PrefetchScalarGridSpec(
            num_scalar_prefetch=1,
            grid=(TILE,),
            in_specs=[
                pl.BlockSpec((SIDE, 200, 128), lambda k, tab: (0, 0, 0)),
                pl.BlockSpec((LEV, 128), lambda k, tab: (0, 0)),
                pl.BlockSpec((LEV, 128), lambda k, tab: (0, 0)),
            ],
            out_specs=pl.BlockSpec((1, PHYS, CELLS), lambda k, tab: (tab[6, k], 0, 0)),
        ),
        out_shape=jax.ShapeDtypeStruct((16, PHYS, CELLS), jnp.float32),
        cost_estimate=pl.CostEstimate(flops=10**7, bytes_accessed=4 * 10**6, transcendentals=0),
        name="package",
    )(tab, y, col, row)


MESH = pl.DeviceIdType.MESH


def halo_kernel(tab, up_ref, w_ref, e_ref, rows_ref, from_w, from_e, got_s, got_n, pick,
                up_send, up_recv, dn_send, dn_recv, we_send, we_recv):
    lat, lon = lax.axis_index("lat"), lax.axis_index("lon")
    bands, count = lax.axis_size("lat"), lax.axis_size("lon")
    sides = (lax.rem(lat + 1, bands), lax.rem(lat + bands - 1, bands))
    got = (got_s, got_n)
    barrier = pltpu.get_barrier_semaphore()

    def greet(d, carry):
        peer = lax.rem(lon + d, count)
        for side in sides:
            pl.semaphore_signal(barrier, inc=1, device_id=(side, peer), device_id_type=MESH)
        return carry

    def greet_band(d, carry):
        pl.semaphore_signal(barrier, inc=1, device_id=(lat, lax.rem(lon + d, count)), device_id_type=MESH)
        return carry

    lax.fori_loop(0, count, greet, 0)
    lax.fori_loop(1, count, greet_band, 0)
    pl.semaphore_wait(barrier, 3 * count - 1)

    def up(n, d):
        peer = lax.rem(lon + d, count)
        return pltpu.make_async_remote_copy(
            src_ref=up_ref.at[peer, 1 - n], dst_ref=got[n].at[lon],
            send_sem=up_send.at[n, d], recv_sem=up_recv.at[n, d],
            device_id=(sides[n], peer), device_id_type=MESH)

    def up_from(n, d):
        peer = lax.rem(lon + count - d, count)
        return pltpu.make_async_remote_copy(
            src_ref=up_ref.at[peer, 1 - n], dst_ref=got[n].at[peer],
            send_sem=up_send.at[n, d], recv_sem=up_recv.at[n, d],
            device_id=(sides[1 - n], peer), device_id_type=MESH)

    def down(n, d):
        peer = lax.rem(lon + d, count)
        return pltpu.make_async_remote_copy(
            src_ref=pick.at[n, peer], dst_ref=rows_ref.at[lon, n],
            send_sem=dn_send.at[n, d], recv_sem=dn_recv.at[n, d],
            device_id=(lat, peer), device_id_type=MESH)

    def down_from(n, d):
        peer = lax.rem(lon + count - d, count)
        return pltpu.make_async_remote_copy(
            src_ref=pick.at[n, peer], dst_ref=rows_ref.at[peer, n],
            send_sem=dn_send.at[n, d], recv_sem=dn_recv.at[n, d],
            device_id=(lat, peer), device_id_type=MESH)

    def each(first, fn):
        def body(d, carry):
            fn(d)
            return carry
        lax.fori_loop(first, count, body, 0)

    to_e = pltpu.make_async_remote_copy(
        src_ref=e_ref, dst_ref=from_w, send_sem=we_send.at[0], recv_sem=we_recv.at[0],
        device_id=(lat, lax.rem(lon + 1, count)), device_id_type=MESH)
    to_w = pltpu.make_async_remote_copy(
        src_ref=w_ref, dst_ref=from_e, send_sem=we_send.at[1], recv_sem=we_recv.at[1],
        device_id=(lat, lax.rem(lon + count - 1, count)), device_id_type=MESH)

    for n in range(2):
        each(0, lambda d: up(n, d).start())
    to_e.start()
    to_w.start()
    for n in range(2):
        each(0, lambda d: up_from(n, d).wait_recv())

        def choose(o):
            value = got[n][tab[2 * n, o]]
            pick[n, o] = jnp.where(tab[2 * n + 1, o] > 0, value, 0.0)

        each(0, choose)
        rows_ref[lon, n] = pick[n, lon]
        each(1, lambda d: down(n, d).start())
    for n in range(2):
        each(1, lambda d: down_from(n, d).wait_recv())
    to_e.wait()
    to_w.wait()
    for n in range(2):
        each(0, lambda d: up(n, d).wait_send())
        each(1, lambda d: down(n, d).wait_send())


def halo(tab, rows, w_out, e_out):
    anywhere = pl.BlockSpec(memory_space=pl.ANY)
    here = pl.BlockSpec(memory_space=VM)
    edge = jax.ShapeDtypeStruct((4, ROWS3, CELLS), jnp.float32)
    dma = pltpu.SemaphoreType.DMA
    rows, from_w, from_e = pl.pallas_call(
        halo_kernel,
        in_specs=[pl.BlockSpec(memory_space=pltpu.SMEM), here, anywhere, anywhere],
        out_specs=[here, anywhere, anywhere],
        out_shape=[jax.ShapeDtypeStruct((16, 2, HALF, 128), jnp.float32), edge, edge],
        scratch_shapes=[VM((16, HALF, 128), jnp.float32), VM((16, HALF, 128), jnp.float32),
                        VM((2, 16, HALF, 128), jnp.float32),
                        dma((2, 16)), dma((2, 16)), dma((2, 16)), dma((2, 16)), dma((2,)), dma((2,))],
        compiler_params=pltpu.CompilerParams(collective_id=1, has_side_effects=True),
        cost_estimate=pl.CostEstimate(flops=10**6, bytes_accessed=10**8, transcendentals=0),
        name="halo",
    )(tab, rows.reshape(16, 2, HALF, 128), w_out, e_out)
    return rows.reshape(8, 2, 2, HALF, 128), from_w, from_e


def heat_kernel(tab, got, wet, light, out, fine):
    lane = lanes()
    group = lane // SIDE
    for r in range(SIDE):
        half = slice(128 * (r // 8), 128 * (r // 8) + 128)
        acc = jnp.zeros((LEV, 128), jnp.float32)
        for k in range(TILE):
            acc = jnp.where(group == k, roll(got[tab[6, k], :, half], (16 * k - 16 * (r % 8)) % 128), acc)
        acc = jnp.where(wet[r:r + 1, :] > 0.0, acc, 0.0)
        for a in range(3):
            fine[pl.ds(3 * r + a, LEV, stride=LEV), :] = acc
    spread = spread_matrix((128, 384), False)
    stacked = jnp.concatenate([spread] * 3, axis=0)

    def level(l, carry):
        x = fine[pl.ds(pl.multiple_of(l * LEV, LEV), LEV), :]
        high = x.astype(jnp.bfloat16)
        rest = x - high.astype(jnp.float32)
        mid = rest.astype(jnp.bfloat16)
        low = (rest - mid.astype(jnp.float32)).astype(jnp.bfloat16)
        wide = jnp.dot(jnp.concatenate([high, mid, low], axis=1), stacked,
                       preferred_element_type=jnp.float32)
        out[l] = (light[...] * wide).astype(jnp.bfloat16)
        return carry

    lax.fori_loop(0, LEV, level, 0)


def heat(tab, got, wet, light):
    return pl.pallas_call(
        heat_kernel,
        in_specs=[pl.BlockSpec(memory_space=pltpu.SMEM)] + [pl.BlockSpec(memory_space=VM)] * 3,
        out_specs=pl.BlockSpec(memory_space=VM),
        out_shape=jax.ShapeDtypeStruct((LEV, 48, 384), jnp.bfloat16),
        scratch_shapes=[VM((LEV * LEV, 128), jnp.float32)],
        cost_estimate=pl.CostEstimate(flops=10**9, bytes_accessed=3 * 10**6, transcendentals=0),
        name="heat",
    )(tab, got, wet, light)


def tables(band, lat, lon):
    wet = band >= 0
    owner = band // SLOTS % 16
    tile = jnp.arange(128) // TILE
    slot_code = (lat * 16 + lon) * SLOTS + jnp.arange(SLOTS)
    hit = band[None, :] == slot_code[:, None]
    full = jnp.any(hit, axis=1)
    block = jnp.sum(jnp.where(hit, jnp.arange(128)[None, :], 0), axis=1)
    west = jnp.sum(jnp.where(jnp.roll(hit, -1, axis=1), band[None, :], 0), axis=1)
    east = jnp.sum(jnp.where(jnp.roll(hit, 1, axis=1), band[None, :], 0), axis=1)
    src = jnp.where(full, block // TILE, 0)
    used = jnp.any((src[None, :] == jnp.arange(16)[:, None]) & full[None, :], axis=1)
    spare = jnp.argmin(used).astype(jnp.int32)
    pair_used = jnp.any(used.reshape(8, 2), axis=1)
    pair_spare = jnp.argmin(pair_used).astype(jnp.int32)
    w_slot = jnp.where(full & (west >= 0), west % SLOTS, 0)
    e_slot = jnp.where(full & (east >= 0), east % SLOTS, 0)
    mine = lax.dynamic_slice_in_dim(band, lon * TILE, TILE)
    t_wet = mine >= 0
    t_own = mine // SLOTS % 16
    t_used = jnp.any((t_own[None, :] == jnp.arange(16)[:, None]) & t_wet[None, :], axis=1)
    t_spare = jnp.argmin(t_used).astype(jnp.int32)
    rows = [src, full, w_slot, e_slot, jnp.where(full, src, spare), t_wet, jnp.where(t_wet, t_own, t_spare), src // 2, jnp.where(full, src // 2, pair_spare)]
    return jnp.stack([r.astype(jnp.int32) for r in rows])


def meeting(band, south, north, lon):
    first = lon // 2 * 16

    def cut(row):
        return lax.dynamic_slice_in_dim(row, first, 16)

    mine = cut(band)
    hit = ((mine // SLOTS % 16)[None, :] == jnp.arange(16)[:, None]) & (mine >= 0)[None, :]
    rows = []
    for other in (cut(south), cut(north)):
        rows.append(jnp.sum(jnp.where(hit & (other >= 0)[None, :], (other // SLOTS % 16)[None, :], 0), axis=1))
        rows.append(jnp.any(hit & (other >= 0)[None, :], axis=1))
    return jnp.stack([r.astype(jnp.int32) for r in rows])


def shift(x, axis, by, closed=True):
    n = lax.axis_size(axis)
    return lax.ppermute(x, axis, [(i, (i + by) % n) for i in range(n) if closed or 0 <= i + by < n])


def swap(x):
    return lax.all_to_all(x, "lon", split_axis=0, concat_axis=0, tiled=True)


def on_device(tracers, phys_fine, mix_coarse, surf_light, land_mask, owner_map):
    tab = tables(owner_map[0], lax.axis_index("lat"), lax.axis_index("lon"))
    wet = land_mask.astype(jnp.float32)
    wet_s = shift(wet[-1], "lat", 1, False)
    wet_n = shift(wet[0], "lat", -1, False)
    wet_w = shift(wet[:, -1], "lon", 1)
    wet_e = shift(wet[:, 0], "lon", -1)
    band = owner_map[0]
    meet = meeting(band, shift(band, "lat", 1), shift(band, "lat", -1), lax.axis_index("lon"))
    rows_out, w_out, e_out = pack(tab, tracers)
    open_e = wet * jnp.concatenate([wet[:, 1:], wet_e[:, None]], axis=1)
    open_w = wet * jnp.concatenate([wet_w[:, None], wet[:, :-1]], axis=1)
    open_n = wet * jnp.concatenate([wet[1:], wet_n[None]], axis=0)
    open_s = wet * jnp.concatenate([wet_s[None], wet[:-1]], axis=0)
    light = jnp.dot(surf_light, spread_matrix((384, 128), True, jnp.float32),
                    precision=lax.Precision.HIGHEST).reshape(SIDE, 3, 128)
    light = (light[:, 0] + light[:, 1] + light[:, 2]) / 9.0
    blank = jnp.zeros_like(wet)
    flags = jnp.stack([open_w, open_e, open_s, open_n, light, wet, blank, blank], axis=1)
    y, col = coarse(jnp.swapaxes(phys_fine, 1, 2), jnp.swapaxes(mix_coarse, 1, 2), flags)
    col = shift(col, "lon", 1)
    row = shift(y[SIDE - 1, 48:96], "lat", 1)
    phys = swap(package(tab, y, col, row))
    current = tracers
    for n in range(2):
        rows, came_west, came_east = halo(meet, rows_out, w_out, e_out)
        if n == 0:
            current, rows_out, w_out, e_out = step(False, tab, current, phys, rows, came_west, came_east)
        else:
            current, light_part = step(True, tab, current, phys, rows, came_west, came_east)
    return current, heat(tab, swap(light_part), wet, surf_light)


def solution(mesh):
    in_specs = (
        P(("lat", "lon"), None, None),
        P("lat", "lon", None),
        P("lat", "lon", None),
        P("lat", "lon"),
        P("lat", "lon"),
        P("lat", None),
    )
    out_specs = (P(("lat", "lon"), None, None), P(None, "lat", "lon"))
    return jax.shard_map(
        on_device, mesh=mesh, in_specs=in_specs, out_specs=out_specs, check_vma=False
    )
```

```python
import functools

import jax
import jax.numpy as jnp
from jax import lax
from jax.experimental import pallas as pl
from jax.experimental.pallas import tpu as pltpu
from jax.sharding import PartitionSpec as P

NTR = 24
LEV = 48
SIDE = 16
CELLS = 256
SLOTS = 8
TILE = 8
PHYS = 224
DIFF = 0.08
VM = pltpu.VMEM
ROWS3 = 3 * LEV
HALF = ROWS3 // 2


def pos(v):
    return jnp.maximum(v, 0.0)


def lanes():
    return lax.broadcasted_iota(jnp.int32, (LEV, 128), 1)


def roll(x, shift):
    return pltpu.roll(x, shift, 1)


def pack_edges(c_ref, rows_ref, w_ref, e_ref, odd):
    lane = lanes()
    group = lane // SIDE
    col = lane % SIDE
    even = lane % 2 == 0
    low = lane < SIDE
    for m in range(3):
        blank = jnp.zeros((LEV, 128), jnp.float32)
        ends = [blank, blank]
        both = [blank, blank]
        for g in range(8):
            t = 3 * g + m
            a = c_ref[0, t * LEV:(t + 1) * LEV, 0:128]
            b = c_ref[0, t * LEV:(t + 1) * LEV, 128:256]
            end = jnp.where(low, a, b)
            ends[g % 2] = jnp.where((group == g) | (group == (g + 7) % 8), roll(end, 16 * g) if g else end, ends[g % 2])
            here = (col == 2 * g) | (col == (2 * g + 15) % 16)
            for h, v in enumerate((a, b)):
                both[h] = jnp.where(here, roll(v, 2 * g) if g else v, both[h])
        flat = group % 2 == 0
        put_rows(rows_ref, 0, m, jnp.where(flat, ends[0], ends[1]))
        put_rows(rows_ref, 1, m, jnp.where(flat, ends[1], ends[0]))
        at = slice(m * LEV, (m + 1) * LEV)
        mine = (lane % 2) == odd
        for h in range(2):
            hs = slice(h * 128, (h + 1) * 128)
            turned = roll(both[h], odd)
            w_ref[0, at, hs] = jnp.where(mine, turned, w_ref[0, at, hs])
            e_ref[0, at, hs] = jnp.where(mine, e_ref[0, at, hs], turned)


def put_rows(rows_ref, d, m, x):
    lo = m * LEV
    if lo < HALF:
        n = min(LEV, HALF - lo)
        rows_ref[0, 0, d, lo:lo + n, :] = x[:n]
        if n < LEV:
            rows_ref[0, 1, d, 0:LEV - n, :] = x[n:]
    else:
        rows_ref[0, 1, d, lo - HALF:lo - HALF + LEV, :] = x


def clear_first(odd, *refs):
    @pl.when(odd == 0)
    def _():
        for ref in refs:
            ref[...] = jnp.zeros_like(ref)


def pack_kernel(tab, c_ref, rows_ref, w_ref, e_ref):
    odd = pl.program_id(0) % 2
    clear_first(odd, w_ref, e_ref)
    pack_edges(c_ref, rows_ref, w_ref, e_ref, odd)


def pack(tab, tracers):
    return pl.pallas_call(
        pack_kernel,
        grid_spec=pltpu.PrefetchScalarGridSpec(
            num_scalar_prefetch=1,
            grid=(SLOTS,),
            in_specs=[pl.BlockSpec((1, NTR * LEV, CELLS), lambda j, tab: (j, 0, 0))],
            out_specs=[
                pl.BlockSpec((1, 2, 2, HALF, 128), lambda j, tab: (tab[8, j], 0, 0, 0, 0)),
                pl.BlockSpec((1, ROWS3, CELLS), lambda j, tab: (j // 2, 0, 0)),
                pl.BlockSpec((1, ROWS3, CELLS), lambda j, tab: (j // 2, 0, 0)),
            ],
        ),
        out_shape=[
            jax.ShapeDtypeStruct((8, 2, 2, HALF, 128), jnp.float32),
            jax.ShapeDtypeStruct((4, ROWS3, CELLS), jnp.float32),
            jax.ShapeDtypeStruct((4, ROWS3, CELLS), jnp.float32),
        ],
        cost_estimate=pl.CostEstimate(flops=10**7, bytes_accessed=12 * 10**6, transcendentals=0),
        name="pack",
    )(tab, tracers)


def react(get, put, par, warm):
    (carbon_dis, alkalinity, oxygen, nitrate, ammonium, phosphate, silicate, iron_free,
     nano_carbon, diat_carbon, nano_chl, diat_chl, nano_iron, diat_iron, diat_silica,
     micro_zoo, meso_zoo, dissolved_org, small_part, big_part, small_iron, big_iron,
     big_silica, calcite) = [functools.partial(get, t) for t in range(NTR)]
    p_am = pos(ammonium())
    nitrogen = pos(nitrate()) + p_am
    limit_nitro = nitrogen / (0.5 + nitrogen)
    p_ph = pos(phosphate())
    p_fe = pos(iron_free())
    p_si = pos(silicate())
    nutr_nano = jnp.minimum(jnp.minimum(limit_nitro, p_ph / (0.3 + p_ph)), p_fe / (0.2 + p_fe))
    nutr_diat = jnp.minimum(nutr_nano, p_si / (1.0 + p_si))
    nc = nano_carbon()
    dc = diat_carbon()
    wp = warm * par
    prod_nano = 0.1 * wp / (par + 0.5) * nutr_nano * nc
    prod_diat = 0.12 * wp / (par + 1.0) * nutr_diat * dc
    share = (p_am + 0.01) / (nitrogen + 0.02)
    mi = micro_zoo()
    me = meso_zoo()
    graze_nano = 0.08 * warm * mi / (1.0 + pos(nc))
    graze_diat = 0.06 * warm * me / (1.0 + pos(dc))
    loss_nano = graze_nano + 0.02
    loss_diat = graze_diat + 0.02
    eaten_nano = graze_nano * nc
    eaten_diat = graze_diat * dc
    death_micro = 0.03 * mi * pos(mi)
    death_meso = 0.03 * me * pos(me)
    do = dissolved_org()
    sp = small_part()
    bp = big_part()
    remin_doc = 0.03 * warm * do
    remin_poc = 0.02 * warm * sp
    remin_goc = 0.01 * warm * bp
    am = ammonium()
    nitrify = 0.05 * am
    cal = calcite()
    melt_cal = 0.01 * cal
    uptake = prod_nano + prod_diat
    remin = remin_doc + remin_poc + remin_goc
    calcify = 0.02 * prod_nano
    shell = melt_cal - calcify
    put(0, carbon_dis() + remin - uptake + shell)
    su = share * uptake
    fresh = uptake - su
    put(1, alkalinity() + 2.0 * shell + 0.16 * (fresh - nitrify))
    put(2, oxygen() + 1.3 * (uptake - remin) - 0.32 * nitrify)
    put(3, nitrate() + 0.16 * (nitrify - fresh))
    put(4, am + 0.16 * (remin - su - nitrify))
    put(5, phosphate() + 0.01 * (remin - uptake))
    bsi = big_silica()
    melt_si = 0.02 * bsi
    put(6, silicate() + melt_si - 0.15 * prod_diat)
    sfe = small_iron()
    bfe = big_iron()
    melt_sfe = 0.02 * sfe
    melt_bfe = 0.01 * bfe
    put(7, iron_free() + melt_sfe + melt_bfe - 0.005 * uptake)
    put(8, nc + prod_nano - loss_nano * nc)
    put(9, dc + prod_diat - loss_diat * dc)
    x = nano_chl()
    put(10, x + 0.03 * prod_nano - loss_nano * x)
    x = diat_chl()
    put(11, x + 0.03 * prod_diat - loss_diat * x)
    x = nano_iron()
    lost = loss_nano * x
    put(12, x + 0.005 * prod_nano - lost)
    put(20, sfe + lost - melt_sfe)
    x = diat_iron()
    lost = loss_diat * x
    put(13, x + 0.005 * prod_diat - lost)
    put(21, bfe + lost - melt_bfe)
    x = diat_silica()
    lost = loss_diat * x
    put(14, x + 0.15 * prod_diat - lost)
    put(22, bsi + lost - melt_si)
    put(15, mi + 0.3 * eaten_nano - death_micro)
    put(16, me + 0.3 * eaten_diat - death_meso)
    put(17, do + 0.3 * eaten_nano + 0.02 * nc - remin_doc)
    put(18, sp + 0.4 * eaten_nano + death_micro - remin_poc)
    put(19, bp + 0.4 * eaten_diat + 0.02 * dc + death_meso - remin_goc)
    put(23, cal - shell)


def tri():
    i = lax.broadcasted_iota(jnp.int32, (LEV, LEV), 0)
    j = lax.broadcasted_iota(jnp.int32, (LEV, LEV), 1)
    return (j < i).astype(jnp.float32)


def depth(absorb):
    return jnp.dot(tri(), absorb, precision=lax.Precision.HIGHEST,
                   preferred_element_type=jnp.float32)


def slot_step(tab, c_ref, phys, rows, west, east, out, coef, par_ref, cross, along):
    j = pl.program_id(0)
    w_odd = tab[2, j] % 2
    e_odd = tab[3, j] % 2
    lane = lanes()
    col = lane % SIDE
    at_w = col == 0
    at_e = col == SIDE - 1
    low = lane < 16
    high = lane >= 112
    H = (slice(0, 128), slice(128, 256))
    edge = jnp.concatenate([phys[0, 200:224, 0:128], phys[0, 200:224, 128:256]], axis=0)
    sel_r = lax.broadcasted_iota(jnp.int32, (128, 256), 0)
    sel_c = lax.broadcasted_iota(jnp.int32, (128, 256), 1)
    sel = ((sel_c == SIDE * sel_r) & (sel_r < SIDE)).astype(jnp.float32)
    edge_lane = jnp.where(low, edge, 0.0)
    edge_w = jnp.dot(edge_lane, sel, precision=lax.Precision.HIGHEST,
                     preferred_element_type=jnp.float32)
    edge_s = roll(edge, 112)
    fn_up = roll(phys[0, 48:96, H[0]], 16)
    level = lax.broadcasted_iota(jnp.int32, (LEV, 128), 0)
    for h in range(2):
        fe = phys[0, 0:48, H[h]]
        fn = phys[0, 48:96, H[h]]
        fw = jnp.where(at_w, edge_w[:, H[h]], roll(fe, 1))
        if h == 0:
            fs = jnp.where(low, edge_s, fn_up)
        else:
            fs = jnp.where(low, fn_up, roll(fn, 16))
        ow = DIFF * phys[0, 192:193, H[h]]
        oe = DIFF * phys[0, 193:194, H[h]]
        os = DIFF * phys[0, 194:195, H[h]]
        on = DIFF * phys[0, 195:196, H[h]]
        coef[0, :, H[h]] = (1.0 - (ow + oe + os + on)) - pos(fe) + jnp.minimum(fw, 0.0) - pos(fn) + jnp.minimum(fs, 0.0)
        coef[1, :, H[h]] = oe - jnp.minimum(fe, 0.0)
        coef[2, :, H[h]] = ow + pos(fw)
        coef[3, :, H[h]] = on - jnp.minimum(fn, 0.0)
        coef[4, :, H[h]] = os + pos(fs)
        coef[5, :, H[h]] = jnp.where(level < LEV - 1, phys[0, 144:192, H[h]], 0.0)

    def mix(moved, k):
        flux = k * (pltpu.roll(moved, LEV - 1, 0) - moved)
        return moved + flux - pltpu.roll(flux, 1, 0)

    wide = lax.broadcasted_iota(jnp.int32, (HALF, 128), 1)
    flat = (wide // SIDE) % 2 == 0
    for p in range(2):
        hp = slice(p * HALF, (p + 1) * HALF)
        upper = rows[0, p, 1, :, :]
        under = roll(rows[0, p, 0, :, :], 32)
        cross[0, hp, :] = jnp.where(flat, upper, under)
        cross[1, hp, :] = jnp.where(flat, under, upper)
        for h in range(2):
            along[hp, H[h]] = jnp.where(wide % 2 == 0, roll(west[0, hp, H[h]], 128 - 15 - w_odd),
                                        roll(east[0, hp, H[h]], 15 - e_odd))

    def group(g, carry):
        for m in range(3):
            at = pl.ds(pl.multiple_of((3 * g + m) * LEV, LEV), LEV)
            hm = slice(m * LEV, (m + 1) * LEV)
            a = c_ref[0, at, H[0]]
            b = c_ref[0, at, H[1]]
            ends = roll(cross[lax.rem(g, 2), hm, :], 112 - 16 * g)
            an, bn = roll(a, 112), roll(b, 112)
            as_, bs = roll(a, 16), roll(b, 16)
            north = (jnp.where(high, bn, an), jnp.where(high, ends, bn))
            south = (jnp.where(low, ends, as_), jnp.where(low, as_, bs))
            for h, v in enumerate((a, b)):
                sides = roll(along[hm, H[h]], lax.rem(128 - 2 * g, 128))
                vw = jnp.where(at_w, sides, roll(v, 1))
                ve = jnp.where(at_e, sides, roll(v, 127))
                moved = (coef[0, :, H[h]] * v + coef[1, :, H[h]] * ve + coef[2, :, H[h]] * vw
                         + coef[3, :, H[h]] * north[h] + coef[4, :, H[h]] * south[h])
                out[0, at, H[h]] = mix(moved, coef[5, :, H[h]])
        return carry

    lax.fori_loop(0, 8, group, 0)
    absorb = 0.04 + 0.02 * (pos(out[0, 480:528, :]) + pos(out[0, 528:576, :]))
    above = depth(absorb)
    par_ref[...] = phys[0, 196:197, :] * jnp.exp(-(above + 0.5 * absorb))
    for h in range(2):
        wet = jnp.broadcast_to(phys[0, 197:198, H[h]], (8, 128))

        def chunk(i, carry):
            l0 = pl.multiple_of(i * 8, 8)

            def get(t):
                return out[0, pl.ds(pl.multiple_of(t * LEV + l0, 8), 8), H[h]]

            held = [get(t) for t in range(NTR)]

            def put(t, v):
                out[0, pl.ds(pl.multiple_of(t * LEV + l0, 8), 8), H[h]] = v * wet

            warm = jnp.exp(0.0639 * phys[0, pl.ds(pl.multiple_of(96 + l0, 8), 8), H[h]])
            par = par_ref[pl.ds(l0, 8), H[h]]
            react(lambda t: held[t], put, par, warm)
            return carry

        lax.fori_loop(0, LEV // 8, chunk, 0)


def first_kernel(tab, c_ref, phys, rows, west, east, out, rows_out, w_out, e_out, coef, par_ref, cross, along):
    j = pl.program_id(0)
    odd = j % 2

    @pl.when(tab[1, j] == 1)
    def _():
        slot_step(tab, c_ref, phys, rows, west, east, out, coef, par_ref, cross, along)

    @pl.when(tab[1, j] == 0)
    def _():
        out[...] = jnp.zeros_like(out)

    clear_first(odd, w_out, e_out)
    pack_edges(out, rows_out, w_out, e_out, odd)


def last_kernel(tab, c_ref, phys, rows, west, east, out, light_out, coef, par_ref, cross, along):
    j = pl.program_id(0)

    @pl.when(tab[1, j] == 1)
    def _():
        slot_step(tab, c_ref, phys, rows, west, east, out, coef, par_ref, cross, along)
        absorb = 0.04 + 0.02 * (pos(out[0, 480:528, :]) + pos(out[0, 528:576, :]))
        above = depth(absorb)
        light_out[0] = jnp.exp(-above) - jnp.exp(-(above + absorb))

    @pl.when(tab[1, j] == 0)
    def _():
        out[...] = jnp.zeros_like(out)
        light_out[...] = jnp.zeros_like(light_out)


def step(last, tab, current, phys, rows, came_west, came_east):
    edge_spec = pl.BlockSpec((1, ROWS3, CELLS), lambda j, tab: (j // 2, 0, 0))
    edge_shape = jax.ShapeDtypeStruct((4, ROWS3, CELLS), jnp.float32)
    if last:
        outs = [pl.BlockSpec((1, LEV, CELLS), lambda j, tab: (tab[4, j], 0, 0))]
        shapes = [jax.ShapeDtypeStruct((16, LEV, CELLS), jnp.float32)]
    else:
        outs = [pl.BlockSpec((1, 2, 2, HALF, 128), lambda j, tab: (tab[8, j], 0, 0, 0, 0)), edge_spec, edge_spec]
        shapes = [jax.ShapeDtypeStruct((8, 2, 2, HALF, 128), jnp.float32), edge_shape, edge_shape]
    return pl.pallas_call(
        last_kernel if last else first_kernel,
        grid_spec=pltpu.PrefetchScalarGridSpec(
            num_scalar_prefetch=1,
            grid=(SLOTS,),
            in_specs=[
                pl.BlockSpec((1, NTR * LEV, CELLS), lambda j, tab: (j, 0, 0)),
                pl.BlockSpec((1, PHYS, CELLS), lambda j, tab: (tab[10, j], 0, 0)),
                pl.BlockSpec((1, 2, 2, HALF, 128), lambda j, tab: (tab[7, j], 0, 0, 0, 0)),
                pl.BlockSpec((1, ROWS3, CELLS), lambda j, tab: (tab[2, j] // 2, 0, 0)),
                pl.BlockSpec((1, ROWS3, CELLS), lambda j, tab: (tab[3, j] // 2, 0, 0)),
            ],
            out_specs=[pl.BlockSpec((1, NTR * LEV, CELLS), lambda j, tab: (j, 0, 0))] + outs,
            scratch_shapes=[VM((6, LEV, CELLS), jnp.float32), VM((LEV, CELLS), jnp.float32),
                            VM((2, ROWS3, 128), jnp.float32), VM((ROWS3, CELLS), jnp.float32)],
        ),
        out_shape=[jax.ShapeDtypeStruct((SLOTS, NTR * LEV, CELLS), jnp.float32)] + shapes,
        cost_estimate=pl.CostEstimate(flops=10**8, bytes_accessed=25 * 10**6, transcendentals=10**6),
        name="last_step" if last else "first_step",
    )(tab, current, phys, rows, came_west, came_east)


def spread_matrix(shape, lhs_wide, dtype=jnp.bfloat16):
    i = lax.broadcasted_iota(jnp.int32, shape, 0)
    j = lax.broadcasted_iota(jnp.int32, shape, 1)
    return (i // 3 == j if lhs_wide else i == j // 3).astype(dtype)


def coarse_kernel(phys, mix, flags, y_ref, col_ref, every_ref, third_ref):
    step = pl.program_id(0)

    @pl.when(step == 0)
    def _():
        i = lax.broadcasted_iota(jnp.int32, (384, 128), 0)
        j = lax.broadcasted_iota(jnp.int32, (384, 128), 1)
        every_ref[...] = (i // 3 == j).astype(jnp.bfloat16)
        third_ref[...] = (i == 3 * j + 2).astype(jnp.bfloat16)
        col_ref[...] = jnp.zeros_like(col_ref)

    def dot(a, b):
        return jnp.dot(a, b, preferred_element_type=jnp.float32)

    u = jnp.concatenate([phys[f, 0:48, :] for f in range(6)], axis=0)
    vt = jnp.concatenate([phys[2, 48:96, :], phys[5, 48:96, :]] + [phys[f, 96:144, :] for f in range(6)], axis=0)
    east = dot(u, third_ref[...])
    rest = dot(vt, every_ref[...])

    def part(x, n):
        return x[48 * n:48 * n + 48]

    for c in range(2):
        e = (part(east, 3 * c) + part(east, 3 * c + 1) + part(east, 3 * c + 2)) / 3.0 * flags[c, 1:2, :]
        y_ref[c, 0:48, :] = e
        y_ref[c, 48:96, :] = part(rest, c) / 3.0 * flags[c, 3:4, :]
        y_ref[c, 96:144, :] = (part(rest, 3 * c + 2) + part(rest, 3 * c + 3) + part(rest, 3 * c + 4)) / 9.0
        y_ref[c, 144:192, :] = mix[c].astype(jnp.float32)
        y_ref[c, 192:200, :] = flags[c]
        r = 2 * step + c
        col_ref[...] = jnp.where(lanes() == r, roll(e, r + 1), col_ref[...])


def coarse(phys_t, mix_t, flags):
    return pl.pallas_call(
        coarse_kernel,
        grid=(SIDE // 2,),
        in_specs=[
            pl.BlockSpec((6, 144, 384), lambda r: (r, 0, 0)),
            pl.BlockSpec((2, LEV, 128), lambda r: (r, 0, 0)),
            pl.BlockSpec((2, 8, 128), lambda r: (r, 0, 0)),
        ],
        out_specs=[
            pl.BlockSpec((2, 200, 128), lambda r: (r, 0, 0)),
            pl.BlockSpec((LEV, 128), lambda r: (0, 0)),
        ],
        out_shape=[
            jax.ShapeDtypeStruct((SIDE, 200, 128), jnp.float32),
            jax.ShapeDtypeStruct((LEV, 128), jnp.float32),
        ],
        scratch_shapes=[VM((384, 128), jnp.bfloat16), VM((384, 128), jnp.bfloat16)],
        cost_estimate=pl.CostEstimate(flops=10**9, bytes_accessed=8 * 10**6, transcendentals=0),
        name="coarse",
    )(phys_t, mix_t, flags)


def package_kernel(tab, y_ref, col_ref, row_ref, out):
    k = pl.program_id(0)
    lane = lanes()
    group = lane // SIDE
    for f in range(5):
        n = 48 if f < 4 else 8
        at = slice(48 * f, 48 * f + n)
        for h in range(2):
            acc = jnp.zeros((n, 128), jnp.float32)
            for g in range(8):
                turned = roll(y_ref[8 * h + g, at, :], (16 * g - 16 * k + 128) % 128)
                acc = jnp.where(group[:n] == g, turned, acc)
            out[0, at, 128 * h:128 * h + 128] = acc
    west = col_ref[...]
    for r in range(SIDE):
        turned = roll(y_ref[r, 0:48, :], (r + 1 - 16 * k + 128) % 128)
        west = jnp.where((lane == r) & (k > 0), turned, west)
    edge = jnp.where(lane < 16, west, roll(row_ref[...], (16 - 16 * k + 128) % 128))
    out[0, 200:224, 0:128] = edge[0:24]
    out[0, 200:224, 128:256] = edge[24:48]


def package(tab, y, col, row):
    return pl.pallas_call(
        package_kernel,
        grid_spec=pltpu.PrefetchScalarGridSpec(
            num_scalar_prefetch=1,
            grid=(TILE,),
            in_specs=[
                pl.BlockSpec((SIDE, 200, 128), lambda k, tab: (0, 0, 0)),
                pl.BlockSpec((LEV, 128), lambda k, tab: (0, 0)),
                pl.BlockSpec((LEV, 128), lambda k, tab: (0, 0)),
            ],
            out_specs=pl.BlockSpec((1, PHYS, CELLS), lambda k, tab: (tab[9, k], 0, 0)),
        ),
        out_shape=jax.ShapeDtypeStruct((8, PHYS, CELLS), jnp.float32),
        cost_estimate=pl.CostEstimate(flops=10**7, bytes_accessed=4 * 10**6, transcendentals=0),
        name="package",
    )(tab, y, col, row)


MESH = pl.DeviceIdType.MESH


def remote(src, dst, send, recv, where):
    return pltpu.make_async_remote_copy(src_ref=src, dst_ref=dst, send_sem=send, recv_sem=recv,
                                        device_id=where, device_id_type=MESH)


def each(first, last, fn):
    def body(d, carry):
        fn(d)
        return carry
    lax.fori_loop(first, last, body, 0)


def halo_kernel(first, *refs):
    if first:
        (tab, up_ref, phys, rows_ref, phys_out, got_s, got_n, pick, mid, turn,
         up_send, up_recv, dn_send, dn_recv, z_send, z_recv, y_send, y_recv, own) = refs
    else:
        (tab, up_ref, w_ref, e_ref, rows_ref, from_w, from_e, got_s, got_n, pick,
         up_send, up_recv, dn_send, dn_recv, we_send, we_recv) = refs
    lat, lon = lax.axis_index("lat"), lax.axis_index("lon")
    bands, count = lax.axis_size("lat"), lax.axis_size("lon")
    sides = (lax.rem(lat + 1, bands), lax.rem(lat + bands - 1, bands))
    row, place = lon // 4, lax.rem(lon, 4)
    got = (got_s, got_n)
    barrier = pltpu.get_barrier_semaphore()

    def greet(d):
        peer = lax.rem(lon + d, count)
        for side in sides:
            pl.semaphore_signal(barrier, inc=1, device_id=(side, peer), device_id_type=MESH)

    each(0, count, greet)
    each(1, count, lambda d: pl.semaphore_signal(
        barrier, inc=1, device_id=(lat, lax.rem(lon + d, count)), device_id_type=MESH))
    pl.semaphore_wait(barrier, 3 * count - 1)

    def up(n, d):
        peer = lax.rem(lon + d, count)
        return remote(up_ref.at[peer, 1 - n], got[n].at[lon], up_send.at[n, d], up_recv.at[n, d], (sides[n], peer))

    def up_from(n, d):
        peer = lax.rem(lon + count - d, count)
        return remote(up_ref.at[peer, 1 - n], got[n].at[peer], up_send.at[n, d], up_recv.at[n, d], (sides[1 - n], peer))

    def down(n, d):
        peer = lax.rem(lon + d, count)
        return remote(pick.at[n, peer], rows_ref.at[lon, n], dn_send.at[n, d], dn_recv.at[n, d], (lat, peer))

    def down_from(n, d):
        peer = lax.rem(lon + count - d, count)
        return remote(pick.at[n, peer], rows_ref.at[peer, n], dn_send.at[n, d], dn_recv.at[n, d], (lat, peer))

    def by_z(d):
        z = lax.rem(place + d, 4)
        return remote(phys.at[z], mid.at[place], z_send.at[d], z_recv.at[d], (lat, 4 * row + z))

    def from_z(d):
        z = lax.rem(place + 4 - d, 4)
        return remote(phys.at[z], mid.at[z], z_send.at[d], z_recv.at[d], (lat, 4 * row + z))

    def by_y(d):
        y = lax.rem(row + d, 4)
        return remote(turn.at[y], phys_out.at[row], y_send.at[d], y_recv.at[d], (lat, 4 * y + place))

    def from_y(d):
        y = lax.rem(row + 4 - d, 4)
        return remote(turn.at[y], phys_out.at[y], y_send.at[d], y_recv.at[d], (lat, 4 * y + place))

    def descend(n):
        each(0, count, lambda d: up_from(n, d).wait_recv())

        def choose(o):
            value = got[n][tab[2 * n, o]]
            pick[n, o] = jnp.where(tab[2 * n + 1, o] > 0, value, 0.0)

        each(0, count, choose)
        rows_ref[lon, n] = pick[n, lon]
        each(1, count, lambda d: down(n, d).start())

    if first:
        each(1, 4, lambda d: by_z(d).start())
        keep = pltpu.make_async_copy(phys.at[place], mid.at[place], own.at[0])
        keep.start()
    for n in range(2):
        each(0, count, lambda d: up(n, d).start())
    if first:
        each(1, 4, lambda d: from_z(d).wait_recv())
        keep.wait()

        def sort(q):
            turn[q // 2, lax.rem(q, 2)] = mid[tab[4, q] // 2, lax.rem(tab[4, q], 2)]

        each(0, 8, sort)
        each(1, 4, lambda d: by_y(d).start())
        phys_out[row] = turn[row]
    else:
        to_e = remote(e_ref, from_w, we_send.at[0], we_recv.at[0], (lat, lax.rem(lon + 1, count)))
        to_w = remote(w_ref, from_e, we_send.at[1], we_recv.at[1], (lat, lax.rem(lon + count - 1, count)))
        to_e.start()
        to_w.start()
    descend(0)
    descend(1)
    for n in range(2):
        each(1, count, lambda d: down_from(n, d).wait_recv())
    for n in range(2):
        each(0, count, lambda d: up(n, d).wait_send())
        each(1, count, lambda d: down(n, d).wait_send())
    if first:
        each(1, 4, lambda d: from_y(d).wait_recv())
        each(1, 4, lambda d: by_z(d).wait_send())
        each(1, 4, lambda d: by_y(d).wait_send())
    else:
        to_e.wait()
        to_w.wait()


def halo(first, tab, rows, *rest):
    anywhere = pl.BlockSpec(memory_space=pl.ANY)
    here = pl.BlockSpec(memory_space=VM)
    edge = jax.ShapeDtypeStruct((4, ROWS3, CELLS), jnp.float32)
    dma = pltpu.SemaphoreType.DMA
    sent = pltpu.VMEM((4, 2, PHYS, CELLS), jnp.float32)
    out = [jax.ShapeDtypeStruct((16, 2, HALF, 128), jnp.float32)]
    scratch = [VM((16, HALF, 128), jnp.float32), VM((16, HALF, 128), jnp.float32),
               VM((2, 16, HALF, 128), jnp.float32)]
    sems = [dma((2, 16)), dma((2, 16)), dma((2, 16)), dma((2, 16))]
    if first:
        in_specs, out_specs = [here], [here, here]
        out.append(jax.ShapeDtypeStruct((4, 2, PHYS, CELLS), jnp.float32))
        scratch += [sent, sent] + sems + [dma((4,)), dma((4,)), dma((4,)), dma((4,)), dma((1,))]
        rest = [rest[0].reshape(4, 2, PHYS, CELLS)]
    else:
        in_specs, out_specs = [anywhere] * 2, [here] + [anywhere] * 2
        out += [edge, edge]
        scratch += sems + [dma((2,)), dma((2,))]
    rows, *more = pl.pallas_call(
        functools.partial(halo_kernel, first),
        in_specs=[pl.BlockSpec(memory_space=pltpu.SMEM), here] + in_specs,
        out_specs=out_specs,
        out_shape=out,
        scratch_shapes=scratch,
        compiler_params=pltpu.CompilerParams(collective_id=1 if first else 2, has_side_effects=True),
        cost_estimate=pl.CostEstimate(flops=10**6, bytes_accessed=10**8, transcendentals=0),
        name="halo_phys" if first else "halo",
    )(tab, rows.reshape(16, 2, HALF, 128), *rest)
    return [rows.reshape(8, 2, 2, HALF, 128)] + more


def heat_kernel(tab, got, wet, light, out, fine):
    lane = lanes()
    group = lane // SIDE
    for r in range(SIDE):
        half = slice(128 * (r // 8), 128 * (r // 8) + 128)
        acc = jnp.zeros((LEV, 128), jnp.float32)
        for k in range(TILE):
            acc = jnp.where(group == k, roll(got[tab[6, k], :, half], (16 * k - 16 * (r % 8)) % 128), acc)
        acc = jnp.where(wet[r:r + 1, :] > 0.0, acc, 0.0)
        for a in range(3):
            fine[pl.ds(3 * r + a, LEV, stride=LEV), :] = acc
    spread = spread_matrix((128, 384), False)
    stacked = jnp.concatenate([spread] * 3, axis=0)

    def levels(i, carry):
        x = fine[pl.ds(pl.multiple_of(i * 8 * LEV, 8 * LEV), 8 * LEV), :]
        high = x.astype(jnp.bfloat16)
        rest = x - high.astype(jnp.float32)
        mid = rest.astype(jnp.bfloat16)
        low = (rest - mid.astype(jnp.float32)).astype(jnp.bfloat16)
        wide = jnp.dot(jnp.concatenate([high, mid, low], axis=1), stacked,
                       preferred_element_type=jnp.float32)
        for l in range(8):
            out[8 * i + l] = (light[...] * wide[l * LEV:l * LEV + LEV]).astype(jnp.bfloat16)
        return carry

    lax.fori_loop(0, LEV // 8, levels, 0)


def heat(tab, got, wet, light):
    return pl.pallas_call(
        heat_kernel,
        in_specs=[pl.BlockSpec(memory_space=pltpu.SMEM)] + [pl.BlockSpec(memory_space=VM)] * 3,
        out_specs=pl.BlockSpec(memory_space=VM),
        out_shape=jax.ShapeDtypeStruct((LEV, 48, 384), jnp.bfloat16),
        scratch_shapes=[VM((LEV * LEV, 128), jnp.float32)],
        cost_estimate=pl.CostEstimate(flops=10**9, bytes_accessed=3 * 10**6, transcendentals=0),
        name="heat",
    )(tab, got, wet, light)


def tables(band, lat, lon):
    wet = band >= 0
    owner = band // SLOTS % 16
    tile = jnp.arange(128) // TILE
    slot_code = (lat * 16 + lon) * SLOTS + jnp.arange(SLOTS)
    hit = band[None, :] == slot_code[:, None]
    full = jnp.any(hit, axis=1)
    block = jnp.sum(jnp.where(hit, jnp.arange(128)[None, :], 0), axis=1)
    west = jnp.sum(jnp.where(jnp.roll(hit, -1, axis=1), band[None, :], 0), axis=1)
    east = jnp.sum(jnp.where(jnp.roll(hit, 1, axis=1), band[None, :], 0), axis=1)
    src = jnp.where(full, block // TILE, 0)
    used = jnp.any((src[None, :] == jnp.arange(16)[:, None]) & full[None, :], axis=1)
    spare = jnp.argmin(used).astype(jnp.int32)
    pair_used = jnp.any(used.reshape(8, 2), axis=1)
    pair_spare = jnp.argmin(pair_used).astype(jnp.int32)
    w_slot = jnp.where(full & (west >= 0), west % SLOTS, 0)
    e_slot = jnp.where(full & (east >= 0), east % SLOTS, 0)
    mine = lax.dynamic_slice_in_dim(band, lon * TILE, TILE)
    t_wet = mine >= 0
    t_own = mine // SLOTS % 16
    t_used = jnp.any((t_own[None, :] == jnp.arange(16)[:, None]) & t_wet[None, :], axis=1)
    t_spare = jnp.argmin(t_used).astype(jnp.int32)
    ids = jnp.arange(128)
    before = (ids[None, :] < ids[:, None]) & wet[None, :]
    near = before & (tile[None, :] == tile[:, None]) & ((owner % 4)[None, :] == (owner % 4)[:, None])
    near = jnp.sum(near.astype(jnp.int32), axis=1)
    far = before & ((ids // 32)[None, :] == (ids // 32)[:, None]) & (owner[None, :] == owner[:, None])
    far = jnp.sum(far.astype(jnp.int32), axis=1)
    my_near = lax.dynamic_slice_in_dim(near, lon * TILE, TILE)
    z_at = (t_own % 4) * 2 + my_near
    z_used = jnp.any((z_at[None, :] == jnp.arange(8)[:, None]) & t_wet[None, :], axis=1)
    z_at = jnp.where(t_wet, z_at, jnp.argmin(z_used).astype(jnp.int32))
    got_at = jnp.sum(jnp.where(hit, (ids // 32 * 2 + far)[None, :], 0), axis=1)
    turn = wet & (ids // 32 == lon // 4) & (owner % 4 == lon % 4)
    turn = turn[None, :] & ((owner // 4 * 2 + far)[None, :] == jnp.arange(8)[:, None])
    turn_from = jnp.sum(jnp.where(turn, (tile % 4 * 2 + near)[None, :], 0), axis=1)
    rows = [src, full, w_slot, e_slot, jnp.where(full, src, spare), t_wet, jnp.where(t_wet, t_own, t_spare),
            src // 2, jnp.where(full, src // 2, pair_spare), z_at, got_at]
    return jnp.stack([r.astype(jnp.int32) for r in rows]), turn_from


def meeting(band, south, north, lon, turn_from):
    first = lon // 2 * 16

    def cut(row):
        return lax.dynamic_slice_in_dim(row, first, 16)

    mine = cut(band)
    hit = ((mine // SLOTS % 16)[None, :] == jnp.arange(16)[:, None]) & (mine >= 0)[None, :]
    rows = []
    for other in (cut(south), cut(north)):
        rows.append(jnp.sum(jnp.where(hit & (other >= 0)[None, :], (other // SLOTS % 16)[None, :], 0), axis=1))
        rows.append(jnp.any(hit & (other >= 0)[None, :], axis=1))
    rows.append(jnp.concatenate([turn_from, turn_from]))
    return jnp.stack([r.astype(jnp.int32) for r in rows])


def shift(x, axis, by, closed=True):
    n = lax.axis_size(axis)
    return lax.ppermute(x, axis, [(i, (i + by) % n) for i in range(n) if closed or 0 <= i + by < n])


def swap(x):
    return lax.all_to_all(x, "lon", split_axis=0, concat_axis=0, tiled=True)


def on_device(tracers, phys_fine, mix_coarse, surf_light, land_mask, owner_map):
    wet = land_mask.astype(jnp.float32)
    band = owner_map[0]
    codes = band.astype(jnp.float32)
    width = wet.shape[1]
    south_in = shift(jnp.concatenate([wet[-1], codes]), "lat", 1)
    north_in = shift(jnp.concatenate([wet[0], codes]), "lat", -1)
    wet_w = shift(wet[:, -1], "lon", 1)
    wet_e = shift(wet[:, 0], "lon", -1)
    lat, lon = lax.axis_index("lat"), lax.axis_index("lon")
    tab, turn_from = tables(band, lat, lon)
    wet_s = jnp.where(lat > 0, south_in[:width], 0.0)
    wet_n = jnp.where(lat < lax.axis_size("lat") - 1, north_in[:width], 0.0)
    meet = meeting(band, south_in[width:].astype(jnp.int32), north_in[width:].astype(jnp.int32), lon, turn_from)
    open_e = wet * jnp.concatenate([wet[:, 1:], wet_e[:, None]], axis=1)
    open_w = wet * jnp.concatenate([wet_w[:, None], wet[:, :-1]], axis=1)
    open_n = wet * jnp.concatenate([wet[1:], wet_n[None]], axis=0)
    open_s = wet * jnp.concatenate([wet_s[None], wet[:-1]], axis=0)
    light = jnp.dot(surf_light, spread_matrix((384, 128), True, jnp.float32),
                    precision=lax.Precision.HIGHEST).reshape(SIDE, 3, 128)
    light = (light[:, 0] + light[:, 1] + light[:, 2]) / 9.0
    blank = jnp.zeros_like(wet)
    flags = jnp.stack([open_w, open_e, open_s, open_n, light, wet, blank, blank], axis=1)
    y, col = coarse(jnp.swapaxes(phys_fine, 1, 2), jnp.swapaxes(mix_coarse, 1, 2), flags)
    tab, y, col = lax.optimization_barrier((tab, y, col))
    west_col = shift(col, "lon", 1)
    south_row = shift(y[SIDE - 1, 48:96], "lat", 1)
    rows_out, w_out, e_out = pack(tab, tracers)
    came_west = shift(e_out, "lon", 1)
    came_east = shift(w_out, "lon", -1)
    y, rows_out = lax.optimization_barrier((y, rows_out))
    packed = package(tab, y, west_col, south_row)
    rows, phys = halo(True, meet, rows_out, packed)
    phys = phys.reshape(8, PHYS, CELLS)
    current, rows_out, w_out, e_out = step(False, tab, tracers, phys, rows, came_west, came_east)
    rows, came_west, came_east = halo(False, meet, rows_out, w_out, e_out)
    current, light_part = step(True, tab, current, phys, rows, came_west, came_east)
    return current, heat(tab, swap(light_part), wet, surf_light)


def solution(mesh):
    in_specs = (
        P(("lat", "lon"), None, None),
        P("lat", "lon", None),
        P("lat", "lon", None),
        P("lat", "lon"),
        P("lat", "lon"),
        P("lat", None),
    )
    out_specs = (P(("lat", "lon"), None, None), P(None, "lat", "lon"))
    return jax.shard_map(
        on_device, mesh=mesh, in_specs=in_specs, out_specs=out_specs, check_vma=False
    )
```

```python
import functools

import jax
import jax.numpy as jnp
from jax import lax
from jax.experimental import pallas as pl
from jax.experimental.pallas import tpu as pltpu
from jax.sharding import PartitionSpec as P

NTR = 24
LEV = 48
SIDE = 16
CELLS = 256
SLOTS = 8
TILE = 8
PHYS = 224
DIFF = 0.08
VM = pltpu.VMEM
ROWS3 = 3 * LEV
HALF = ROWS3 // 2


def pos(v):
    return jnp.maximum(v, 0.0)


def lanes():
    return lax.broadcasted_iota(jnp.int32, (LEV, 128), 1)


def roll(x, shift):
    return pltpu.roll(x, shift, 1)


def pack_edges(c_ref, rows_ref, w_ref, e_ref, odd):
    lane = lanes()
    group = lane // SIDE
    col = lane % SIDE
    even = lane % 2 == 0
    low = lane < SIDE
    for m in range(3):
        blank = jnp.zeros((LEV, 128), jnp.float32)
        ends = [blank, blank]
        both = [blank, blank]
        for g in range(8):
            t = 3 * g + m
            a = c_ref[0, t * LEV:(t + 1) * LEV, 0:128]
            b = c_ref[0, t * LEV:(t + 1) * LEV, 128:256]
            end = jnp.where(low, a, b)
            ends[g % 2] = jnp.where((group == g) | (group == (g + 7) % 8), roll(end, 16 * g) if g else end, ends[g % 2])
            here = (col == 2 * g) | (col == (2 * g + 15) % 16)
            for h, v in enumerate((a, b)):
                both[h] = jnp.where(here, roll(v, 2 * g) if g else v, both[h])
        flat = group % 2 == 0
        put_rows(rows_ref, 0, m, jnp.where(flat, ends[0], ends[1]))
        put_rows(rows_ref, 1, m, jnp.where(flat, ends[1], ends[0]))
        at = slice(m * LEV, (m + 1) * LEV)
        mine = (lane % 2) == odd
        for h in range(2):
            hs = slice(h * 128, (h + 1) * 128)
            turned = roll(both[h], odd)
            w_ref[0, at, hs] = jnp.where(mine, turned, w_ref[0, at, hs])
            e_ref[0, at, hs] = jnp.where(mine, e_ref[0, at, hs], turned)


def put_rows(rows_ref, d, m, x):
    lo = m * LEV
    if lo < HALF:
        n = min(LEV, HALF - lo)
        rows_ref[0, 0, d, lo:lo + n, :] = x[:n]
        if n < LEV:
            rows_ref[0, 1, d, 0:LEV - n, :] = x[n:]
    else:
        rows_ref[0, 1, d, lo - HALF:lo - HALF + LEV, :] = x


def clear_first(odd, *refs):
    @pl.when(odd == 0)
    def _():
        for ref in refs:
            ref[...] = jnp.zeros_like(ref)


def pack_kernel(tab, c_ref, rows_ref, w_ref, e_ref):
    odd = pl.program_id(0) % 2
    clear_first(odd, w_ref, e_ref)
    pack_edges(c_ref, rows_ref, w_ref, e_ref, odd)


def pack(tab, tracers):
    return pl.pallas_call(
        pack_kernel,
        grid_spec=pltpu.PrefetchScalarGridSpec(
            num_scalar_prefetch=1,
            grid=(SLOTS,),
            in_specs=[pl.BlockSpec((1, NTR * LEV, CELLS), lambda j, tab: (j, 0, 0))],
            out_specs=[
                pl.BlockSpec((1, 2, 2, HALF, 128), lambda j, tab: (tab[j, 4], 0, 0, 0, 0)),
                pl.BlockSpec((1, ROWS3, CELLS), lambda j, tab: (j // 2, 0, 0)),
                pl.BlockSpec((1, ROWS3, CELLS), lambda j, tab: (j // 2, 0, 0)),
            ],
        ),
        out_shape=[
            jax.ShapeDtypeStruct((8, 2, 2, HALF, 128), jnp.float32),
            jax.ShapeDtypeStruct((4, ROWS3, CELLS), jnp.float32),
            jax.ShapeDtypeStruct((4, ROWS3, CELLS), jnp.float32),
        ],
        cost_estimate=pl.CostEstimate(flops=10**7, bytes_accessed=12 * 10**6, transcendentals=0),
        name="pack",
    )(tab, tracers)


def react(get, put, par, warm):
    (carbon_dis, alkalinity, oxygen, nitrate, ammonium, phosphate, silicate, iron_free,
     nano_carbon, diat_carbon, nano_chl, diat_chl, nano_iron, diat_iron, diat_silica,
     micro_zoo, meso_zoo, dissolved_org, small_part, big_part, small_iron, big_iron,
     big_silica, calcite) = [functools.partial(get, t) for t in range(NTR)]
    p_am = pos(ammonium())
    nitrogen = pos(nitrate()) + p_am
    limit_nitro = nitrogen / (0.5 + nitrogen)
    p_ph = pos(phosphate())
    p_fe = pos(iron_free())
    p_si = pos(silicate())
    nutr_nano = jnp.minimum(jnp.minimum(limit_nitro, p_ph / (0.3 + p_ph)), p_fe / (0.2 + p_fe))
    nutr_diat = jnp.minimum(nutr_nano, p_si / (1.0 + p_si))
    nc = nano_carbon()
    dc = diat_carbon()
    wp = warm * par
    prod_nano = 0.1 * wp / (par + 0.5) * nutr_nano * nc
    prod_diat = 0.12 * wp / (par + 1.0) * nutr_diat * dc
    share = (p_am + 0.01) / (nitrogen + 0.02)
    mi = micro_zoo()
    me = meso_zoo()
    graze_nano = 0.08 * warm * mi / (1.0 + pos(nc))
    graze_diat = 0.06 * warm * me / (1.0 + pos(dc))
    loss_nano = graze_nano + 0.02
    loss_diat = graze_diat + 0.02
    eaten_nano = graze_nano * nc
    eaten_diat = graze_diat * dc
    death_micro = 0.03 * mi * pos(mi)
    death_meso = 0.03 * me * pos(me)
    do = dissolved_org()
    sp = small_part()
    bp = big_part()
    remin_doc = 0.03 * warm * do
    remin_poc = 0.02 * warm * sp
    remin_goc = 0.01 * warm * bp
    am = ammonium()
    nitrify = 0.05 * am
    cal = calcite()
    melt_cal = 0.01 * cal
    uptake = prod_nano + prod_diat
    remin = remin_doc + remin_poc + remin_goc
    calcify = 0.02 * prod_nano
    shell = melt_cal - calcify
    put(0, carbon_dis() + remin - uptake + shell)
    su = share * uptake
    fresh = uptake - su
    put(1, alkalinity() + 2.0 * shell + 0.16 * (fresh - nitrify))
    put(2, oxygen() + 1.3 * (uptake - remin) - 0.32 * nitrify)
    put(3, nitrate() + 0.16 * (nitrify - fresh))
    put(4, am + 0.16 * (remin - su - nitrify))
    put(5, phosphate() + 0.01 * (remin - uptake))
    bsi = big_silica()
    melt_si = 0.02 * bsi
    put(6, silicate() + melt_si - 0.15 * prod_diat)
    sfe = small_iron()
    bfe = big_iron()
    melt_sfe = 0.02 * sfe
    melt_bfe = 0.01 * bfe
    put(7, iron_free() + melt_sfe + melt_bfe - 0.005 * uptake)
    put(8, nc + prod_nano - loss_nano * nc)
    put(9, dc + prod_diat - loss_diat * dc)
    x = nano_chl()
    put(10, x + 0.03 * prod_nano - loss_nano * x)
    x = diat_chl()
    put(11, x + 0.03 * prod_diat - loss_diat * x)
    x = nano_iron()
    lost = loss_nano * x
    put(12, x + 0.005 * prod_nano - lost)
    put(20, sfe + lost - melt_sfe)
    x = diat_iron()
    lost = loss_diat * x
    put(13, x + 0.005 * prod_diat - lost)
    put(21, bfe + lost - melt_bfe)
    x = diat_silica()
    lost = loss_diat * x
    put(14, x + 0.15 * prod_diat - lost)
    put(22, bsi + lost - melt_si)
    put(15, mi + 0.3 * eaten_nano - death_micro)
    put(16, me + 0.3 * eaten_diat - death_meso)
    put(17, do + 0.3 * eaten_nano + 0.02 * nc - remin_doc)
    put(18, sp + 0.4 * eaten_nano + death_micro - remin_poc)
    put(19, bp + 0.4 * eaten_diat + 0.02 * dc + death_meso - remin_goc)
    put(23, cal - shell)


def tri():
    i = lax.broadcasted_iota(jnp.int32, (LEV, LEV), 0)
    j = lax.broadcasted_iota(jnp.int32, (LEV, LEV), 1)
    return (j < i).astype(jnp.float32)


def depth(absorb):
    return jnp.dot(tri(), absorb, precision=lax.Precision.HIGHEST,
                   preferred_element_type=jnp.float32)


def slot_step(tab, c_ref, phys, rows, west, east, out, coef, par_ref, cross, along):
    j = pl.program_id(0)
    w_odd = tab[j, 0] % 2
    e_odd = tab[j, 1] % 2
    lane = lanes()
    col = lane % SIDE
    at_w = col == 0
    at_e = col == SIDE - 1
    low = lane < 16
    high = lane >= 112
    H = (slice(0, 128), slice(128, 256))
    edge = jnp.concatenate([phys[0, 200:224, 0:128], phys[0, 200:224, 128:256]], axis=0)
    sel_r = lax.broadcasted_iota(jnp.int32, (128, 256), 0)
    sel_c = lax.broadcasted_iota(jnp.int32, (128, 256), 1)
    sel = ((sel_c == SIDE * sel_r) & (sel_r < SIDE)).astype(jnp.float32)
    edge_lane = jnp.where(low, edge, 0.0)
    edge_w = jnp.dot(edge_lane, sel, precision=lax.Precision.HIGHEST,
                     preferred_element_type=jnp.float32)
    edge_s = roll(edge, 112)
    fn_up = roll(phys[0, 48:96, H[0]], 16)
    level = lax.broadcasted_iota(jnp.int32, (LEV, 128), 0)
    for h in range(2):
        fe = phys[0, 0:48, H[h]]
        fn = phys[0, 48:96, H[h]]
        fw = jnp.where(at_w, edge_w[:, H[h]], roll(fe, 1))
        if h == 0:
            fs = jnp.where(low, edge_s, fn_up)
        else:
            fs = jnp.where(low, fn_up, roll(fn, 16))
        ow = DIFF * phys[0, 192:193, H[h]]
        oe = DIFF * phys[0, 193:194, H[h]]
        os = DIFF * phys[0, 194:195, H[h]]
        on = DIFF * phys[0, 195:196, H[h]]
        coef[0, :, H[h]] = (1.0 - (ow + oe + os + on)) - pos(fe) + jnp.minimum(fw, 0.0) - pos(fn) + jnp.minimum(fs, 0.0)
        coef[1, :, H[h]] = oe - jnp.minimum(fe, 0.0)
        coef[2, :, H[h]] = ow + pos(fw)
        coef[3, :, H[h]] = on - jnp.minimum(fn, 0.0)
        coef[4, :, H[h]] = os + pos(fs)
        coef[5, :, H[h]] = jnp.where(level < LEV - 1, phys[0, 144:192, H[h]], 0.0)

    def mix(moved, k):
        flux = k * (pltpu.roll(moved, LEV - 1, 0) - moved)
        return moved + flux - pltpu.roll(flux, 1, 0)

    wide = lax.broadcasted_iota(jnp.int32, (HALF, 128), 1)
    flat = (wide // SIDE) % 2 == 0
    for p in range(2):
        hp = slice(p * HALF, (p + 1) * HALF)
        upper = rows[0, p, 1, :, :]
        under = roll(rows[0, p, 0, :, :], 32)
        cross[0, hp, :] = jnp.where(flat, upper, under)
        cross[1, hp, :] = jnp.where(flat, under, upper)
        for h in range(2):
            along[hp, H[h]] = jnp.where(wide % 2 == 0, roll(west[0, hp, H[h]], 128 - 15 - w_odd),
                                        roll(east[0, hp, H[h]], 15 - e_odd))

    def group(g, carry):
        for m in range(3):
            at = pl.ds(pl.multiple_of((3 * g + m) * LEV, LEV), LEV)
            hm = slice(m * LEV, (m + 1) * LEV)
            a = c_ref[0, at, H[0]]
            b = c_ref[0, at, H[1]]
            ends = roll(cross[lax.rem(g, 2), hm, :], 112 - 16 * g)
            an, bn = roll(a, 112), roll(b, 112)
            as_, bs = roll(a, 16), roll(b, 16)
            north = (jnp.where(high, bn, an), jnp.where(high, ends, bn))
            south = (jnp.where(low, ends, as_), jnp.where(low, as_, bs))
            for h, v in enumerate((a, b)):
                sides = roll(along[hm, H[h]], lax.rem(128 - 2 * g, 128))
                vw = jnp.where(at_w, sides, roll(v, 1))
                ve = jnp.where(at_e, sides, roll(v, 127))
                moved = (coef[0, :, H[h]] * v + coef[1, :, H[h]] * ve + coef[2, :, H[h]] * vw
                         + coef[3, :, H[h]] * north[h] + coef[4, :, H[h]] * south[h])
                out[0, at, H[h]] = mix(moved, coef[5, :, H[h]])
        return carry

    lax.fori_loop(0, 8, group, 0)
    absorb = 0.04 + 0.02 * (pos(out[0, 480:528, :]) + pos(out[0, 528:576, :]))
    above = depth(absorb)
    par_ref[...] = phys[0, 196:197, :] * jnp.exp(-(above + 0.5 * absorb))
    for h in range(2):
        wet = jnp.broadcast_to(phys[0, 197:198, H[h]], (8, 128))

        def chunk(i, carry):
            l0 = pl.multiple_of(i * 8, 8)

            def get(t):
                return out[0, pl.ds(pl.multiple_of(t * LEV + l0, 8), 8), H[h]]

            held = [get(t) for t in range(NTR)]

            def put(t, v):
                out[0, pl.ds(pl.multiple_of(t * LEV + l0, 8), 8), H[h]] = v * wet

            warm = jnp.exp(0.0639 * phys[0, pl.ds(pl.multiple_of(96 + l0, 8), 8), H[h]])
            par = par_ref[pl.ds(l0, 8), H[h]]
            react(lambda t: held[t], put, par, warm)
            return carry

        lax.fori_loop(0, LEV // 8, chunk, 0)


def first_kernel(tab, c_ref, phys, rows, west, east, out, rows_out, w_out, e_out, coef, par_ref, cross, along):
    j = pl.program_id(0)
    odd = j % 2

    @pl.when(tab[j, 2] == 1)
    def _():
        slot_step(tab, c_ref, phys, rows, west, east, out, coef, par_ref, cross, along)

    @pl.when(tab[j, 2] == 0)
    def _():
        out[...] = jnp.zeros_like(out)

    clear_first(odd, w_out, e_out)
    pack_edges(out, rows_out, w_out, e_out, odd)


def last_kernel(tab, c_ref, phys, rows, west, east, out, light_out, coef, par_ref, cross, along):
    j = pl.program_id(0)

    @pl.when(tab[j, 2] == 1)
    def _():
        slot_step(tab, c_ref, phys, rows, west, east, out, coef, par_ref, cross, along)
        absorb = 0.04 + 0.02 * (pos(out[0, 480:528, :]) + pos(out[0, 528:576, :]))
        above = depth(absorb)
        light_out[0] = jnp.exp(-above) - jnp.exp(-(above + absorb))

    @pl.when(tab[j, 2] == 0)
    def _():
        out[...] = jnp.zeros_like(out)
        light_out[...] = jnp.zeros_like(light_out)


def step(last, tab, current, phys, rows, came_west, came_east):
    edge_spec = pl.BlockSpec((1, ROWS3, CELLS), lambda j, tab: (j // 2, 0, 0))
    edge_shape = jax.ShapeDtypeStruct((4, ROWS3, CELLS), jnp.float32)
    if last:
        outs = [pl.BlockSpec((1, LEV, CELLS), lambda j, tab: (tab[j, 5], 0, 0))]
        shapes = [jax.ShapeDtypeStruct((16, LEV, CELLS), jnp.float32)]
    else:
        outs = [pl.BlockSpec((1, 2, 2, HALF, 128), lambda j, tab: (tab[j, 4], 0, 0, 0, 0)), edge_spec, edge_spec]
        shapes = [jax.ShapeDtypeStruct((8, 2, 2, HALF, 128), jnp.float32), edge_shape, edge_shape]
    return pl.pallas_call(
        last_kernel if last else first_kernel,
        grid_spec=pltpu.PrefetchScalarGridSpec(
            num_scalar_prefetch=1,
            grid=(SLOTS,),
            in_specs=[
                pl.BlockSpec((1, NTR * LEV, CELLS), lambda j, tab: (j, 0, 0)),
                pl.BlockSpec((1, PHYS, CELLS), lambda j, tab: (tab[j, 8], 0, 0)),
                pl.BlockSpec((1, 2, 2, HALF, 128), lambda j, tab: (tab[j, 3], 0, 0, 0, 0)),
                pl.BlockSpec((1, ROWS3, CELLS), lambda j, tab: (tab[j, 0] // 2, 0, 0)),
                pl.BlockSpec((1, ROWS3, CELLS), lambda j, tab: (tab[j, 1] // 2, 0, 0)),
            ],
            out_specs=[pl.BlockSpec((1, NTR * LEV, CELLS), lambda j, tab: (j, 0, 0))] + outs,
            scratch_shapes=[VM((6, LEV, CELLS), jnp.float32), VM((LEV, CELLS), jnp.float32),
                            VM((2, ROWS3, 128), jnp.float32), VM((ROWS3, CELLS), jnp.float32)],
        ),
        out_shape=[jax.ShapeDtypeStruct((SLOTS, NTR * LEV, CELLS), jnp.float32)] + shapes,
        cost_estimate=pl.CostEstimate(flops=10**8, bytes_accessed=25 * 10**6, transcendentals=10**6),
        name="last_step" if last else "first_step",
    )(tab, current, phys, rows, came_west, came_east)


def spread_matrix(shape, lhs_wide, dtype=jnp.bfloat16):
    i = lax.broadcasted_iota(jnp.int32, shape, 0)
    j = lax.broadcasted_iota(jnp.int32, shape, 1)
    return (i // 3 == j if lhs_wide else i == j // 3).astype(dtype)


def coarse_kernel(phys, mix, flags, y_ref, col_ref, every_ref, third_ref):
    step = pl.program_id(0)

    @pl.when(step == 0)
    def _():
        i = lax.broadcasted_iota(jnp.int32, (384, 128), 0)
        j = lax.broadcasted_iota(jnp.int32, (384, 128), 1)
        every_ref[...] = (i // 3 == j).astype(jnp.bfloat16)
        third_ref[...] = (i == 3 * j + 2).astype(jnp.bfloat16)
        col_ref[...] = jnp.zeros_like(col_ref)

    def dot(a, b):
        return jnp.dot(a, b, preferred_element_type=jnp.float32)

    u = jnp.concatenate([phys[f, 0:48, :] for f in range(6)], axis=0)
    vt = jnp.concatenate([phys[2, 48:96, :], phys[5, 48:96, :]] + [phys[f, 96:144, :] for f in range(6)], axis=0)
    east = dot(u, third_ref[...])
    rest = dot(vt, every_ref[...])

    def part(x, n):
        return x[48 * n:48 * n + 48]

    for c in range(2):
        e = (part(east, 3 * c) + part(east, 3 * c + 1) + part(east, 3 * c + 2)) / 3.0 * flags[c, 1:2, :]
        y_ref[c, 0:48, :] = e
        y_ref[c, 48:96, :] = part(rest, c) / 3.0 * flags[c, 3:4, :]
        y_ref[c, 96:144, :] = (part(rest, 3 * c + 2) + part(rest, 3 * c + 3) + part(rest, 3 * c + 4)) / 9.0
        y_ref[c, 144:192, :] = mix[c].astype(jnp.float32)
        y_ref[c, 192:200, :] = flags[c]
        r = 2 * step + c
        col_ref[...] = jnp.where(lanes() == r, roll(e, r + 1), col_ref[...])


def coarse(phys_t, mix_t, flags):
    return pl.pallas_call(
        coarse_kernel,
        grid=(SIDE // 2,),
        in_specs=[
            pl.BlockSpec((6, 144, 384), lambda r: (r, 0, 0)),
            pl.BlockSpec((2, LEV, 128), lambda r: (r, 0, 0)),
            pl.BlockSpec((2, 8, 128), lambda r: (r, 0, 0)),
        ],
        out_specs=[
            pl.BlockSpec((2, 200, 128), lambda r: (r, 0, 0)),
            pl.BlockSpec((LEV, 128), lambda r: (0, 0)),
        ],
        out_shape=[
            jax.ShapeDtypeStruct((SIDE, 200, 128), jnp.float32),
            jax.ShapeDtypeStruct((LEV, 128), jnp.float32),
        ],
        scratch_shapes=[VM((384, 128), jnp.bfloat16), VM((384, 128), jnp.bfloat16)],
        cost_estimate=pl.CostEstimate(flops=10**9, bytes_accessed=8 * 10**6, transcendentals=0),
        name="coarse",
    )(phys_t, mix_t, flags)


def package_kernel(tab, y_ref, col_ref, row_ref, out):
    k = pl.program_id(0)
    lane = lanes()
    group = lane // SIDE
    for f in range(5):
        n = 48 if f < 4 else 8
        at = slice(48 * f, 48 * f + n)
        for h in range(2):
            acc = jnp.zeros((n, 128), jnp.float32)
            for g in range(8):
                turned = roll(y_ref[8 * h + g, at, :], (16 * g - 16 * k + 128) % 128)
                acc = jnp.where(group[:n] == g, turned, acc)
            out[0, at, 128 * h:128 * h + 128] = acc
    west = col_ref[...]
    for r in range(SIDE):
        turned = roll(y_ref[r, 0:48, :], (r + 1 - 16 * k + 128) % 128)
        west = jnp.where((lane == r) & (k > 0), turned, west)
    edge = jnp.where(lane < 16, west, roll(row_ref[...], (16 - 16 * k + 128) % 128))
    out[0, 200:224, 0:128] = edge[0:24]
    out[0, 200:224, 128:256] = edge[24:48]


def package(tab, y, col, row):
    return pl.pallas_call(
        package_kernel,
        grid_spec=pltpu.PrefetchScalarGridSpec(
            num_scalar_prefetch=1,
            grid=(TILE,),
            in_specs=[
                pl.BlockSpec((SIDE, 200, 128), lambda k, tab: (0, 0, 0)),
                pl.BlockSpec((LEV, 128), lambda k, tab: (0, 0)),
                pl.BlockSpec((LEV, 128), lambda k, tab: (0, 0)),
            ],
            out_specs=pl.BlockSpec((1, PHYS, CELLS), lambda k, tab: (tab[k, 7], 0, 0)),
        ),
        out_shape=jax.ShapeDtypeStruct((8, PHYS, CELLS), jnp.float32),
        cost_estimate=pl.CostEstimate(flops=10**7, bytes_accessed=4 * 10**6, transcendentals=0),
        name="package",
    )(tab, y, col, row)


MESH = pl.DeviceIdType.MESH


def remote(src, dst, send, recv, where):
    return pltpu.make_async_remote_copy(src_ref=src, dst_ref=dst, send_sem=send, recv_sem=recv,
                                        device_id=where, device_id_type=MESH)


PARTS = 4
PART = PHYS // PARTS
ORDER = (0, 5, 10, 15, 4, 1, 8, 2, 12, 3, 6, 9, 7, 13, 11, 14)


def each(first, last, fn):
    def body(d, carry):
        fn(d)
        return carry
    lax.fori_loop(first, last, body, 0)


def halo_kernel(first, *refs):
    if first:
        (tab, up_ref, phys, rows_ref, phys_out, got_s, got_n, pick, turn, mid0, mid1, mid2, mid3,
         up_send, up_recv, dn_send, dn_recv, z_send, z_recv, y_send, y_recv, own) = refs
        mid = (mid0, mid1, mid2, mid3)
    else:
        (tab, up_ref, w_ref, e_ref, rows_ref, from_w, from_e, got_s, got_n, pick,
         up_send, up_recv, dn_send, dn_recv, we_send, we_recv) = refs
    lat, lon = lax.axis_index("lat"), lax.axis_index("lon")
    bands, count = lax.axis_size("lat"), lax.axis_size("lon")
    sides = (lax.rem(lat + 1, bands), lax.rem(lat + bands - 1, bands))
    row, place = lon // 4, lax.rem(lon, 4)
    got = (got_s, got_n)
    barrier = pltpu.get_barrier_semaphore()

    def ahead(d):
        return lax.rem(row + d // 4, 4) * 4 + lax.rem(place + d % 4, 4)

    def behind(d):
        return lax.rem(row + 4 - d // 4, 4) * 4 + lax.rem(place + 4 - d % 4, 4)

    def greet(d):
        peer = lax.rem(lon + d, count)
        for side in sides:
            pl.semaphore_signal(barrier, inc=1, device_id=(side, peer), device_id_type=MESH)

    each(0, count, greet)
    each(1, count, lambda d: pl.semaphore_signal(
        barrier, inc=1, device_id=(lat, lax.rem(lon + d, count)), device_id_type=MESH))
    pl.semaphore_wait(barrier, 3 * count - 1)

    def up(n, d):
        peer = ahead(d)
        return remote(up_ref.at[peer, 1 - n], got[n].at[lon], up_send.at[n, d], up_recv.at[n, d], (sides[n], peer))

    def up_from(n, d):
        peer = behind(d)
        return remote(up_ref.at[peer, 1 - n], got[n].at[peer], up_send.at[n, d], up_recv.at[n, d], (sides[1 - n], peer))

    def down(n, d):
        peer = ahead(d)
        return remote(pick.at[n, peer], rows_ref.at[lon, n], dn_send.at[n, d], dn_recv.at[n, d], (lat, peer))

    def down_from(n, d):
        peer = behind(d)
        return remote(pick.at[n, peer], rows_ref.at[peer, n], dn_send.at[n, d], dn_recv.at[n, d], (lat, peer))

    def piece(p):
        return pl.ds(p * PART, PART)

    def by_z(p, d):
        z = lax.rem(place + d, 4)
        return remote(phys.at[z, :, piece(p)], mid[p].at[place], z_send.at[p, d], z_recv.at[p, d], (lat, 4 * row + z))

    def from_z(p, d):
        z = lax.rem(place + 4 - d, 4)
        return remote(phys.at[z, :, piece(p)], mid[p].at[z], z_send.at[p, d], z_recv.at[p, d], (lat, 4 * row + z))

    def by_y(p, d):
        y = lax.rem(row + d, 4)
        return remote(turn.at[y, :, piece(p)], phys_out.at[row, :, piece(p)], y_send.at[p, d], y_recv.at[p, d], (lat, 4 * y + place))

    def from_y(p, d):
        y = lax.rem(row + 4 - d, 4)
        return remote(turn.at[y, :, piece(p)], phys_out.at[y, :, piece(p)], y_send.at[p, d], y_recv.at[p, d], (lat, 4 * y + place))

    def lift(n):
        for d in ORDER:
            up(n, d).start()

    def descend(n):
        for d in ORDER:
            up_from(n, d).wait_recv()

        def choose(o):
            value = got[n][tab[o, 2 * n]]
            pick[n, o] = jnp.where(tab[o, 2 * n + 1] > 0, value, 0.0)

        each(0, count, choose)
        rows_ref[lon, n] = pick[n, lon]
        for d in ORDER[1:]:
            down(n, d).start()

    def stay(p):
        return pltpu.make_async_copy(phys.at[place, :, piece(p)], mid[p].at[place], own.at[p])

    def send_z(p):
        for d in (2, 1, 3):
            by_z(p, d).start()
        stay(p).start()

    def send_y(p):
        for d in (1, 2, 3):
            from_z(p, d).wait_recv()
        stay(p).wait()

        def sort(q):
            turn[q // 2, lax.rem(q, 2), piece(p)] = mid[p][tab[q, 4] // 2, lax.rem(tab[q, 4], 2)]

        each(0, 8, sort)
        for d in (2, 1, 3):
            by_y(p, d).start()
        phys_out[row, :, piece(p)] = turn[row, :, piece(p)]

    if first:
        send_z(0)
        lift(0)
        send_z(1)
        lift(1)
        send_z(2)
        send_z(3)
        send_y(0)
        descend(0)
        send_y(1)
        descend(1)
        send_y(2)
        send_y(3)
    else:
        to_e = remote(e_ref, from_w, we_send.at[0], we_recv.at[0], (lat, lax.rem(lon + 1, count)))
        to_w = remote(w_ref, from_e, we_send.at[1], we_recv.at[1], (lat, lax.rem(lon + count - 1, count)))
        lift(0)
        lift(1)
        descend(0)
        to_e.start()
        to_w.start()
        descend(1)
    for n in range(2):
        for d in ORDER[1:]:
            down_from(n, d).wait_recv()
    for n in range(2):
        for d in ORDER:
            up(n, d).wait_send()
        for d in ORDER[1:]:
            down(n, d).wait_send()
    if first:
        for p in range(PARTS):
            for d in (1, 2, 3):
                from_y(p, d).wait_recv()
                by_z(p, d).wait_send()
                by_y(p, d).wait_send()
    else:
        to_e.wait()
        to_w.wait()


def halo(first, tab, rows, *rest):
    anywhere = pl.BlockSpec(memory_space=pl.ANY)
    here = pl.BlockSpec(memory_space=VM)
    edge = jax.ShapeDtypeStruct((4, ROWS3, CELLS), jnp.float32)
    dma = pltpu.SemaphoreType.DMA
    sent = pltpu.VMEM((4, 2, PHYS, CELLS), jnp.float32)
    out = [jax.ShapeDtypeStruct((16, 2, HALF, 128), jnp.float32)]
    scratch = [VM((16, HALF, 128), jnp.float32), VM((16, HALF, 128), jnp.float32),
               VM((2, 16, HALF, 128), jnp.float32)]
    sems = [dma((2, 16)), dma((2, 16)), dma((2, 16)), dma((2, 16))]
    if first:
        in_specs, out_specs = [here], [here, here]
        out.append(jax.ShapeDtypeStruct((4, 2, PHYS, CELLS), jnp.float32))
        scratch += [sent] + [VM((4, 2, PART, CELLS), jnp.float32)] * PARTS
        scratch += sems + [dma((PARTS, 4))] * 4 + [dma((PARTS,))]
        rest = [rest[0].reshape(4, 2, PHYS, CELLS)]
    else:
        in_specs, out_specs = [anywhere] * 2, [here] + [anywhere] * 2
        out += [edge, edge]
        scratch += sems + [dma((2,)), dma((2,))]
    rows, *more = pl.pallas_call(
        functools.partial(halo_kernel, first),
        in_specs=[pl.BlockSpec(memory_space=pltpu.SMEM), here] + in_specs,
        out_specs=out_specs,
        out_shape=out,
        scratch_shapes=scratch,
        compiler_params=pltpu.CompilerParams(collective_id=1 if first else 2, has_side_effects=True),
        cost_estimate=pl.CostEstimate(flops=10**6, bytes_accessed=10**8, transcendentals=0),
        name="halo_phys" if first else "halo",
    )(tab, rows.reshape(16, 2, HALF, 128), *rest)
    return [rows.reshape(8, 2, 2, HALF, 128)] + more


def heat_kernel(tab, got, wet, light, out, fine):
    lane = lanes()
    group = lane // SIDE
    for r in range(SIDE):
        half = slice(128 * (r // 8), 128 * (r // 8) + 128)
        acc = jnp.zeros((LEV, 128), jnp.float32)
        for k in range(TILE):
            acc = jnp.where(group == k, roll(got[tab[k, 6], :, half], (16 * k - 16 * (r % 8)) % 128), acc)
        acc = jnp.where(wet[r:r + 1, :] > 0.0, acc, 0.0)
        for a in range(3):
            fine[pl.ds(3 * r + a, LEV, stride=LEV), :] = acc
    spread = spread_matrix((128, 384), False)
    stacked = jnp.concatenate([spread] * 3, axis=0)

    def levels(i, carry):
        x = fine[pl.ds(pl.multiple_of(i * 8 * LEV, 8 * LEV), 8 * LEV), :]
        high = x.astype(jnp.bfloat16)
        rest = x - high.astype(jnp.float32)
        mid = rest.astype(jnp.bfloat16)
        low = (rest - mid.astype(jnp.float32)).astype(jnp.bfloat16)
        wide = jnp.dot(jnp.concatenate([high, mid, low], axis=1), stacked,
                       preferred_element_type=jnp.float32)
        for l in range(8):
            out[8 * i + l] = (light[...] * wide[l * LEV:l * LEV + LEV]).astype(jnp.bfloat16)
        return carry

    lax.fori_loop(0, LEV // 8, levels, 0)


def heat(tab, got, wet, light):
    return pl.pallas_call(
        heat_kernel,
        in_specs=[pl.BlockSpec(memory_space=pltpu.SMEM)] + [pl.BlockSpec(memory_space=VM)] * 3,
        out_specs=pl.BlockSpec(memory_space=VM),
        out_shape=jax.ShapeDtypeStruct((LEV, 48, 384), jnp.bfloat16),
        scratch_shapes=[VM((LEV * LEV, 128), jnp.float32)],
        cost_estimate=pl.CostEstimate(flops=10**9, bytes_accessed=3 * 10**6, transcendentals=0),
        name="heat",
    )(tab, got, wet, light)


def prep_kernel(base, south, north, west, east, light, flags, tab, meet, sums):
    lat, lon = lax.axis_index("lat"), lax.axis_index("lon")
    wet = base[0:16, :]
    lane = lax.broadcasted_iota(jnp.int32, (SIDE, 128), 1)
    line = lax.broadcasted_iota(jnp.int32, (SIDE, 128), 0)
    wet_e = jnp.where(lane == 127, roll(east[0:16, :], 127), roll(wet, 127))
    wet_w = jnp.where(lane == 0, roll(west[0:16, :], 1), roll(wet, 1))
    inner_n = (lat < lax.axis_size("lat") - 1).astype(jnp.float32)
    inner_s = (lat > 0).astype(jnp.float32)
    wet_n = jnp.where(line == 15, inner_n * north[0:1, :], pltpu.roll(wet, 15, 0))
    wet_s = jnp.where(line == 0, inner_s * south[15:16, :], pltpu.roll(wet, 1, 0))
    sums[...] = jnp.dot(light[...], spread_matrix((384, 128), True, jnp.float32),
                        precision=lax.Precision.HIGHEST, preferred_element_type=jnp.float32)
    mean = sums[pl.ds(0, 16, stride=3), :] + sums[pl.ds(1, 16, stride=3), :] + sums[pl.ds(2, 16, stride=3), :]
    values = (wet * wet_w, wet * wet_e, wet * wet_s, wet * wet_n, mean / 9.0, wet,
              jnp.zeros_like(wet), jnp.zeros_like(wet))
    for i, v in enumerate(values):
        flags[pl.ds(i, 16, stride=8), :] = v

    def ints(ref):
        return ref[16:17, :].astype(jnp.int32)

    def owner_of(code):
        return lax.shift_right_arithmetic(code, 3) & 15

    def f32(x):
        return x.astype(jnp.float32)

    def wide(x, n):
        return jnp.broadcast_to(x, (n, 128))

    band = ints(base)
    big_i = lax.broadcasted_iota(jnp.int32, (128, 128), 0)
    big_j = lax.broadcasted_iota(jnp.int32, (128, 128), 1)
    down = jnp.sum(jnp.where(big_i == big_j, f32(wide(band, 128)), 0.0), axis=1, keepdims=True).astype(jnp.int32)
    down = jnp.broadcast_to(down, (128, 128))
    own_i, own_j = owner_of(down), owner_of(wide(band, 128))
    before = (big_i < big_j) & (down >= 0)
    near = jnp.sum(f32(before & (big_i // 8 == big_j // 8) & ((own_i & 3) == (own_j & 3))), axis=0, keepdims=True)
    far = jnp.sum(f32(before & (big_i // 32 == big_j // 32) & (own_i == own_j)), axis=0, keepdims=True)
    ids = lax.broadcasted_iota(jnp.int32, (1, 128), 1)
    own = owner_of(band)
    wet_b = band >= 0

    def total(mask, value):
        n = mask.shape[0]
        return jnp.sum(jnp.where(mask, wide(f32(value), n), 0.0), axis=1, keepdims=True)

    slot = lax.broadcasted_iota(jnp.int32, (8, 128), 0)
    ids8 = wide(ids, 8)
    band8 = wide(band, 8)
    hit = band8 == (lat * 16 + lon) * SLOTS + slot
    full = total(hit, jnp.ones_like(band))
    pair = total(hit, ids // 16)
    got_at = total(hit, ids // 32 * 2) + total(hit, far)
    west_code = total(hit, roll(band, 1))
    east_code = total(hit, roll(band, 127))

    def slot_of(code):
        code = code.astype(jnp.int32)
        return f32(jnp.where(code >= 0, code & 7, 0))

    w_slot, e_slot = slot_of(west_code), slot_of(east_code)
    some = jnp.broadcast_to(ids8 // 16 == slot, (8, 128))
    band_hit = wide(f32(jnp.max(f32(hit), axis=0, keepdims=True)), 8) > 0.0
    first_of = lax.broadcasted_iota(jnp.int32, (8, 1), 0).astype(jnp.float32)
    pair_used = total(some & band_hit, jnp.ones_like(band))
    pair_spare = jnp.min(jnp.where(pair_used > 0.0, 99.0, first_of), axis=0, keepdims=True)
    my_tile = ids // TILE == lon
    tile_mask = (ids8 // TILE == lon) & (ids8 - TILE * lon == slot)
    t_wet = total(tile_mask & (band8 >= 0), jnp.ones_like(band))
    t_own = total(tile_mask & (band8 >= 0), own)
    z_key = (own & 3) * 2 + near.astype(jnp.int32)
    z_at = total(tile_mask & (band8 >= 0), z_key)
    z_used = total(wide(my_tile & wet_b, 8) & (wide(z_key, 8) == slot), jnp.ones_like(band))
    z_spare = jnp.min(jnp.where(z_used > 0.0, 99.0, first_of), axis=0, keepdims=True)
    z_at = jnp.where(t_wet > 0.0, z_at, jnp.minimum(z_spare, 7.0))
    t_first = lax.broadcasted_iota(jnp.int32, (16, 1), 0).astype(jnp.float32)
    row16 = lax.broadcasted_iota(jnp.int32, (16, 128), 0)
    in_tile = wide(my_tile & wet_b, 16)
    to_me = jnp.max(f32(hit), axis=0, keepdims=True)
    src_used = total((wide(ids // TILE, 16) == row16) & (wide(to_me, 16) > 0.0), jnp.ones_like(band))
    src_spare = jnp.min(jnp.where(src_used > 0.0, 99.0, t_first), axis=0, keepdims=True)
    src = total(hit, ids // TILE)
    fields = (w_slot, e_slot, full, pair, jnp.where(full > 0.0, pair, jnp.minimum(pair_spare, 7.0)),
              jnp.where(full > 0.0, src, src_spare), t_own, z_at, got_at)
    acc = jnp.zeros((8, 128), jnp.float32)
    for i, v in enumerate(fields):
        acc = jnp.where(ids8 == i, v, acc)
    tab[...] = acc.astype(jnp.int32)
    ids16 = wide(ids, 16)
    here = (ids16 // 16 == lon // 2) & wide(wet_b, 16) & (wide(own, 16) == row16)
    acc = jnp.zeros((16, 128), jnp.float32)
    for i, other in enumerate((ints(south), ints(north))):
        both = here & (wide(other, 16) >= 0)
        acc = jnp.where(ids16 == 2 * i, total(both, owner_of(other)), acc)
        acc = jnp.where(ids16 == 2 * i + 1, total(both, jnp.ones_like(band)), acc)
    mine = wet_b & (ids // 32 == lon // 4) & ((own & 3) == lax.rem(lon, 4))
    y_key = lax.shift_right_arithmetic(own, 2) * 2 + far.astype(jnp.int32)
    turn = wide(mine, 16) & (wide(y_key, 16) == row16)
    acc = jnp.where(ids16 == 4, total(turn, (ids // 8 & 3) * 2 + near.astype(jnp.int32)), acc)
    meet[...] = acc.astype(jnp.int32)


def prep(base, south, north, west, east, light):
    flags, tab, meet = pl.pallas_call(
        prep_kernel,
        in_specs=[pl.BlockSpec(memory_space=VM)] * 6,
        out_specs=[pl.BlockSpec(memory_space=VM)] * 3,
        out_shape=[jax.ShapeDtypeStruct((128, 128), jnp.float32),
                   jax.ShapeDtypeStruct((8, 128), jnp.int32),
                   jax.ShapeDtypeStruct((16, 128), jnp.int32)],
        scratch_shapes=[VM((48, 128), jnp.float32)],
        cost_estimate=pl.CostEstimate(flops=10**7, bytes_accessed=10**5, transcendentals=0),
        name="prep",
    )(base, south, north, west, east, light)
    return flags.reshape(SIDE, 8, 128), tab, meet


def shift(x, axis, by):
    n = lax.axis_size(axis)
    return lax.ppermute(x, axis, [(i, (i + by) % n) for i in range(n)])


def swap(x):
    return lax.all_to_all(x, "lon", split_axis=0, concat_axis=0, tiled=True)


def on_device(tracers, phys_fine, mix_coarse, surf_light, land_mask, owner_map):
    wet = land_mask.astype(jnp.float32)
    base = jnp.concatenate([wet, owner_map.astype(jnp.float32)], axis=0)
    flags, tab, meet = prep(base, shift(base, "lat", 1), shift(base, "lat", -1),
                            shift(base, "lon", 1), shift(base, "lon", -1), surf_light)
    y, col = coarse(jnp.swapaxes(phys_fine, 1, 2), jnp.swapaxes(mix_coarse, 1, 2), flags)
    tab, y, col = lax.optimization_barrier((tab, y, col))
    west_col = shift(col, "lon", 1)
    south_row = shift(y[SIDE - 1, 48:96], "lat", 1)
    rows_out, w_out, e_out = pack(tab, tracers)
    came_west = shift(e_out, "lon", 1)
    came_east = shift(w_out, "lon", -1)
    y, rows_out = lax.optimization_barrier((y, rows_out))
    packed = package(tab, y, west_col, south_row)
    rows, phys = halo(True, meet, rows_out, packed)
    phys = phys.reshape(8, PHYS, CELLS)
    current, rows_out, w_out, e_out = step(False, tab, tracers, phys, rows, came_west, came_east)
    rows, came_west, came_east = halo(False, meet, rows_out, w_out, e_out)
    current, light_part = step(True, tab, current, phys, rows, came_west, came_east)
    return current, heat(tab, swap(light_part), wet, surf_light)


def solution(mesh):
    in_specs = (
        P(("lat", "lon"), None, None),
        P("lat", "lon", None),
        P("lat", "lon", None),
        P("lat", "lon"),
        P("lat", "lon"),
        P("lat", None),
    )
    out_specs = (P(("lat", "lon"), None, None), P(None, "lat", "lon"))
    return jax.shard_map(
        on_device, mesh=mesh, in_specs=in_specs, out_specs=out_specs, check_vma=False
    )
```

```python
import functools

import jax
import jax.numpy as jnp
from jax import lax
from jax.experimental import pallas as pl
from jax.experimental.pallas import tpu as pltpu
from jax.sharding import PartitionSpec as P

NTR = 24
LEV = 48
SIDE = 16
CELLS = 256
SLOTS = 8
TILE = 8
PHYS = 224
DIFF = 0.08
VM = pltpu.VMEM
ROWS3 = 3 * LEV
HALF = ROWS3 // 2


def pos(v):
    return jnp.maximum(v, 0.0)


def lanes():
    return lax.broadcasted_iota(jnp.int32, (LEV, 128), 1)


def roll(x, shift):
    return pltpu.roll(x, shift, 1)


def pack_edges(c_ref, rows_ref, w_ref, e_ref, odd):
    lane = lanes()
    group = lane // SIDE
    col = lane % SIDE
    low = lane < SIDE
    for m in range(3):
        blank = jnp.zeros((LEV, 128), jnp.float32)
        ends = [blank, blank]
        both = [blank, blank]
        for g in range(8):
            t = 3 * g + m
            a = c_ref[0, t * LEV:(t + 1) * LEV, 0:128]
            b = c_ref[0, t * LEV:(t + 1) * LEV, 128:256]
            end = jnp.where(low, a, b)
            ends[g % 2] = jnp.where((group == g) | (group == (g + 7) % 8), roll(end, 16 * g) if g else end, ends[g % 2])
            here = (col == 2 * g) | (col == (2 * g + 15) % 16)
            for h, v in enumerate((a, b)):
                both[h] = jnp.where(here, roll(v, 2 * g) if g else v, both[h])
        flat = group % 2 == 0
        put_rows(rows_ref, 0, m, jnp.where(flat, ends[0], ends[1]))
        put_rows(rows_ref, 1, m, jnp.where(flat, ends[1], ends[0]))
        at = slice(m * LEV, (m + 1) * LEV)
        mine = (lane % 2) == odd
        for h in range(2):
            hs = slice(h * 128, (h + 1) * 128)
            turned = roll(both[h], odd)
            w_ref[0, at, hs] = jnp.where(mine, turned, w_ref[0, at, hs])
            e_ref[0, at, hs] = jnp.where(mine, e_ref[0, at, hs], turned)


def put_rows(rows_ref, d, m, x):
    lo = m * LEV
    if lo < HALF:
        n = min(LEV, HALF - lo)
        rows_ref[0, 0, d, lo:lo + n, :] = x[:n]
        if n < LEV:
            rows_ref[0, 1, d, 0:LEV - n, :] = x[n:]
    else:
        rows_ref[0, 1, d, lo - HALF:lo - HALF + LEV, :] = x


def clear_first(odd, *refs):
    @pl.when(odd == 0)
    def _():
        for ref in refs:
            ref[...] = jnp.zeros_like(ref)


def pack_kernel(tab, c_ref, rows_ref, w_ref, e_ref):
    p = pl.program_id(0)
    lane = lanes()
    group = lane // SIDE
    col = lane % SIDE
    even = lane % 2 == 0
    low = lane < SIDE
    flat = group % 2 == 0
    for m in range(3):
        at = slice(m * LEV, (m + 1) * LEV)
        blank = jnp.zeros((LEV, 128), jnp.float32)
        both = [[blank, blank], [blank, blank]]
        for i in range(2):
            ends = [blank, blank]
            for g in range(8):
                t = 3 * g + m
                a = c_ref[i, t * LEV:(t + 1) * LEV, 0:128]
                b = c_ref[i, t * LEV:(t + 1) * LEV, 128:256]
                end = jnp.where(low, a, b)
                ends[g % 2] = jnp.where((group == g) | (group == (g + 7) % 8), roll(end, 16 * g) if g else end, ends[g % 2])
                here = (col == 2 * g) | (col == (2 * g + 15) % 16)
                for h, v in enumerate((a, b)):
                    both[i][h] = jnp.where(here, roll(v, 2 * g) if g else v, both[i][h])
            view = rows_ref.at[pl.ds(tab[2 * p + i, 4], 1)]
            put_rows(view, 0, m, jnp.where(flat, ends[0], ends[1]))
            put_rows(view, 1, m, jnp.where(flat, ends[1], ends[0]))
        for h in range(2):
            hs = slice(h * 128, (h + 1) * 128)
            other = roll(both[1][h], 1)
            w_ref[0, at, hs] = jnp.where(even, both[0][h], other)
            e_ref[0, at, hs] = jnp.where(even, other, both[0][h])


def pack(tab, tracers):
    return pl.pallas_call(
        pack_kernel,
        grid_spec=pltpu.PrefetchScalarGridSpec(
            num_scalar_prefetch=1,
            grid=(SLOTS // 2,),
            in_specs=[pl.BlockSpec((2, NTR * LEV, CELLS), lambda j, tab: (j, 0, 0))],
            out_specs=[
                pl.BlockSpec((8, 2, 2, HALF, 128), lambda j, tab: (0, 0, 0, 0, 0)),
                pl.BlockSpec((1, ROWS3, CELLS), lambda j, tab: (j, 0, 0)),
                pl.BlockSpec((1, ROWS3, CELLS), lambda j, tab: (j, 0, 0)),
            ],
        ),
        out_shape=[
            jax.ShapeDtypeStruct((8, 2, 2, HALF, 128), jnp.float32),
            jax.ShapeDtypeStruct((4, ROWS3, CELLS), jnp.float32),
            jax.ShapeDtypeStruct((4, ROWS3, CELLS), jnp.float32),
        ],
        cost_estimate=pl.CostEstimate(flops=10**7, bytes_accessed=12 * 10**6, transcendentals=0),
        name="pack",
    )(tab, tracers)


def react(get, put, par, warm):
    (carbon_dis, alkalinity, oxygen, nitrate, ammonium, phosphate, silicate, iron_free,
     nano_carbon, diat_carbon, nano_chl, diat_chl, nano_iron, diat_iron, diat_silica,
     micro_zoo, meso_zoo, dissolved_org, small_part, big_part, small_iron, big_iron,
     big_silica, calcite) = [functools.partial(get, t) for t in range(NTR)]
    p_am = pos(ammonium())
    nitrogen = pos(nitrate()) + p_am
    limit_nitro = nitrogen / (0.5 + nitrogen)
    p_ph = pos(phosphate())
    p_fe = pos(iron_free())
    p_si = pos(silicate())
    nutr_nano = jnp.minimum(jnp.minimum(limit_nitro, p_ph / (0.3 + p_ph)), p_fe / (0.2 + p_fe))
    nutr_diat = jnp.minimum(nutr_nano, p_si / (1.0 + p_si))
    nc = nano_carbon()
    dc = diat_carbon()
    wp = warm * par
    prod_nano = 0.1 * wp / (par + 0.5) * nutr_nano * nc
    prod_diat = 0.12 * wp / (par + 1.0) * nutr_diat * dc
    share = (p_am + 0.01) / (nitrogen + 0.02)
    mi = micro_zoo()
    me = meso_zoo()
    graze_nano = 0.08 * warm * mi / (1.0 + pos(nc))
    graze_diat = 0.06 * warm * me / (1.0 + pos(dc))
    loss_nano = graze_nano + 0.02
    loss_diat = graze_diat + 0.02
    eaten_nano = graze_nano * nc
    eaten_diat = graze_diat * dc
    death_micro = 0.03 * mi * pos(mi)
    death_meso = 0.03 * me * pos(me)
    do = dissolved_org()
    sp = small_part()
    bp = big_part()
    remin_doc = 0.03 * warm * do
    remin_poc = 0.02 * warm * sp
    remin_goc = 0.01 * warm * bp
    am = ammonium()
    nitrify = 0.05 * am
    cal = calcite()
    melt_cal = 0.01 * cal
    uptake = prod_nano + prod_diat
    remin = remin_doc + remin_poc + remin_goc
    calcify = 0.02 * prod_nano
    shell = melt_cal - calcify
    put(0, carbon_dis() + remin - uptake + shell)
    su = share * uptake
    fresh = uptake - su
    put(1, alkalinity() + 2.0 * shell + 0.16 * (fresh - nitrify))
    put(2, oxygen() + 1.3 * (uptake - remin) - 0.32 * nitrify)
    put(3, nitrate() + 0.16 * (nitrify - fresh))
    put(4, am + 0.16 * (remin - su - nitrify))
    put(5, phosphate() + 0.01 * (remin - uptake))
    bsi = big_silica()
    melt_si = 0.02 * bsi
    put(6, silicate() + melt_si - 0.15 * prod_diat)
    sfe = small_iron()
    bfe = big_iron()
    melt_sfe = 0.02 * sfe
    melt_bfe = 0.01 * bfe
    put(7, iron_free() + melt_sfe + melt_bfe - 0.005 * uptake)
    put(8, nc + prod_nano - loss_nano * nc)
    put(9, dc + prod_diat - loss_diat * dc)
    x = nano_chl()
    put(10, x + 0.03 * prod_nano - loss_nano * x)
    x = diat_chl()
    put(11, x + 0.03 * prod_diat - loss_diat * x)
    x = nano_iron()
    lost = loss_nano * x
    put(12, x + 0.005 * prod_nano - lost)
    put(20, sfe + lost - melt_sfe)
    x = diat_iron()
    lost = loss_diat * x
    put(13, x + 0.005 * prod_diat - lost)
    put(21, bfe + lost - melt_bfe)
    x = diat_silica()
    lost = loss_diat * x
    put(14, x + 0.15 * prod_diat - lost)
    put(22, bsi + lost - melt_si)
    put(15, mi + 0.3 * eaten_nano - death_micro)
    put(16, me + 0.3 * eaten_diat - death_meso)
    put(17, do + 0.3 * eaten_nano + 0.02 * nc - remin_doc)
    put(18, sp + 0.4 * eaten_nano + death_micro - remin_poc)
    put(19, bp + 0.4 * eaten_diat + 0.02 * dc + death_meso - remin_goc)
    put(23, cal - shell)


def tri():
    i = lax.broadcasted_iota(jnp.int32, (LEV, LEV), 0)
    j = lax.broadcasted_iota(jnp.int32, (LEV, LEV), 1)
    return (j < i).astype(jnp.float32)


def depth(absorb):
    return jnp.dot(tri(), absorb, precision=lax.Precision.HIGHEST,
                   preferred_element_type=jnp.float32)


def slot_step(tab, c_ref, phys, rows, west, east, out, coef, par_ref, cross, along, one, two):
    j = pl.program_id(0)
    w_odd = tab[j, 0] % 2
    e_odd = tab[j, 1] % 2
    lane = lanes()
    col = lane % SIDE
    at_w = col == 0
    at_e = col == SIDE - 1
    low = lane < 16
    high = lane >= 112
    H = (slice(0, 128), slice(128, 256))
    edge = jnp.concatenate([phys[0, 200:224, 0:128], phys[0, 200:224, 128:256]], axis=0)
    sel_r = lax.broadcasted_iota(jnp.int32, (128, 256), 0)
    sel_c = lax.broadcasted_iota(jnp.int32, (128, 256), 1)
    sel = ((sel_c == SIDE * sel_r) & (sel_r < SIDE)).astype(jnp.float32)
    edge_lane = jnp.where(low, edge, 0.0)
    edge_w = jnp.dot(edge_lane, sel, precision=lax.Precision.HIGHEST,
                     preferred_element_type=jnp.float32)
    edge_s = roll(edge, 112)
    fn_up = roll(phys[0, 48:96, H[0]], 16)
    level = lax.broadcasted_iota(jnp.int32, (LEV, 128), 0)
    for h in range(2):
        fe = phys[0, 0:48, H[h]]
        fn = phys[0, 48:96, H[h]]
        fw = jnp.where(at_w, edge_w[:, H[h]], roll(fe, 1))
        if h == 0:
            fs = jnp.where(low, edge_s, fn_up)
        else:
            fs = jnp.where(low, fn_up, roll(fn, 16))
        ow = DIFF * phys[0, 192:193, H[h]]
        oe = DIFF * phys[0, 193:194, H[h]]
        os = DIFF * phys[0, 194:195, H[h]]
        on = DIFF * phys[0, 195:196, H[h]]
        coef[0, :, H[h]] = (1.0 - (ow + oe + os + on)) - pos(fe) + jnp.minimum(fw, 0.0) - pos(fn) + jnp.minimum(fs, 0.0)
        coef[1, :, H[h]] = oe - jnp.minimum(fe, 0.0)
        coef[2, :, H[h]] = ow + pos(fw)
        coef[3, :, H[h]] = on - jnp.minimum(fn, 0.0)
        coef[4, :, H[h]] = os + pos(fs)
        below = jnp.where(level < LEV - 1, phys[0, 144:192, H[h]], 0.0)
        coef[5, :, H[h]] = below

    wide = lax.broadcasted_iota(jnp.int32, (HALF, 128), 1)
    flat = (wide // SIDE) % 2 == 0
    for p in range(2):
        hp = slice(p * HALF, (p + 1) * HALF)
        upper = rows[0, p, 1, :, :]
        under = roll(rows[0, p, 0, :, :], 32)
        cross[0, hp, :] = jnp.where(flat, upper, under)
        cross[1, hp, :] = jnp.where(flat, under, upper)
        for h in range(2):
            along[hp, H[h]] = jnp.where(wide % 2 == 0, roll(west[0, hp, H[h]], 128 - 15 - w_odd),
                                        roll(east[0, hp, H[h]], 15 - e_odd))

    def where(g, m):
        return pl.ds(pl.multiple_of((3 * g + m) * LEV, LEV), LEV)

    def turn_to(g, m, around):
        hm = slice(m * LEV, (m + 1) * LEV)
        a = c_ref[0, where(g, m), H[0]]
        b = c_ref[0, where(g, m), H[1]]
        ends = roll(cross[lax.rem(g, 2), hm, :], 112 - 16 * g)
        an, bn = roll(a, 112), roll(b, 112)
        as_, bs = roll(a, 16), roll(b, 16)
        around[m, 0, :, H[0]] = jnp.where(high, bn, an)
        around[m, 0, :, H[1]] = jnp.where(high, ends, bn)
        around[m, 1, :, H[0]] = jnp.where(low, ends, as_)
        around[m, 1, :, H[1]] = jnp.where(low, as_, bs)
        for h, v in enumerate((a, b)):
            sides = roll(along[hm, H[h]], lax.rem(128 - 2 * g, 128))
            around[m, 2, :, H[h]] = jnp.where(at_w, sides, roll(v, 1))
            around[m, 3, :, H[h]] = jnp.where(at_e, sides, roll(v, 127))

    def move(g, m, around):
        for h in range(2):
            v = c_ref[0, where(g, m), H[h]]
            moved = (coef[0, :, H[h]] * v + coef[1, :, H[h]] * around[m, 3, :, H[h]]
                     + coef[2, :, H[h]] * around[m, 2, :, H[h]]
                     + coef[3, :, H[h]] * around[m, 0, :, H[h]] + coef[4, :, H[h]] * around[m, 1, :, H[h]])
            flux = coef[5, :, H[h]] * (pltpu.roll(moved, LEV - 1, 0) - moved)
            out[0, where(g, m), H[h]] = moved + flux - pltpu.roll(flux, 1, 0)

    for m in range(3):
        turn_to(0, m, one)

    def pair(i, carry):
        for now, then, g in ((one, two, 2 * i), (two, one, 2 * i + 1)):
            for m in range(3):
                move(g, m, now)
                turn_to(jnp.minimum(g + 1, 7), m, then)
        return carry

    lax.fori_loop(0, 4, pair, 0)
    absorb = 0.04 + 0.02 * (pos(out[0, 480:528, :]) + pos(out[0, 528:576, :]))
    above = depth(absorb)
    par_ref[...] = phys[0, 196:197, :] * jnp.exp(-(above + 0.5 * absorb))
    for h in range(2):
        wet = jnp.broadcast_to(phys[0, 197:198, H[h]], (8, 128))

        def chunk(i, carry):
            l0 = pl.multiple_of(i * 8, 8)

            def get(t):
                return out[0, pl.ds(pl.multiple_of(t * LEV + l0, 8), 8), H[h]]

            held = [get(t) for t in range(NTR)]

            def put(t, v):
                out[0, pl.ds(pl.multiple_of(t * LEV + l0, 8), 8), H[h]] = v * wet

            warm = jnp.exp(0.0639 * phys[0, pl.ds(pl.multiple_of(96 + l0, 8), 8), H[h]])
            par = par_ref[pl.ds(l0, 8), H[h]]
            react(lambda t: held[t], put, par, warm)
            return carry

        lax.fori_loop(0, LEV // 8, chunk, 0)


def first_kernel(tab, c_ref, phys, rows, west, east, out, rows_out, w_out, e_out, coef, par_ref, cross, along, one, two):
    j = pl.program_id(0)
    odd = j % 2

    @pl.when(tab[j, 2] == 1)
    def _():
        slot_step(tab, c_ref, phys, rows, west, east, out, coef, par_ref, cross, along, one, two)

    @pl.when(tab[j, 2] == 0)
    def _():
        out[...] = jnp.zeros_like(out)

    clear_first(odd, w_out, e_out)
    pack_edges(out, rows_out, w_out, e_out, odd)


def last_kernel(tab, c_ref, phys, rows, west, east, out, light_out, coef, par_ref, cross, along, one, two):
    j = pl.program_id(0)

    @pl.when(tab[j, 2] == 1)
    def _():
        slot_step(tab, c_ref, phys, rows, west, east, out, coef, par_ref, cross, along, one, two)
        absorb = 0.04 + 0.02 * (pos(out[0, 480:528, :]) + pos(out[0, 528:576, :]))
        above = depth(absorb)
        light_out[0] = jnp.exp(-above) - jnp.exp(-(above + absorb))

    @pl.when(tab[j, 2] == 0)
    def _():
        out[...] = jnp.zeros_like(out)
        light_out[...] = jnp.zeros_like(light_out)


def step(last, tab, current, phys, rows, came_west, came_east):
    edge_spec = pl.BlockSpec((1, ROWS3, CELLS), lambda j, tab: (j // 2, 0, 0))
    edge_shape = jax.ShapeDtypeStruct((4, ROWS3, CELLS), jnp.float32)
    if last:
        outs = [pl.BlockSpec((1, LEV, CELLS), lambda j, tab: (tab[j, 5], 0, 0))]
        shapes = [jax.ShapeDtypeStruct((16, LEV, CELLS), jnp.float32)]
    else:
        outs = [pl.BlockSpec((1, 2, 2, HALF, 128), lambda j, tab: (tab[j, 4], 0, 0, 0, 0)), edge_spec, edge_spec]
        shapes = [jax.ShapeDtypeStruct((8, 2, 2, HALF, 128), jnp.float32), edge_shape, edge_shape]
    return pl.pallas_call(
        last_kernel if last else first_kernel,
        grid_spec=pltpu.PrefetchScalarGridSpec(
            num_scalar_prefetch=1,
            grid=(SLOTS,),
            in_specs=[
                pl.BlockSpec((1, NTR * LEV, CELLS), lambda j, tab: (j, 0, 0)),
                pl.BlockSpec((1, PHYS, CELLS), lambda j, tab: (tab[j, 8], 0, 0)),
                pl.BlockSpec((1, 2, 2, HALF, 128), lambda j, tab: (tab[j, 3], 0, 0, 0, 0)),
                pl.BlockSpec((1, ROWS3, CELLS), lambda j, tab: (tab[j, 0] // 2, 0, 0)),
                pl.BlockSpec((1, ROWS3, CELLS), lambda j, tab: (tab[j, 1] // 2, 0, 0)),
            ],
            out_specs=[pl.BlockSpec((1, NTR * LEV, CELLS), lambda j, tab: (j, 0, 0))] + outs,
            scratch_shapes=[VM((6, LEV, CELLS), jnp.float32), VM((LEV, CELLS), jnp.float32),
                            VM((2, ROWS3, 128), jnp.float32), VM((ROWS3, CELLS), jnp.float32),
                            VM((3, 4, LEV, CELLS), jnp.float32), VM((3, 4, LEV, CELLS), jnp.float32)],
        ),
        out_shape=[jax.ShapeDtypeStruct((SLOTS, NTR * LEV, CELLS), jnp.float32)] + shapes,
        cost_estimate=pl.CostEstimate(flops=10**8, bytes_accessed=25 * 10**6, transcendentals=10**6),
        name="last_step" if last else "first_step",
    )(tab, current, phys, rows, came_west, came_east)


def spread_matrix(shape, lhs_wide, dtype=jnp.bfloat16):
    i = lax.broadcasted_iota(jnp.int32, shape, 0)
    j = lax.broadcasted_iota(jnp.int32, shape, 1)
    return (i // 3 == j if lhs_wide else i == j // 3).astype(dtype)


def coarse_kernel(phys, mix, flags, y_ref, col_ref, every_ref, third_ref):
    step = pl.program_id(0)

    @pl.when(step == 0)
    def _():
        i = lax.broadcasted_iota(jnp.int32, (384, 128), 0)
        j = lax.broadcasted_iota(jnp.int32, (384, 128), 1)
        every_ref[...] = (i // 3 == j).astype(jnp.bfloat16)
        third_ref[...] = (i == 3 * j + 2).astype(jnp.bfloat16)
        col_ref[...] = jnp.zeros_like(col_ref)

    def dot(a, b):
        return jnp.dot(a, b, preferred_element_type=jnp.float32)

    u = jnp.concatenate([phys[f, 0:48, :] for f in range(6)], axis=0)
    vt = jnp.concatenate([phys[2, 48:96, :], phys[5, 48:96, :]] + [phys[f, 96:144, :] for f in range(6)], axis=0)
    east = dot(u, third_ref[...])
    rest = dot(vt, every_ref[...])

    def part(x, n):
        return x[48 * n:48 * n + 48]

    for c in range(2):
        e = (part(east, 3 * c) + part(east, 3 * c + 1) + part(east, 3 * c + 2)) / 3.0 * flags[c, 1:2, :]
        y_ref[c, 0:48, :] = e
        y_ref[c, 48:96, :] = part(rest, c) / 3.0 * flags[c, 3:4, :]
        y_ref[c, 96:144, :] = (part(rest, 3 * c + 2) + part(rest, 3 * c + 3) + part(rest, 3 * c + 4)) / 9.0
        y_ref[c, 144:192, :] = mix[c].astype(jnp.float32)
        y_ref[c, 192:200, :] = flags[c]
        r = 2 * step + c
        col_ref[...] = jnp.where(lanes() == r, roll(e, r + 1), col_ref[...])


def coarse(phys_t, mix_t, flags):
    return pl.pallas_call(
        coarse_kernel,
        grid=(SIDE // 2,),
        in_specs=[
            pl.BlockSpec((6, 144, 384), lambda r: (r, 0, 0)),
            pl.BlockSpec((2, LEV, 128), lambda r: (r, 0, 0)),
            pl.BlockSpec((2, 8, 128), lambda r: (r, 0, 0)),
        ],
        out_specs=[
            pl.BlockSpec((2, 200, 128), lambda r: (r, 0, 0)),
            pl.BlockSpec((LEV, 128), lambda r: (0, 0)),
        ],
        out_shape=[
            jax.ShapeDtypeStruct((SIDE, 200, 128), jnp.float32),
            jax.ShapeDtypeStruct((LEV, 128), jnp.float32),
        ],
        scratch_shapes=[VM((384, 128), jnp.bfloat16), VM((384, 128), jnp.bfloat16)],
        cost_estimate=pl.CostEstimate(flops=10**9, bytes_accessed=8 * 10**6, transcendentals=0),
        name="coarse",
    )(phys_t, mix_t, flags)


def package_kernel(tab, y_ref, col_ref, row_ref, out):
    group = lax.broadcasted_iota(jnp.int32, (8, 128), 1) // SIDE

    def chunk(i, carry):
        at = pl.ds(pl.multiple_of(8 * i, 8), 8)
        for h in range(2):
            vals = [y_ref[8 * h + g, at, :] for g in range(8)]
            for d in (1, 2, 4):
                lower = (group // d) % 2 == 0
                for g in range(8):
                    if g & d:
                        continue
                    a, b = vals[g], vals[g + d]
                    vals[g] = jnp.where(lower, a, roll(b, 16 * d))
                    vals[g + d] = jnp.where(lower, roll(a, 128 - 16 * d), b)
            for k in range(TILE):
                out[tab[k, 7], at, 128 * h:128 * h + 128] = vals[k]
        return carry

    lax.fori_loop(0, 25, chunk, 0)
    i = lax.broadcasted_iota(jnp.int32, (256, 128), 0)
    j = lax.broadcasted_iota(jnp.int32, (256, 128), 1)
    last = (i == SIDE * j + SIDE - 1).astype(jnp.float32)
    low = lanes() < SIDE
    for k in range(TILE):
        if k:
            west = jnp.dot(out[tab[k - 1, 7], 0:48, :], last, precision=lax.Precision.HIGHEST,
                           preferred_element_type=jnp.float32)
        else:
            west = col_ref[...]
        edge = jnp.where(low, west, roll(row_ref[...], (16 - 16 * k) % 128))
        out[tab[k, 7], 200:224, 0:128] = edge[0:24]
        out[tab[k, 7], 200:224, 128:256] = edge[24:48]


def package(tab, y, col, row):
    return pl.pallas_call(
        package_kernel,
        in_specs=[pl.BlockSpec(memory_space=pltpu.SMEM)] + [pl.BlockSpec(memory_space=VM)] * 3,
        out_specs=pl.BlockSpec(memory_space=VM),
        out_shape=jax.ShapeDtypeStruct((8, PHYS, CELLS), jnp.float32),
        cost_estimate=pl.CostEstimate(flops=10**7, bytes_accessed=4 * 10**6, transcendentals=0),
        name="package",
    )(tab, y, col, row)


MESH = pl.DeviceIdType.MESH


def remote(src, dst, send, recv, where):
    return pltpu.make_async_remote_copy(src_ref=src, dst_ref=dst, send_sem=send, recv_sem=recv,
                                        device_id=where, device_id_type=MESH)


PARTS = 4
PART = PHYS // PARTS
ORDER = (0, 5, 10, 15, 4, 1, 8, 2, 12, 3, 6, 9, 7, 13, 11, 14)


def each(first, last, fn):
    def body(d, carry):
        fn(d)
        return carry

    lax.fori_loop(first, last, body, 0)


def halo_kernel(first, *refs):
    if first:
        (tab, up_ref, phys, rows_ref, phys_out, got_s, got_n, pick, turn, mid0, mid1, mid2, mid3,
         up_send, up_recv, dn_send, dn_recv, z_send, z_recv, y_send, y_recv, own) = refs
        mid = (mid0, mid1, mid2, mid3)
    else:
        (tab, up_ref, w_ref, e_ref, rows_ref, from_w, from_e, got_s, got_n, pick,
         up_send, up_recv, dn_send, dn_recv, we_send, we_recv) = refs
    lat, lon = lax.axis_index("lat"), lax.axis_index("lon")
    bands, count = lax.axis_size("lat"), lax.axis_size("lon")
    sides = (lax.rem(lat + 1, bands), lax.rem(lat + bands - 1, bands))
    row, place = lon // 4, lax.rem(lon, 4)
    got = (got_s, got_n)
    barrier = pltpu.get_barrier_semaphore()

    def ahead(d):
        return lax.rem(row + d // 4, 4) * 4 + lax.rem(place + d % 4, 4)

    def behind(d):
        return lax.rem(row + 4 - d // 4, 4) * 4 + lax.rem(place + 4 - d % 4, 4)

    def greet(d):
        peer = lax.rem(lon + d, count)
        for side in sides:
            pl.semaphore_signal(barrier, inc=1, device_id=(side, peer), device_id_type=MESH)

    each(0, count, greet)
    each(1, count, lambda d: pl.semaphore_signal(
        barrier, inc=1, device_id=(lat, lax.rem(lon + d, count)), device_id_type=MESH))
    pl.semaphore_wait(barrier, 3 * count - 1)

    def up(n, d):
        peer = ahead(d)
        return remote(up_ref.at[peer, 1 - n], got[n].at[lon], up_send.at[n, d], up_recv.at[n, d], (sides[n], peer))

    def up_from(n, d):
        peer = behind(d)
        return remote(up_ref.at[peer, 1 - n], got[n].at[peer], up_send.at[n, d], up_recv.at[n, d], (sides[1 - n], peer))

    def down(n, d):
        peer = ahead(d)
        return remote(pick.at[n, peer], rows_ref.at[lon, n], dn_send.at[n, d], dn_recv.at[n, d], (lat, peer))

    def down_from(n, d):
        peer = behind(d)
        return remote(pick.at[n, peer], rows_ref.at[peer, n], dn_send.at[n, d], dn_recv.at[n, d], (lat, peer))

    def piece(p):
        return pl.ds(p * PART, PART)

    def by_z(p, d):
        z = lax.rem(place + d, 4)
        return remote(phys.at[z, :, piece(p)], mid[p].at[place], z_send.at[p, d], z_recv.at[p, d], (lat, 4 * row + z))

    def from_z(p, d):
        z = lax.rem(place + 4 - d, 4)
        return remote(phys.at[z, :, piece(p)], mid[p].at[z], z_send.at[p, d], z_recv.at[p, d], (lat, 4 * row + z))

    def by_y(p, d):
        y = lax.rem(row + d, 4)
        return remote(turn.at[y, :, piece(p)], phys_out.at[row, :, piece(p)], y_send.at[p, d], y_recv.at[p, d], (lat, 4 * y + place))

    def from_y(p, d):
        y = lax.rem(row + 4 - d, 4)
        return remote(turn.at[y, :, piece(p)], phys_out.at[y, :, piece(p)], y_send.at[p, d], y_recv.at[p, d], (lat, 4 * y + place))

    def lift(n):
        for d in ORDER:
            up(n, d).start()

    def descend(n):
        for d in ORDER:
            up_from(n, d).wait_recv()

        def choose(o):
            value = got[n][tab[o, 2 * n]]
            pick[n, o] = jnp.where(tab[o, 2 * n + 1] > 0, value, 0.0)

        each(0, count, choose)
        rows_ref[lon, n] = pick[n, lon]
        for d in ORDER[1:]:
            down(n, d).start()

    def stay(p):
        return pltpu.make_async_copy(phys.at[place, :, piece(p)], mid[p].at[place], own.at[p])

    def send_z(p):
        for d in (2, 1, 3):
            by_z(p, d).start()
        stay(p).start()

    def send_y(p):
        for d in (1, 2, 3):
            from_z(p, d).wait_recv()
        stay(p).wait()

        def sort(q):
            turn[q // 2, lax.rem(q, 2), piece(p)] = mid[p][tab[q, 4] // 2, lax.rem(tab[q, 4], 2)]

        each(0, 8, sort)
        for d in (2, 1, 3):
            by_y(p, d).start()
        phys_out[row, :, piece(p)] = turn[row, :, piece(p)]

    if first:
        send_z(0)
        lift(0)
        send_z(1)
        lift(1)
        send_z(2)
        send_z(3)
        send_y(0)
        descend(0)
        send_y(1)
        descend(1)
        send_y(2)
        send_y(3)
    else:
        to_e = remote(e_ref, from_w, we_send.at[0], we_recv.at[0], (lat, lax.rem(lon + 1, count)))
        to_w = remote(w_ref, from_e, we_send.at[1], we_recv.at[1], (lat, lax.rem(lon + count - 1, count)))
        lift(0)
        lift(1)
        descend(0)
        to_e.start()
        to_w.start()
        descend(1)
    for n in range(2):
        for d in ORDER[1:]:
            down_from(n, d).wait_recv()
    for n in range(2):
        for d in ORDER:
            up(n, d).wait_send()
        for d in ORDER[1:]:
            down(n, d).wait_send()
    if first:
        for p in range(PARTS):
            for d in (1, 2, 3):
                from_y(p, d).wait_recv()
                by_z(p, d).wait_send()
                by_y(p, d).wait_send()
    else:
        to_e.wait()
        to_w.wait()


def halo(first, tab, rows, *rest):
    anywhere = pl.BlockSpec(memory_space=pl.ANY)
    here = pl.BlockSpec(memory_space=VM)
    edge = jax.ShapeDtypeStruct((4, ROWS3, CELLS), jnp.float32)
    dma = pltpu.SemaphoreType.DMA
    sent = pltpu.VMEM((4, 2, PHYS, CELLS), jnp.float32)
    out = [jax.ShapeDtypeStruct((16, 2, HALF, 128), jnp.float32)]
    scratch = [VM((16, HALF, 128), jnp.float32), VM((16, HALF, 128), jnp.float32),
               VM((2, 16, HALF, 128), jnp.float32)]
    sems = [dma((2, 16)), dma((2, 16)), dma((2, 16)), dma((2, 16))]
    if first:
        in_specs, out_specs = [here], [here, here]
        out.append(jax.ShapeDtypeStruct((4, 2, PHYS, CELLS), jnp.float32))
        scratch += [sent] + [VM((4, 2, PART, CELLS), jnp.float32)] * PARTS
        scratch += sems + [dma((PARTS, 4))] * 4 + [dma((PARTS,))]
        rest = [rest[0].reshape(4, 2, PHYS, CELLS)]
    else:
        in_specs, out_specs = [anywhere] * 2, [here] + [anywhere] * 2
        out += [edge, edge]
        scratch += sems + [dma((2,)), dma((2,))]
    rows, *more = pl.pallas_call(
        functools.partial(halo_kernel, first),
        in_specs=[pl.BlockSpec(memory_space=pltpu.SMEM), here] + in_specs,
        out_specs=out_specs,
        out_shape=out,
        scratch_shapes=scratch,
        compiler_params=pltpu.CompilerParams(collective_id=1 if first else 2, has_side_effects=True),
        cost_estimate=pl.CostEstimate(flops=10**6, bytes_accessed=10**8, transcendentals=0),
        name="halo_phys" if first else "halo",
    )(tab, rows.reshape(16, 2, HALF, 128), *rest)
    return [rows.reshape(8, 2, 2, HALF, 128)] + more


def heat_kernel(tab, got, wet, light, out, fine):
    lane = lanes()
    group = lane // SIDE
    for r in range(SIDE):
        half = slice(128 * (r // 8), 128 * (r // 8) + 128)
        acc = jnp.zeros((LEV, 128), jnp.float32)
        for k in range(TILE):
            acc = jnp.where(group == k, roll(got[tab[k, 6], :, half], (16 * k - 16 * (r % 8)) % 128), acc)
        acc = jnp.where(wet[r:r + 1, :] > 0.0, acc, 0.0)
        for a in range(3):
            fine[pl.ds(3 * r + a, LEV, stride=LEV), :] = acc
    spread = spread_matrix((128, 384), False)
    stacked = jnp.concatenate([spread] * 3, axis=0)

    def levels(i, carry):
        x = fine[pl.ds(pl.multiple_of(i * 8 * LEV, 8 * LEV), 8 * LEV), :]
        high = x.astype(jnp.bfloat16)
        rest = x - high.astype(jnp.float32)
        mid = rest.astype(jnp.bfloat16)
        low = (rest - mid.astype(jnp.float32)).astype(jnp.bfloat16)
        wide = jnp.dot(jnp.concatenate([high, mid, low], axis=1), stacked,
                       preferred_element_type=jnp.float32)
        for l in range(8):
            out[8 * i + l] = (light[...] * wide[l * LEV:l * LEV + LEV]).astype(jnp.bfloat16)
        return carry

    lax.fori_loop(0, LEV // 8, levels, 0)


def heat(tab, got, wet, light):
    return pl.pallas_call(
        heat_kernel,
        in_specs=[pl.BlockSpec(memory_space=pltpu.SMEM)] + [pl.BlockSpec(memory_space=VM)] * 3,
        out_specs=pl.BlockSpec(memory_space=VM),
        out_shape=jax.ShapeDtypeStruct((LEV, 48, 384), jnp.bfloat16),
        scratch_shapes=[VM((LEV * LEV, 128), jnp.float32)],
        cost_estimate=pl.CostEstimate(flops=10**9, bytes_accessed=3 * 10**6, transcendentals=0),
        name="heat",
    )(tab, got, wet, light)


def prep_kernel(base, south, north, west, east, light, flags, tab, meet, sums):
    lat, lon = lax.axis_index("lat"), lax.axis_index("lon")
    wet = base[0:16, :]
    lane = lax.broadcasted_iota(jnp.int32, (SIDE, 128), 1)
    line = lax.broadcasted_iota(jnp.int32, (SIDE, 128), 0)
    wet_e = jnp.where(lane == 127, roll(east[0:16, :], 127), roll(wet, 127))
    wet_w = jnp.where(lane == 0, roll(west[0:16, :], 1), roll(wet, 1))
    inner_n = (lat < lax.axis_size("lat") - 1).astype(jnp.float32)
    inner_s = (lat > 0).astype(jnp.float32)
    wet_n = jnp.where(line == 15, inner_n * north[0:1, :], pltpu.roll(wet, 15, 0))
    wet_s = jnp.where(line == 0, inner_s * south[15:16, :], pltpu.roll(wet, 1, 0))
    sums[...] = jnp.dot(light[...], spread_matrix((384, 128), True, jnp.float32),
                        precision=lax.Precision.HIGHEST, preferred_element_type=jnp.float32)
    mean = sums[pl.ds(0, 16, stride=3), :] + sums[pl.ds(1, 16, stride=3), :] + sums[pl.ds(2, 16, stride=3), :]
    values = (wet * wet_w, wet * wet_e, wet * wet_s, wet * wet_n, mean / 9.0, wet,
              jnp.zeros_like(wet), jnp.zeros_like(wet))
    for i, v in enumerate(values):
        flags[pl.ds(i, 16, stride=8), :] = v

    def ints(ref):
        return ref[16:17, :].astype(jnp.int32)

    def owner_of(code):
        return lax.shift_right_arithmetic(code, 3) & 15

    def f32(x):
        return x.astype(jnp.float32)

    def wide(x, n):
        return jnp.broadcast_to(x, (n, 128))

    band = ints(base)
    big_i = lax.broadcasted_iota(jnp.int32, (128, 128), 0)
    big_j = lax.broadcasted_iota(jnp.int32, (128, 128), 1)
    down = jnp.sum(jnp.where(big_i == big_j, f32(wide(band, 128)), 0.0), axis=1, keepdims=True).astype(jnp.int32)
    down = jnp.broadcast_to(down, (128, 128))
    own_i, own_j = owner_of(down), owner_of(wide(band, 128))
    before = (big_i < big_j) & (down >= 0)
    near = jnp.sum(f32(before & (big_i // 8 == big_j // 8) & ((own_i & 3) == (own_j & 3))), axis=0, keepdims=True)
    far = jnp.sum(f32(before & (big_i // 32 == big_j // 32) & (own_i == own_j)), axis=0, keepdims=True)
    ids = lax.broadcasted_iota(jnp.int32, (1, 128), 1)
    own = owner_of(band)
    wet_b = band >= 0

    def total(mask, value):
        n = mask.shape[0]
        return jnp.sum(jnp.where(mask, wide(f32(value), n), 0.0), axis=1, keepdims=True)

    slot = lax.broadcasted_iota(jnp.int32, (8, 128), 0)
    ids8 = wide(ids, 8)
    band8 = wide(band, 8)
    hit = band8 == (lat * 16 + lon) * SLOTS + slot
    full = total(hit, jnp.ones_like(band))
    pair = total(hit, ids // 16)
    got_at = total(hit, ids // 32 * 2) + total(hit, far)
    west_code = total(hit, roll(band, 1))
    east_code = total(hit, roll(band, 127))

    def slot_of(code):
        code = code.astype(jnp.int32)
        return f32(jnp.where(code >= 0, code & 7, 0))

    w_slot, e_slot = slot_of(west_code), slot_of(east_code)
    some = jnp.broadcast_to(ids8 // 16 == slot, (8, 128))
    band_hit = wide(f32(jnp.max(f32(hit), axis=0, keepdims=True)), 8) > 0.0
    first_of = lax.broadcasted_iota(jnp.int32, (8, 1), 0).astype(jnp.float32)
    pair_used = total(some & band_hit, jnp.ones_like(band))
    pair_spare = jnp.min(jnp.where(pair_used > 0.0, 99.0, first_of), axis=0, keepdims=True)
    my_tile = ids // TILE == lon
    tile_mask = (ids8 // TILE == lon) & (ids8 - TILE * lon == slot)
    t_wet = total(tile_mask & (band8 >= 0), jnp.ones_like(band))
    t_own = total(tile_mask & (band8 >= 0), own)
    z_key = (own & 3) * 2 + near.astype(jnp.int32)
    z_at = total(tile_mask & (band8 >= 0), z_key)
    z_used = total(wide(my_tile & wet_b, 8) & (wide(z_key, 8) == slot), jnp.ones_like(band))
    z_spare = jnp.min(jnp.where(z_used > 0.0, 99.0, first_of), axis=0, keepdims=True)
    z_at = jnp.where(t_wet > 0.0, z_at, jnp.minimum(z_spare, 7.0))
    t_first = lax.broadcasted_iota(jnp.int32, (16, 1), 0).astype(jnp.float32)
    row16 = lax.broadcasted_iota(jnp.int32, (16, 128), 0)
    in_tile = wide(my_tile & wet_b, 16)
    to_me = jnp.max(f32(hit), axis=0, keepdims=True)
    src_used = total((wide(ids // TILE, 16) == row16) & (wide(to_me, 16) > 0.0), jnp.ones_like(band))
    src_spare = jnp.min(jnp.where(src_used > 0.0, 99.0, t_first), axis=0, keepdims=True)
    src = total(hit, ids // TILE)
    fields = (w_slot, e_slot, full, pair, jnp.where(full > 0.0, pair, jnp.minimum(pair_spare, 7.0)),
              jnp.where(full > 0.0, src, src_spare), t_own, z_at, got_at)
    acc = jnp.zeros((8, 128), jnp.float32)
    for i, v in enumerate(fields):
        acc = jnp.where(ids8 == i, v, acc)
    tab[...] = acc.astype(jnp.int32)
    ids16 = wide(ids, 16)
    here = (ids16 // 16 == lon // 2) & wide(wet_b, 16) & (wide(own, 16) == row16)
    acc = jnp.zeros((16, 128), jnp.float32)
    for i, other in enumerate((ints(south), ints(north))):
        both = here & (wide(other, 16) >= 0)
        acc = jnp.where(ids16 == 2 * i, total(both, owner_of(other)), acc)
        acc = jnp.where(ids16 == 2 * i + 1, total(both, jnp.ones_like(band)), acc)
    mine = wet_b & (ids // 32 == lon // 4) & ((own & 3) == lax.rem(lon, 4))
    y_key = lax.shift_right_arithmetic(own, 2) * 2 + far.astype(jnp.int32)
    turn = wide(mine, 16) & (wide(y_key, 16) == row16)
    acc = jnp.where(ids16 == 4, total(turn, (ids // 8 & 3) * 2 + near.astype(jnp.int32)), acc)
    meet[...] = acc.astype(jnp.int32)


def prep(base, south, north, west, east, light):
    flags, tab, meet = pl.pallas_call(
        prep_kernel,
        in_specs=[pl.BlockSpec(memory_space=VM)] * 6,
        out_specs=[pl.BlockSpec(memory_space=VM)] * 3,
        out_shape=[jax.ShapeDtypeStruct((128, 128), jnp.float32),
                   jax.ShapeDtypeStruct((8, 128), jnp.int32),
                   jax.ShapeDtypeStruct((16, 128), jnp.int32)],
        scratch_shapes=[VM((48, 128), jnp.float32)],
        cost_estimate=pl.CostEstimate(flops=10**7, bytes_accessed=10**5, transcendentals=0),
        name="prep",
    )(base, south, north, west, east, light)
    return flags.reshape(SIDE, 8, 128), tab, meet


def shift(x, axis, by):
    n = lax.axis_size(axis)
    return lax.ppermute(x, axis, [(i, (i + by) % n) for i in range(n)])


def swap(x):
    return lax.all_to_all(x, "lon", split_axis=0, concat_axis=0, tiled=True)


def on_device(tracers, phys_fine, mix_coarse, surf_light, land_mask, owner_map):
    wet = land_mask.astype(jnp.float32)
    base = jnp.concatenate([wet, owner_map.astype(jnp.float32)], axis=0)
    flags, tab, meet = prep(base, shift(base, "lat", 1), shift(base, "lat", -1),
                            shift(base, "lon", 1), shift(base, "lon", -1), surf_light)
    y, col = coarse(jnp.swapaxes(phys_fine, 1, 2), jnp.swapaxes(mix_coarse, 1, 2), flags)
    tab, y, col = lax.optimization_barrier((tab, y, col))
    west_col = shift(col, "lon", 1)
    south_row = shift(y[SIDE - 1, 48:96], "lat", 1)
    rows_out, w_out, e_out = pack(tab, tracers)
    came_west = shift(e_out, "lon", 1)
    came_east = shift(w_out, "lon", -1)
    y, rows_out = lax.optimization_barrier((y, rows_out))
    packed = package(tab, y, west_col, south_row)
    rows, phys = halo(True, meet, rows_out, packed)
    phys = phys.reshape(8, PHYS, CELLS)
    current, rows_out, w_out, e_out = step(False, tab, tracers, phys, rows, came_west, came_east)
    rows, came_west, came_east = halo(False, meet, rows_out, w_out, e_out)
    current, light_part = step(True, tab, current, phys, rows, came_west, came_east)
    return current, heat(tab, swap(light_part), wet, surf_light)


def solution(mesh):
    in_specs = (
        P(("lat", "lon"), None, None),
        P("lat", "lon", None),
        P("lat", "lon", None),
        P("lat", "lon"),
        P("lat", "lon"),
        P("lat", None),
    )
    out_specs = (P(("lat", "lon"), None, None), P(None, "lat", "lon"))
    return jax.shard_map(
        on_device, mesh=mesh, in_specs=in_specs, out_specs=out_specs, check_vma=False
    )
```

```python
import functools

import jax
import jax.numpy as jnp
from jax import lax
from jax.experimental import pallas as pl
from jax.experimental.pallas import tpu as pltpu
from jax.sharding import PartitionSpec as P

NTR = 24
LEV = 48
SIDE = 16
CELLS = 256
SLOTS = 8
TILE = 8
PHYS = 224
DIFF = 0.08
VM = pltpu.VMEM
ROWS3 = 3 * LEV
HALF = ROWS3 // 2


def pos(v):
    return jnp.maximum(v, 0.0)


def lanes():
    return lax.broadcasted_iota(jnp.int32, (LEV, 128), 1)


def roll(x, shift):
    return pltpu.roll(x, shift, 1)


def pack_edges(c_ref, rows_ref, w_ref, e_ref, odd):
    lane = lanes()
    group = lane // SIDE
    col = lane % SIDE
    low = lane < SIDE
    for m in range(3):
        blank = jnp.zeros((LEV, 128), jnp.float32)
        ends = [blank, blank]
        both = [blank, blank]
        for g in range(8):
            t = 3 * g + m
            a = c_ref[0, t * LEV:(t + 1) * LEV, 0:128]
            b = c_ref[0, t * LEV:(t + 1) * LEV, 128:256]
            end = jnp.where(low, a, b)
            ends[g % 2] = jnp.where((group == g) | (group == (g + 7) % 8), roll(end, 16 * g) if g else end, ends[g % 2])
            here = (col == 2 * g) | (col == (2 * g + 15) % 16)
            for h, v in enumerate((a, b)):
                both[h] = jnp.where(here, roll(v, 2 * g) if g else v, both[h])
        flat = group % 2 == 0
        put_rows(rows_ref, 0, m, jnp.where(flat, ends[0], ends[1]))
        put_rows(rows_ref, 1, m, jnp.where(flat, ends[1], ends[0]))
        at = slice(m * LEV, (m + 1) * LEV)
        mine = (lane % 2) == odd
        for h in range(2):
            hs = slice(h * 128, (h + 1) * 128)
            turned = roll(both[h], odd)
            w_ref[0, at, hs] = jnp.where(mine, turned, w_ref[0, at, hs])
            e_ref[0, at, hs] = jnp.where(mine, e_ref[0, at, hs], turned)


def put_rows(rows_ref, d, m, x):
    lo = m * LEV
    if lo < HALF:
        n = min(LEV, HALF - lo)
        rows_ref[0, 0, d, lo:lo + n, :] = x[:n]
        if n < LEV:
            rows_ref[0, 1, d, 0:LEV - n, :] = x[n:]
    else:
        rows_ref[0, 1, d, lo - HALF:lo - HALF + LEV, :] = x


def clear_first(odd, *refs):
    @pl.when(odd == 0)
    def _():
        for ref in refs:
            ref[...] = jnp.zeros_like(ref)


def pack_kernel(tab, c_ref, rows_ref, w_ref, e_ref):
    p = pl.program_id(0)
    lane = lanes()
    group = lane // SIDE
    col = lane % SIDE
    even = lane % 2 == 0
    low = lane < SIDE
    flat = group % 2 == 0
    for m in range(3):
        at = slice(m * LEV, (m + 1) * LEV)
        blank = jnp.zeros((LEV, 128), jnp.float32)
        both = [[blank, blank], [blank, blank]]
        for i in range(2):
            ends = [blank, blank]
            for g in range(8):
                t = 3 * g + m
                a = c_ref[i, t * LEV:(t + 1) * LEV, 0:128]
                b = c_ref[i, t * LEV:(t + 1) * LEV, 128:256]
                end = jnp.where(low, a, b)
                ends[g % 2] = jnp.where((group == g) | (group == (g + 7) % 8), roll(end, 16 * g) if g else end, ends[g % 2])
                here = (col == 2 * g) | (col == (2 * g + 15) % 16)
                for h, v in enumerate((a, b)):
                    both[i][h] = jnp.where(here, roll(v, 2 * g) if g else v, both[i][h])
            view = rows_ref.at[pl.ds(tab[2 * p + i, 4], 1)]
            put_rows(view, 0, m, jnp.where(flat, ends[0], ends[1]))
            put_rows(view, 1, m, jnp.where(flat, ends[1], ends[0]))
        for h in range(2):
            hs = slice(h * 128, (h + 1) * 128)
            other = roll(both[1][h], 1)
            w_ref[0, at, hs] = jnp.where(even, both[0][h], other)
            e_ref[0, at, hs] = jnp.where(even, other, both[0][h])


def pack(tab, tracers):
    return pl.pallas_call(
        pack_kernel,
        grid_spec=pltpu.PrefetchScalarGridSpec(
            num_scalar_prefetch=1,
            grid=(SLOTS // 2,),
            in_specs=[pl.BlockSpec((2, NTR * LEV, CELLS), lambda j, tab: (j, 0, 0))],
            out_specs=[
                pl.BlockSpec((8, 2, 2, HALF, 128), lambda j, tab: (0, 0, 0, 0, 0)),
                pl.BlockSpec((1, ROWS3, CELLS), lambda j, tab: (j, 0, 0)),
                pl.BlockSpec((1, ROWS3, CELLS), lambda j, tab: (j, 0, 0)),
            ],
        ),
        out_shape=[
            jax.ShapeDtypeStruct((8, 2, 2, HALF, 128), jnp.float32),
            jax.ShapeDtypeStruct((4, ROWS3, CELLS), jnp.float32),
            jax.ShapeDtypeStruct((4, ROWS3, CELLS), jnp.float32),
        ],
        cost_estimate=pl.CostEstimate(flops=10**7, bytes_accessed=12 * 10**6, transcendentals=0),
        name="pack",
    )(tab, tracers)


def react(get, put, par, warm):
    (carbon_dis, alkalinity, oxygen, nitrate, ammonium, phosphate, silicate, iron_free,
     nano_carbon, diat_carbon, nano_chl, diat_chl, nano_iron, diat_iron, diat_silica,
     micro_zoo, meso_zoo, dissolved_org, small_part, big_part, small_iron, big_iron,
     big_silica, calcite) = [functools.partial(get, t) for t in range(NTR)]
    p_am = pos(ammonium())
    nitrogen = pos(nitrate()) + p_am
    limit_nitro = nitrogen / (0.5 + nitrogen)
    p_ph = pos(phosphate())
    p_fe = pos(iron_free())
    p_si = pos(silicate())
    nutr_nano = jnp.minimum(jnp.minimum(limit_nitro, p_ph / (0.3 + p_ph)), p_fe / (0.2 + p_fe))
    nutr_diat = jnp.minimum(nutr_nano, p_si / (1.0 + p_si))
    nc = nano_carbon()
    dc = diat_carbon()
    wp = warm * par
    prod_nano = 0.1 * wp / (par + 0.5) * nutr_nano * nc
    prod_diat = 0.12 * wp / (par + 1.0) * nutr_diat * dc
    share = (p_am + 0.01) / (nitrogen + 0.02)
    mi = micro_zoo()
    me = meso_zoo()
    graze_nano = 0.08 * warm * mi / (1.0 + pos(nc))
    graze_diat = 0.06 * warm * me / (1.0 + pos(dc))
    loss_nano = graze_nano + 0.02
    loss_diat = graze_diat + 0.02
    eaten_nano = graze_nano * nc
    eaten_diat = graze_diat * dc
    death_micro = 0.03 * mi * pos(mi)
    death_meso = 0.03 * me * pos(me)
    do = dissolved_org()
    sp = small_part()
    bp = big_part()
    remin_doc = 0.03 * warm * do
    remin_poc = 0.02 * warm * sp
    remin_goc = 0.01 * warm * bp
    am = ammonium()
    nitrify = 0.05 * am
    cal = calcite()
    melt_cal = 0.01 * cal
    uptake = prod_nano + prod_diat
    remin = remin_doc + remin_poc + remin_goc
    calcify = 0.02 * prod_nano
    shell = melt_cal - calcify
    put(0, carbon_dis() + remin - uptake + shell)
    su = share * uptake
    fresh = uptake - su
    put(1, alkalinity() + 2.0 * shell + 0.16 * (fresh - nitrify))
    put(2, oxygen() + 1.3 * (uptake - remin) - 0.32 * nitrify)
    put(3, nitrate() + 0.16 * (nitrify - fresh))
    put(4, am + 0.16 * (remin - su - nitrify))
    put(5, phosphate() + 0.01 * (remin - uptake))
    bsi = big_silica()
    melt_si = 0.02 * bsi
    put(6, silicate() + melt_si - 0.15 * prod_diat)
    sfe = small_iron()
    bfe = big_iron()
    melt_sfe = 0.02 * sfe
    melt_bfe = 0.01 * bfe
    put(7, iron_free() + melt_sfe + melt_bfe - 0.005 * uptake)
    put(8, nc + prod_nano - loss_nano * nc)
    put(9, dc + prod_diat - loss_diat * dc)
    x = nano_chl()
    put(10, x + 0.03 * prod_nano - loss_nano * x)
    x = diat_chl()
    put(11, x + 0.03 * prod_diat - loss_diat * x)
    x = nano_iron()
    lost = loss_nano * x
    put(12, x + 0.005 * prod_nano - lost)
    put(20, sfe + lost - melt_sfe)
    x = diat_iron()
    lost = loss_diat * x
    put(13, x + 0.005 * prod_diat - lost)
    put(21, bfe + lost - melt_bfe)
    x = diat_silica()
    lost = loss_diat * x
    put(14, x + 0.15 * prod_diat - lost)
    put(22, bsi + lost - melt_si)
    put(15, mi + 0.3 * eaten_nano - death_micro)
    put(16, me + 0.3 * eaten_diat - death_meso)
    put(17, do + 0.3 * eaten_nano + 0.02 * nc - remin_doc)
    put(18, sp + 0.4 * eaten_nano + death_micro - remin_poc)
    put(19, bp + 0.4 * eaten_diat + 0.02 * dc + death_meso - remin_goc)
    put(23, cal - shell)


def tri():
    i = lax.broadcasted_iota(jnp.int32, (LEV, LEV), 0)
    j = lax.broadcasted_iota(jnp.int32, (LEV, LEV), 1)
    return (j < i).astype(jnp.float32)


def depth(absorb):
    return jnp.dot(tri(), absorb, precision=lax.Precision.HIGHEST,
                   preferred_element_type=jnp.float32)


def slot_step(tab, c_ref, phys, rows, west, east, out, coef, par_ref, cross, along, one, two):
    j = pl.program_id(0)
    w_odd = tab[j, 0] % 2
    e_odd = tab[j, 1] % 2
    lane = lanes()
    col = lane % SIDE
    at_w = col == 0
    at_e = col == SIDE - 1
    low = lane < 16
    high = lane >= 112
    H = (slice(0, 128), slice(128, 256))
    edge = jnp.concatenate([phys[0, 200:224, 0:128], phys[0, 200:224, 128:256]], axis=0)
    sel_r = lax.broadcasted_iota(jnp.int32, (128, 256), 0)
    sel_c = lax.broadcasted_iota(jnp.int32, (128, 256), 1)
    sel = ((sel_c == SIDE * sel_r) & (sel_r < SIDE)).astype(jnp.float32)
    edge_lane = jnp.where(low, edge, 0.0)
    edge_w = jnp.dot(edge_lane, sel, precision=lax.Precision.HIGHEST,
                     preferred_element_type=jnp.float32)
    edge_s = roll(edge, 112)
    fn_up = roll(phys[0, 48:96, H[0]], 16)
    level = lax.broadcasted_iota(jnp.int32, (LEV, 128), 0)
    for h in range(2):
        fe = phys[0, 0:48, H[h]]
        fn = phys[0, 48:96, H[h]]
        fw = jnp.where(at_w, edge_w[:, H[h]], roll(fe, 1))
        if h == 0:
            fs = jnp.where(low, edge_s, fn_up)
        else:
            fs = jnp.where(low, fn_up, roll(fn, 16))
        ow = DIFF * phys[0, 192:193, H[h]]
        oe = DIFF * phys[0, 193:194, H[h]]
        os = DIFF * phys[0, 194:195, H[h]]
        on = DIFF * phys[0, 195:196, H[h]]
        coef[0, :, H[h]] = (1.0 - (ow + oe + os + on)) - pos(fe) + jnp.minimum(fw, 0.0) - pos(fn) + jnp.minimum(fs, 0.0)
        coef[1, :, H[h]] = oe - jnp.minimum(fe, 0.0)
        coef[2, :, H[h]] = ow + pos(fw)
        coef[3, :, H[h]] = on - jnp.minimum(fn, 0.0)
        coef[4, :, H[h]] = os + pos(fs)
        below = jnp.where(level < LEV - 1, phys[0, 144:192, H[h]], 0.0)
        coef[5, :, H[h]] = below

    wide = lax.broadcasted_iota(jnp.int32, (HALF, 128), 1)
    flat = (wide // SIDE) % 2 == 0
    for p in range(2):
        hp = slice(p * HALF, (p + 1) * HALF)
        upper = rows[0, p, 1, :, :]
        under = roll(rows[0, p, 0, :, :], 32)
        cross[0, hp, :] = jnp.where(flat, upper, under)
        cross[1, hp, :] = jnp.where(flat, under, upper)
        for h in range(2):
            along[hp, H[h]] = jnp.where(wide % 2 == 0, roll(west[0, hp, H[h]], 128 - 15 - w_odd),
                                        roll(east[0, hp, H[h]], 15 - e_odd))

    def where(g, m):
        return pl.ds(pl.multiple_of((3 * g + m) * LEV, LEV), LEV)

    def turn_to(g, m, around):
        hm = slice(m * LEV, (m + 1) * LEV)
        a = c_ref[0, where(g, m), H[0]]
        b = c_ref[0, where(g, m), H[1]]
        ends = roll(cross[lax.rem(g, 2), hm, :], 112 - 16 * g)
        an, bn = roll(a, 112), roll(b, 112)
        as_, bs = roll(a, 16), roll(b, 16)
        around[m, 0, :, H[0]] = jnp.where(high, bn, an)
        around[m, 0, :, H[1]] = jnp.where(high, ends, bn)
        around[m, 1, :, H[0]] = jnp.where(low, ends, as_)
        around[m, 1, :, H[1]] = jnp.where(low, as_, bs)
        for h, v in enumerate((a, b)):
            sides = roll(along[hm, H[h]], lax.rem(128 - 2 * g, 128))
            around[m, 2, :, H[h]] = jnp.where(at_w, sides, roll(v, 1))
            around[m, 3, :, H[h]] = jnp.where(at_e, sides, roll(v, 127))

    def move(g, m, around):
        for h in range(2):
            v = c_ref[0, where(g, m), H[h]]
            moved = (coef[0, :, H[h]] * v + coef[1, :, H[h]] * around[m, 3, :, H[h]]
                     + coef[2, :, H[h]] * around[m, 2, :, H[h]]
                     + coef[3, :, H[h]] * around[m, 0, :, H[h]] + coef[4, :, H[h]] * around[m, 1, :, H[h]])
            flux = coef[5, :, H[h]] * (pltpu.roll(moved, LEV - 1, 0) - moved)
            out[0, where(g, m), H[h]] = moved + flux - pltpu.roll(flux, 1, 0)

    for m in range(3):
        turn_to(0, m, one)

    def pair(i, carry):
        for now, then, g in ((one, two, 2 * i), (two, one, 2 * i + 1)):
            for m in range(3):
                move(g, m, now)
                turn_to(jnp.minimum(g + 1, 7), m, then)
        return carry

    lax.fori_loop(0, 4, pair, 0)
    absorb = 0.04 + 0.02 * (pos(out[0, 480:528, :]) + pos(out[0, 528:576, :]))
    above = depth(absorb)
    par_ref[...] = phys[0, 196:197, :] * jnp.exp(-(above + 0.5 * absorb))
    for h in range(2):
        wet = jnp.broadcast_to(phys[0, 197:198, H[h]], (8, 128))

        def chunk(i, carry):
            l0 = pl.multiple_of(i * 8, 8)

            def get(t):
                return out[0, pl.ds(pl.multiple_of(t * LEV + l0, 8), 8), H[h]]

            held = [get(t) for t in range(NTR)]

            def put(t, v):
                out[0, pl.ds(pl.multiple_of(t * LEV + l0, 8), 8), H[h]] = v * wet

            warm = jnp.exp(0.0639 * phys[0, pl.ds(pl.multiple_of(96 + l0, 8), 8), H[h]])
            par = par_ref[pl.ds(l0, 8), H[h]]
            react(lambda t: held[t], put, par, warm)
            return carry

        lax.fori_loop(0, LEV // 8, chunk, 0)


def first_kernel(tab, c_ref, phys, rows, west, east, out, rows_out, w_out, e_out, coef, par_ref, cross, along, one, two):
    j = pl.program_id(0)
    odd = j % 2

    @pl.when(tab[j, 2] == 1)
    def _():
        slot_step(tab, c_ref, phys, rows, west, east, out, coef, par_ref, cross, along, one, two)

    @pl.when(tab[j, 2] == 0)
    def _():
        out[...] = jnp.zeros_like(out)

    clear_first(odd, w_out, e_out)
    pack_edges(out, rows_out, w_out, e_out, odd)


def last_kernel(tab, c_ref, phys, rows, west, east, out, light_out, coef, par_ref, cross, along, one, two):
    j = pl.program_id(0)

    @pl.when(tab[j, 2] == 1)
    def _():
        slot_step(tab, c_ref, phys, rows, west, east, out, coef, par_ref, cross, along, one, two)
        absorb = 0.04 + 0.02 * (pos(out[0, 480:528, :]) + pos(out[0, 528:576, :]))
        above = depth(absorb)
        light_out[0] = jnp.exp(-above) - jnp.exp(-(above + absorb))

    @pl.when(tab[j, 2] == 0)
    def _():
        out[...] = jnp.zeros_like(out)
        light_out[...] = jnp.zeros_like(light_out)


def step(last, tab, current, phys, rows, came_west, came_east):
    edge_spec = pl.BlockSpec((1, ROWS3, CELLS), lambda j, tab: (j // 2, 0, 0))
    edge_shape = jax.ShapeDtypeStruct((4, ROWS3, CELLS), jnp.float32)
    if last:
        outs = [pl.BlockSpec((1, LEV, CELLS), lambda j, tab: (tab[j, 5], 0, 0))]
        shapes = [jax.ShapeDtypeStruct((16, LEV, CELLS), jnp.float32)]
    else:
        outs = [pl.BlockSpec((1, 2, 2, HALF, 128), lambda j, tab: (tab[j, 4], 0, 0, 0, 0)), edge_spec, edge_spec]
        shapes = [jax.ShapeDtypeStruct((8, 2, 2, HALF, 128), jnp.float32), edge_shape, edge_shape]
    return pl.pallas_call(
        last_kernel if last else first_kernel,
        grid_spec=pltpu.PrefetchScalarGridSpec(
            num_scalar_prefetch=1,
            grid=(SLOTS,),
            in_specs=[
                pl.BlockSpec((1, NTR * LEV, CELLS), lambda j, tab: (j, 0, 0)),
                pl.BlockSpec((1, PHYS, CELLS), lambda j, tab: (tab[j, 8], 0, 0)),
                pl.BlockSpec((1, 2, 2, HALF, 128), lambda j, tab: (tab[j, 3], 0, 0, 0, 0)),
                pl.BlockSpec((1, ROWS3, CELLS), lambda j, tab: (tab[j, 0] // 2, 0, 0)),
                pl.BlockSpec((1, ROWS3, CELLS), lambda j, tab: (tab[j, 1] // 2, 0, 0)),
            ],
            out_specs=[pl.BlockSpec((1, NTR * LEV, CELLS), lambda j, tab: (j, 0, 0))] + outs,
            scratch_shapes=[VM((6, LEV, CELLS), jnp.float32), VM((LEV, CELLS), jnp.float32),
                            VM((2, ROWS3, 128), jnp.float32), VM((ROWS3, CELLS), jnp.float32),
                            VM((3, 4, LEV, CELLS), jnp.float32), VM((3, 4, LEV, CELLS), jnp.float32)],
        ),
        out_shape=[jax.ShapeDtypeStruct((SLOTS, NTR * LEV, CELLS), jnp.float32)] + shapes,
        cost_estimate=pl.CostEstimate(flops=10**8, bytes_accessed=25 * 10**6, transcendentals=10**6),
        name="last_step" if last else "first_step",
    )(tab, current, phys, rows, came_west, came_east)


def spread_matrix(shape, lhs_wide, dtype=jnp.bfloat16):
    i = lax.broadcasted_iota(jnp.int32, shape, 0)
    j = lax.broadcasted_iota(jnp.int32, shape, 1)
    return (i // 3 == j if lhs_wide else i == j // 3).astype(dtype)


def coarse_kernel(phys, mix, flags, y_ref, col_ref, every_ref, third_ref):
    step = pl.program_id(0)

    @pl.when(step == 0)
    def _():
        i = lax.broadcasted_iota(jnp.int32, (384, 128), 0)
        j = lax.broadcasted_iota(jnp.int32, (384, 128), 1)
        every_ref[...] = (i // 3 == j).astype(jnp.bfloat16)
        third_ref[...] = (i == 3 * j + 2).astype(jnp.bfloat16)
        col_ref[...] = jnp.zeros_like(col_ref)

    def dot(a, b):
        return jnp.dot(a, b, preferred_element_type=jnp.float32)

    u = jnp.concatenate([phys[f, 0:48, :] for f in range(6)], axis=0)
    vt = jnp.concatenate([phys[2, 48:96, :], phys[5, 48:96, :]] + [phys[f, 96:144, :] for f in range(6)], axis=0)
    east = dot(u, third_ref[...])
    rest = dot(vt, every_ref[...])

    def part(x, n):
        return x[48 * n:48 * n + 48]

    for c in range(2):
        e = (part(east, 3 * c) + part(east, 3 * c + 1) + part(east, 3 * c + 2)) / 3.0 * flags[c, 1:2, :]
        y_ref[c, 0:48, :] = e
        y_ref[c, 48:96, :] = part(rest, c) / 3.0 * flags[c, 3:4, :]
        y_ref[c, 96:144, :] = (part(rest, 3 * c + 2) + part(rest, 3 * c + 3) + part(rest, 3 * c + 4)) / 9.0
        y_ref[c, 144:192, :] = mix[c].astype(jnp.float32)
        y_ref[c, 192:200, :] = flags[c]
        r = 2 * step + c
        col_ref[...] = jnp.where(lanes() == r, roll(e, r + 1), col_ref[...])


def coarse(phys_t, mix_t, flags):
    return pl.pallas_call(
        coarse_kernel,
        grid=(SIDE // 2,),
        in_specs=[
            pl.BlockSpec((6, 144, 384), lambda r: (r, 0, 0)),
            pl.BlockSpec((2, LEV, 128), lambda r: (r, 0, 0)),
            pl.BlockSpec((2, 8, 128), lambda r: (r, 0, 0)),
        ],
        out_specs=[
            pl.BlockSpec((2, 200, 128), lambda r: (r, 0, 0)),
            pl.BlockSpec((LEV, 128), lambda r: (0, 0)),
        ],
        out_shape=[
            jax.ShapeDtypeStruct((SIDE, 200, 128), jnp.float32),
            jax.ShapeDtypeStruct((LEV, 128), jnp.float32),
        ],
        scratch_shapes=[VM((384, 128), jnp.bfloat16), VM((384, 128), jnp.bfloat16)],
        cost_estimate=pl.CostEstimate(flops=10**9, bytes_accessed=8 * 10**6, transcendentals=0),
        name="coarse",
    )(phys_t, mix_t, flags)


def package_kernel(tab, y_ref, col_ref, row_ref, out):
    group = lax.broadcasted_iota(jnp.int32, (8, 128), 1) // SIDE

    def chunk(i, carry):
        at = pl.ds(pl.multiple_of(8 * i, 8), 8)
        for h in range(2):
            vals = [y_ref[8 * h + g, at, :] for g in range(8)]
            for d in (1, 2, 4):
                lower = (group // d) % 2 == 0
                for g in range(8):
                    if g & d:
                        continue
                    a, b = vals[g], vals[g + d]
                    vals[g] = jnp.where(lower, a, roll(b, 16 * d))
                    vals[g + d] = jnp.where(lower, roll(a, 128 - 16 * d), b)
            for k in range(TILE):
                out[tab[k, 7], at, 128 * h:128 * h + 128] = vals[k]
        return carry

    lax.fori_loop(0, 25, chunk, 0)
    i = lax.broadcasted_iota(jnp.int32, (256, 128), 0)
    j = lax.broadcasted_iota(jnp.int32, (256, 128), 1)
    last = (i == SIDE * j + SIDE - 1).astype(jnp.float32)
    low = lanes() < SIDE
    for k in range(TILE):
        if k:
            west = jnp.dot(out[tab[k - 1, 7], 0:48, :], last, precision=lax.Precision.HIGHEST,
                           preferred_element_type=jnp.float32)
        else:
            west = col_ref[...]
        edge = jnp.where(low, west, roll(row_ref[...], (16 - 16 * k) % 128))
        out[tab[k, 7], 200:224, 0:128] = edge[0:24]
        out[tab[k, 7], 200:224, 128:256] = edge[24:48]


def package(tab, y, col, row):
    return pl.pallas_call(
        package_kernel,
        in_specs=[pl.BlockSpec(memory_space=pltpu.SMEM)] + [pl.BlockSpec(memory_space=VM)] * 3,
        out_specs=pl.BlockSpec(memory_space=VM),
        out_shape=jax.ShapeDtypeStruct((8, PHYS, CELLS), jnp.float32),
        cost_estimate=pl.CostEstimate(flops=10**7, bytes_accessed=4 * 10**6, transcendentals=0),
        name="package",
    )(tab, y, col, row)


MESH = pl.DeviceIdType.MESH


def remote(src, dst, send, recv, where):
    return pltpu.make_async_remote_copy(src_ref=src, dst_ref=dst, send_sem=send, recv_sem=recv,
                                        device_id=where, device_id_type=MESH)


PARTS = 4
PART = PHYS // PARTS
ORDER = (0, 5, 10, 15, 4, 1, 8, 2, 12, 3, 6, 9, 7, 13, 11, 14)


def each(first, last, fn):
    def body(d, carry):
        fn(d)
        return carry

    lax.fori_loop(first, last, body, 0)


def halo_kernel(first, *refs):
    if first:
        (tab, up_ref, phys, rows_ref, phys_out, got_s, got_n, pick, turn, mid0, mid1, mid2, mid3,
         up_send, up_recv, dn_send, dn_recv, z_send, z_recv, y_send, y_recv, own, rest, home) = refs
        mid = (mid0, mid1, mid2, mid3)
    else:
        (tab, up_ref, w_ref, e_ref, rows_ref, from_w, from_e, got_s, got_n, pick,
         up_send, up_recv, dn_send, dn_recv, we_send, we_recv, home) = refs
    lat, lon = lax.axis_index("lat"), lax.axis_index("lon")
    bands, count = lax.axis_size("lat"), lax.axis_size("lon")
    sides = (lax.rem(lat + 1, bands), lax.rem(lat + bands - 1, bands))
    row, place = lon // 4, lax.rem(lon, 4)
    got = (got_s, got_n)
    barrier = pltpu.get_barrier_semaphore()

    def ahead(d):
        return lax.rem(row + d // 4, 4) * 4 + lax.rem(place + d % 4, 4)

    def behind(d):
        return lax.rem(row + 4 - d // 4, 4) * 4 + lax.rem(place + 4 - d % 4, 4)

    def greet(d):
        peer = lax.rem(lon + d, count)
        for side in sides:
            pl.semaphore_signal(barrier, inc=1, device_id=(side, peer), device_id_type=MESH)

    each(0, count, greet)
    each(1, count, lambda d: pl.semaphore_signal(
        barrier, inc=1, device_id=(lat, lax.rem(lon + d, count)), device_id_type=MESH))
    pl.semaphore_wait(barrier, 3 * count - 1)

    def up(n, d):
        peer = ahead(d)
        return remote(up_ref.at[peer, 1 - n], got[n].at[lon], up_send.at[n, d], up_recv.at[n, d], (sides[n], peer))

    def up_from(n, d):
        peer = behind(d)
        return remote(up_ref.at[peer, 1 - n], got[n].at[peer], up_send.at[n, d], up_recv.at[n, d], (sides[1 - n], peer))

    def down(n, d):
        peer = ahead(d)
        return remote(pick.at[n, peer], rows_ref.at[lon, n], dn_send.at[n, d], dn_recv.at[n, d], (lat, peer))

    def down_from(n, d):
        peer = behind(d)
        return remote(pick.at[n, peer], rows_ref.at[peer, n], dn_send.at[n, d], dn_recv.at[n, d], (lat, peer))

    def piece(p):
        return pl.ds(p * PART, PART)

    def by_z(p, d):
        z = lax.rem(place + d, 4)
        return remote(phys.at[z, :, piece(p)], mid[p].at[place], z_send.at[p, d], z_recv.at[p, d], (lat, 4 * row + z))

    def from_z(p, d):
        z = lax.rem(place + 4 - d, 4)
        return remote(phys.at[z, :, piece(p)], mid[p].at[z], z_send.at[p, d], z_recv.at[p, d], (lat, 4 * row + z))

    def by_y(p, d):
        y = lax.rem(row + d, 4)
        return remote(turn.at[y, :, piece(p)], phys_out.at[row, :, piece(p)], y_send.at[p, d], y_recv.at[p, d], (lat, 4 * y + place))

    def from_y(p, d):
        y = lax.rem(row + 4 - d, 4)
        return remote(turn.at[y, :, piece(p)], phys_out.at[y, :, piece(p)], y_send.at[p, d], y_recv.at[p, d], (lat, 4 * y + place))

    def at_home(n):
        return pltpu.make_async_copy(pick.at[n, lon], rows_ref.at[lon, n], home.at[n])

    def remain(p):
        return pltpu.make_async_copy(turn.at[row, :, piece(p)], phys_out.at[row, :, piece(p)], rest.at[p])

    def lift(n):
        for d in ORDER:
            up(n, d).start()

    def descend(n):
        for d in ORDER:
            up_from(n, d).wait_recv()

        def choose(o):
            value = got[n][tab[o, 2 * n]]
            pick[n, o] = jnp.where(tab[o, 2 * n + 1] > 0, value, 0.0)

        each(0, count, choose)
        keep = at_home(n)
        keep.start()
        for d in ORDER[1:]:
            down(n, d).start()

    def stay(p):
        return pltpu.make_async_copy(phys.at[place, :, piece(p)], mid[p].at[place], own.at[p])

    def send_z(p):
        for d in (2, 1, 3):
            by_z(p, d).start()
        stay(p).start()

    def send_y(p):
        for d in (1, 2, 3):
            from_z(p, d).wait_recv()
        stay(p).wait()

        def sort(q):
            turn[q // 2, lax.rem(q, 2), piece(p)] = mid[p][tab[q, 4] // 2, lax.rem(tab[q, 4], 2)]

        each(0, 8, sort)
        for d in (2, 1, 3):
            by_y(p, d).start()
        remain(p).start()

    if first:
        send_z(0)
        lift(0)
        send_z(1)
        lift(1)
        send_z(2)
        send_z(3)
        send_y(0)
        descend(0)
        send_y(1)
        descend(1)
        send_y(2)
        send_y(3)
    else:
        to_e = remote(e_ref, from_w, we_send.at[0], we_recv.at[0], (lat, lax.rem(lon + 1, count)))
        to_w = remote(w_ref, from_e, we_send.at[1], we_recv.at[1], (lat, lax.rem(lon + count - 1, count)))
        lift(0)
        lift(1)
        descend(0)
        to_e.start()
        to_w.start()
        descend(1)
    for n in range(2):
        at_home(n).wait()
        for d in ORDER[1:]:
            down_from(n, d).wait_recv()
    for n in range(2):
        for d in ORDER:
            up(n, d).wait_send()
        for d in ORDER[1:]:
            down(n, d).wait_send()
    if first:
        for p in range(PARTS):
            for d in (1, 2, 3):
                from_y(p, d).wait_recv()
                by_z(p, d).wait_send()
                by_y(p, d).wait_send()
            remain(p).wait()
    else:
        to_e.wait()
        to_w.wait()


def halo(first, tab, rows, *rest):
    anywhere = pl.BlockSpec(memory_space=pl.ANY)
    edge = jax.ShapeDtypeStruct((4, ROWS3, CELLS), jnp.float32)
    dma = pltpu.SemaphoreType.DMA
    sent = pltpu.VMEM((4, 2, PHYS, CELLS), jnp.float32)
    out = [jax.ShapeDtypeStruct((16, 2, HALF, 128), jnp.float32)]
    scratch = [VM((16, HALF, 128), jnp.float32), VM((16, HALF, 128), jnp.float32),
               VM((2, 16, HALF, 128), jnp.float32)]
    sems = [dma((2, 16)), dma((2, 16)), dma((2, 16)), dma((2, 16))]
    if first:
        in_specs, out_specs = [anywhere], [anywhere, anywhere]
        out.append(jax.ShapeDtypeStruct((4, 2, PHYS, CELLS), jnp.float32))
        scratch += [sent] + [VM((4, 2, PART, CELLS), jnp.float32)] * PARTS
        scratch += sems + [dma((PARTS, 4))] * 4 + [dma((PARTS,)), dma((PARTS,)), dma((2,))]
        rest = [rest[0].reshape(4, 2, PHYS, CELLS)]
    else:
        in_specs, out_specs = [anywhere] * 2, [anywhere] * 3
        out += [edge, edge]
        scratch += sems + [dma((2,)), dma((2,)), dma((2,))]
    rows, *more = pl.pallas_call(
        functools.partial(halo_kernel, first),
        in_specs=[pl.BlockSpec(memory_space=pltpu.SMEM), anywhere] + in_specs,
        out_specs=out_specs,
        out_shape=out,
        scratch_shapes=scratch,
        compiler_params=pltpu.CompilerParams(collective_id=1 if first else 2, has_side_effects=True),
        cost_estimate=pl.CostEstimate(flops=10**6, bytes_accessed=10**8, transcendentals=0),
        name="halo_phys" if first else "halo",
    )(tab, rows.reshape(16, 2, HALF, 128), *rest)
    return [rows.reshape(8, 2, 2, HALF, 128)] + more


def heat_kernel(tab, got, wet, light, out, fine):
    lane = lanes()
    group = lane // SIDE
    for r in range(SIDE):
        half = slice(128 * (r // 8), 128 * (r // 8) + 128)
        acc = jnp.zeros((LEV, 128), jnp.float32)
        for k in range(TILE):
            acc = jnp.where(group == k, roll(got[tab[k, 6], :, half], (16 * k - 16 * (r % 8)) % 128), acc)
        acc = jnp.where(wet[r:r + 1, :] > 0.0, acc, 0.0)
        for a in range(3):
            fine[pl.ds(3 * r + a, LEV, stride=LEV), :] = acc
    spread = spread_matrix((128, 384), False)
    stacked = jnp.concatenate([spread] * 3, axis=0)

    def levels(i, carry):
        x = fine[pl.ds(pl.multiple_of(i * 8 * LEV, 8 * LEV), 8 * LEV), :]
        high = x.astype(jnp.bfloat16)
        rest = x - high.astype(jnp.float32)
        mid = rest.astype(jnp.bfloat16)
        low = (rest - mid.astype(jnp.float32)).astype(jnp.bfloat16)
        wide = jnp.dot(jnp.concatenate([high, mid, low], axis=1), stacked,
                       preferred_element_type=jnp.float32)
        for l in range(8):
            out[8 * i + l] = (light[...] * wide[l * LEV:l * LEV + LEV]).astype(jnp.bfloat16)
        return carry

    lax.fori_loop(0, LEV // 8, levels, 0)


def heat(tab, got, wet, light):
    return pl.pallas_call(
        heat_kernel,
        in_specs=[pl.BlockSpec(memory_space=pltpu.SMEM)] + [pl.BlockSpec(memory_space=VM)] * 3,
        out_specs=pl.BlockSpec(memory_space=VM),
        out_shape=jax.ShapeDtypeStruct((LEV, 48, 384), jnp.bfloat16),
        scratch_shapes=[VM((LEV * LEV, 128), jnp.float32)],
        cost_estimate=pl.CostEstimate(flops=10**9, bytes_accessed=3 * 10**6, transcendentals=0),
        name="heat",
    )(tab, got, wet, light)


def prep_kernel(base, south, north, west, east, light, flags, tab, meet, sums):
    lat, lon = lax.axis_index("lat"), lax.axis_index("lon")
    wet = base[0:16, :]
    lane = lax.broadcasted_iota(jnp.int32, (SIDE, 128), 1)
    line = lax.broadcasted_iota(jnp.int32, (SIDE, 128), 0)
    wet_e = jnp.where(lane == 127, roll(east[0:16, :], 127), roll(wet, 127))
    wet_w = jnp.where(lane == 0, roll(west[0:16, :], 1), roll(wet, 1))
    inner_n = (lat < lax.axis_size("lat") - 1).astype(jnp.float32)
    inner_s = (lat > 0).astype(jnp.float32)
    wet_n = jnp.where(line == 15, inner_n * north[0:1, :], pltpu.roll(wet, 15, 0))
    wet_s = jnp.where(line == 0, inner_s * south[15:16, :], pltpu.roll(wet, 1, 0))
    sums[...] = jnp.dot(light[...], spread_matrix((384, 128), True, jnp.float32),
                        precision=lax.Precision.HIGHEST, preferred_element_type=jnp.float32)
    mean = sums[pl.ds(0, 16, stride=3), :] + sums[pl.ds(1, 16, stride=3), :] + sums[pl.ds(2, 16, stride=3), :]
    values = (wet * wet_w, wet * wet_e, wet * wet_s, wet * wet_n, mean / 9.0, wet,
              jnp.zeros_like(wet), jnp.zeros_like(wet))
    for i, v in enumerate(values):
        flags[pl.ds(i, 16, stride=8), :] = v

    def ints(ref):
        return ref[16:17, :].astype(jnp.int32)

    def owner_of(code):
        return lax.shift_right_arithmetic(code, 3) & 15

    def f32(x):
        return x.astype(jnp.float32)

    def wide(x, n):
        return jnp.broadcast_to(x, (n, 128))

    band = ints(base)
    big_i = lax.broadcasted_iota(jnp.int32, (128, 128), 0)
    big_j = lax.broadcasted_iota(jnp.int32, (128, 128), 1)
    down = jnp.sum(jnp.where(big_i == big_j, f32(wide(band, 128)), 0.0), axis=1, keepdims=True).astype(jnp.int32)
    down = jnp.broadcast_to(down, (128, 128))
    own_i, own_j = owner_of(down), owner_of(wide(band, 128))
    before = (big_i < big_j) & (down >= 0)
    near = jnp.sum(f32(before & (big_i // 8 == big_j // 8) & ((own_i & 3) == (own_j & 3))), axis=0, keepdims=True)
    far = jnp.sum(f32(before & (big_i // 32 == big_j // 32) & (own_i == own_j)), axis=0, keepdims=True)
    ids = lax.broadcasted_iota(jnp.int32, (1, 128), 1)
    own = owner_of(band)
    wet_b = band >= 0

    def total(mask, value):
        n = mask.shape[0]
        return jnp.sum(jnp.where(mask, wide(f32(value), n), 0.0), axis=1, keepdims=True)

    slot = lax.broadcasted_iota(jnp.int32, (8, 128), 0)
    ids8 = wide(ids, 8)
    band8 = wide(band, 8)
    hit = band8 == (lat * 16 + lon) * SLOTS + slot
    full = total(hit, jnp.ones_like(band))
    pair = total(hit, ids // 16)
    got_at = total(hit, ids // 32 * 2) + total(hit, far)
    west_code = total(hit, roll(band, 1))
    east_code = total(hit, roll(band, 127))

    def slot_of(code):
        code = code.astype(jnp.int32)
        return f32(jnp.where(code >= 0, code & 7, 0))

    w_slot, e_slot = slot_of(west_code), slot_of(east_code)
    some = jnp.broadcast_to(ids8 // 16 == slot, (8, 128))
    band_hit = wide(f32(jnp.max(f32(hit), axis=0, keepdims=True)), 8) > 0.0
    first_of = lax.broadcasted_iota(jnp.int32, (8, 1), 0).astype(jnp.float32)
    pair_used = total(some & band_hit, jnp.ones_like(band))
    pair_spare = jnp.min(jnp.where(pair_used > 0.0, 99.0, first_of), axis=0, keepdims=True)
    my_tile = ids // TILE == lon
    tile_mask = (ids8 // TILE == lon) & (ids8 - TILE * lon == slot)
    t_wet = total(tile_mask & (band8 >= 0), jnp.ones_like(band))
    t_own = total(tile_mask & (band8 >= 0), own)
    z_key = (own & 3) * 2 + near.astype(jnp.int32)
    z_at = total(tile_mask & (band8 >= 0), z_key)
    z_used = total(wide(my_tile & wet_b, 8) & (wide(z_key, 8) == slot), jnp.ones_like(band))
    z_spare = jnp.min(jnp.where(z_used > 0.0, 99.0, first_of), axis=0, keepdims=True)
    z_at = jnp.where(t_wet > 0.0, z_at, jnp.minimum(z_spare, 7.0))
    t_first = lax.broadcasted_iota(jnp.int32, (16, 1), 0).astype(jnp.float32)
    row16 = lax.broadcasted_iota(jnp.int32, (16, 128), 0)
    in_tile = wide(my_tile & wet_b, 16)
    to_me = jnp.max(f32(hit), axis=0, keepdims=True)
    src_used = total((wide(ids // TILE, 16) == row16) & (wide(to_me, 16) > 0.0), jnp.ones_like(band))
    src_spare = jnp.min(jnp.where(src_used > 0.0, 99.0, t_first), axis=0, keepdims=True)
    src = total(hit, ids // TILE)
    fields = (w_slot, e_slot, full, pair, jnp.where(full > 0.0, pair, jnp.minimum(pair_spare, 7.0)),
              jnp.where(full > 0.0, src, src_spare), t_own, z_at, got_at)
    acc = jnp.zeros((8, 128), jnp.float32)
    for i, v in enumerate(fields):
        acc = jnp.where(ids8 == i, v, acc)
    tab[...] = acc.astype(jnp.int32)
    ids16 = wide(ids, 16)
    here = (ids16 // 16 == lon // 2) & wide(wet_b, 16) & (wide(own, 16) == row16)
    acc = jnp.zeros((16, 128), jnp.float32)
    for i, other in enumerate((ints(south), ints(north))):
        both = here & (wide(other, 16) >= 0)
        acc = jnp.where(ids16 == 2 * i, total(both, owner_of(other)), acc)
        acc = jnp.where(ids16 == 2 * i + 1, total(both, jnp.ones_like(band)), acc)
    mine = wet_b & (ids // 32 == lon // 4) & ((own & 3) == lax.rem(lon, 4))
    y_key = lax.shift_right_arithmetic(own, 2) * 2 + far.astype(jnp.int32)
    turn = wide(mine, 16) & (wide(y_key, 16) == row16)
    acc = jnp.where(ids16 == 4, total(turn, (ids // 8 & 3) * 2 + near.astype(jnp.int32)), acc)
    meet[...] = acc.astype(jnp.int32)


def prep(base, south, north, west, east, light):
    flags, tab, meet = pl.pallas_call(
        prep_kernel,
        in_specs=[pl.BlockSpec(memory_space=VM)] * 6,
        out_specs=[pl.BlockSpec(memory_space=VM)] * 3,
        out_shape=[jax.ShapeDtypeStruct((128, 128), jnp.float32),
                   jax.ShapeDtypeStruct((8, 128), jnp.int32),
                   jax.ShapeDtypeStruct((16, 128), jnp.int32)],
        scratch_shapes=[VM((48, 128), jnp.float32)],
        cost_estimate=pl.CostEstimate(flops=10**7, bytes_accessed=10**5, transcendentals=0),
        name="prep",
    )(base, south, north, west, east, light)
    return flags.reshape(SIDE, 8, 128), tab, meet


def shift(x, axis, by):
    n = lax.axis_size(axis)
    return lax.ppermute(x, axis, [(i, (i + by) % n) for i in range(n)])


def swap(x):
    return lax.all_to_all(x, "lon", split_axis=0, concat_axis=0, tiled=True)


def on_device(tracers, phys_fine, mix_coarse, surf_light, land_mask, owner_map):
    wet = land_mask.astype(jnp.float32)
    base = jnp.concatenate([wet, owner_map.astype(jnp.float32)], axis=0)
    flags, tab, meet = prep(base, shift(base, "lat", 1), shift(base, "lat", -1),
                            shift(base, "lon", 1), shift(base, "lon", -1), surf_light)
    y, col = coarse(jnp.swapaxes(phys_fine, 1, 2), jnp.swapaxes(mix_coarse, 1, 2), flags)
    tab, y, col = lax.optimization_barrier((tab, y, col))
    west_col = shift(col, "lon", 1)
    south_row = shift(y[SIDE - 1, 48:96], "lat", 1)
    rows_out, w_out, e_out = pack(tab, tracers)
    came_west = shift(e_out, "lon", 1)
    came_east = shift(w_out, "lon", -1)
    y, rows_out = lax.optimization_barrier((y, rows_out))
    packed = package(tab, y, west_col, south_row)
    rows, phys = halo(True, meet, rows_out, packed)
    phys = phys.reshape(8, PHYS, CELLS)
    current, rows_out, w_out, e_out = step(False, tab, tracers, phys, rows, came_west, came_east)
    rows, came_west, came_east = halo(False, meet, rows_out, w_out, e_out)
    current, light_part = step(True, tab, current, phys, rows, came_west, came_east)
    return current, heat(tab, swap(light_part), wet, surf_light)


def solution(mesh):
    in_specs = (
        P(("lat", "lon"), None, None),
        P("lat", "lon", None),
        P("lat", "lon", None),
        P("lat", "lon"),
        P("lat", "lon"),
        P("lat", None),
    )
    out_specs = (P(("lat", "lon"), None, None), P(None, "lat", "lon"))
    return jax.shard_map(
        on_device, mesh=mesh, in_specs=in_specs, out_specs=out_specs, check_vma=False
    )
```

```python
import functools

import jax
import jax.numpy as jnp
from jax import lax
from jax.experimental import pallas as pl
from jax.experimental.pallas import tpu as pltpu
from jax.sharding import PartitionSpec as P

NTR = 24
LEV = 48
SIDE = 16
CELLS = 256
SLOTS = 8
TILE = 8
PHYS = 224
DIFF = 0.08
VM = pltpu.VMEM
ROWS3 = 3 * LEV
HALF = ROWS3 // 2


def pos(v):
    return jnp.maximum(v, 0.0)


def lanes():
    return lax.broadcasted_iota(jnp.int32, (LEV, 128), 1)


def roll(x, shift):
    return pltpu.roll(x, shift, 1)


def pack_edges(c_ref, rows_ref, w_ref, e_ref, odd):
    lane = lanes()
    group = lane // SIDE
    col = lane % SIDE
    low = lane < SIDE
    for m in range(3):
        blank = jnp.zeros((LEV, 128), jnp.float32)
        ends = [blank, blank]
        both = [blank, blank]
        for g in range(8):
            t = 3 * g + m
            a = c_ref[0, t * LEV:(t + 1) * LEV, 0:128]
            b = c_ref[0, t * LEV:(t + 1) * LEV, 128:256]
            end = jnp.where(low, a, b)
            ends[g % 2] = jnp.where((group == g) | (group == (g + 7) % 8), roll(end, 16 * g) if g else end, ends[g % 2])
            here = (col == 2 * g) | (col == (2 * g + 15) % 16)
            for h, v in enumerate((a, b)):
                both[h] = jnp.where(here, roll(v, 2 * g) if g else v, both[h])
        flat = group % 2 == 0
        put_rows(rows_ref, 0, m, jnp.where(flat, ends[0], ends[1]))
        put_rows(rows_ref, 1, m, jnp.where(flat, ends[1], ends[0]))
        at = slice(m * LEV, (m + 1) * LEV)
        mine = (lane % 2) == odd
        for h in range(2):
            hs = slice(h * 128, (h + 1) * 128)
            turned = roll(both[h], odd)
            w_ref[0, at, hs] = jnp.where(mine, turned, w_ref[0, at, hs])
            e_ref[0, at, hs] = jnp.where(mine, e_ref[0, at, hs], turned)


def put_rows(rows_ref, d, m, x):
    lo = m * LEV
    if lo < HALF:
        n = min(LEV, HALF - lo)
        rows_ref[0, 0, d, lo:lo + n, :] = x[:n]
        if n < LEV:
            rows_ref[0, 1, d, 0:LEV - n, :] = x[n:]
    else:
        rows_ref[0, 1, d, lo - HALF:lo - HALF + LEV, :] = x


def clear_first(odd, *refs):
    @pl.when(odd == 0)
    def _():
        for ref in refs:
            ref[...] = jnp.zeros_like(ref)


def pack_kernel(tab, c_ref, rows_ref, w_ref, e_ref):
    p = pl.program_id(0)
    lane = lanes()
    group = lane // SIDE
    col = lane % SIDE
    even = lane % 2 == 0
    low = lane < SIDE
    flat = group % 2 == 0
    for m in range(3):
        at = slice(m * LEV, (m + 1) * LEV)
        blank = jnp.zeros((LEV, 128), jnp.float32)
        both = [[blank, blank], [blank, blank]]
        for i in range(2):
            ends = [blank, blank]
            for g in range(8):
                t = 3 * g + m
                a = c_ref[i, t * LEV:(t + 1) * LEV, 0:128]
                b = c_ref[i, t * LEV:(t + 1) * LEV, 128:256]
                end = jnp.where(low, a, b)
                ends[g % 2] = jnp.where((group == g) | (group == (g + 7) % 8), roll(end, 16 * g) if g else end, ends[g % 2])
                here = (col == 2 * g) | (col == (2 * g + 15) % 16)
                for h, v in enumerate((a, b)):
                    both[i][h] = jnp.where(here, roll(v, 2 * g) if g else v, both[i][h])
            view = rows_ref.at[pl.ds(tab[2 * p + i, 4], 1)]
            put_rows(view, 0, m, jnp.where(flat, ends[0], ends[1]))
            put_rows(view, 1, m, jnp.where(flat, ends[1], ends[0]))
        for h in range(2):
            hs = slice(h * 128, (h + 1) * 128)
            other = roll(both[1][h], 1)
            w_ref[0, at, hs] = jnp.where(even, both[0][h], other)
            e_ref[0, at, hs] = jnp.where(even, other, both[0][h])


def pack(tab, tracers):
    return pl.pallas_call(
        pack_kernel,
        grid_spec=pltpu.PrefetchScalarGridSpec(
            num_scalar_prefetch=1,
            grid=(SLOTS // 2,),
            in_specs=[pl.BlockSpec((2, NTR * LEV, CELLS), lambda j, tab: (j, 0, 0))],
            out_specs=[
                pl.BlockSpec((8, 2, 2, HALF, 128), lambda j, tab: (0, 0, 0, 0, 0)),
                pl.BlockSpec((1, ROWS3, CELLS), lambda j, tab: (j, 0, 0)),
                pl.BlockSpec((1, ROWS3, CELLS), lambda j, tab: (j, 0, 0)),
            ],
        ),
        out_shape=[
            jax.ShapeDtypeStruct((8, 2, 2, HALF, 128), jnp.float32),
            jax.ShapeDtypeStruct((4, ROWS3, CELLS), jnp.float32),
            jax.ShapeDtypeStruct((4, ROWS3, CELLS), jnp.float32),
        ],
        cost_estimate=pl.CostEstimate(flops=10**7, bytes_accessed=12 * 10**6, transcendentals=0),
        name="pack",
    )(tab, tracers)


def react(get, put, par, warm):
    (carbon_dis, alkalinity, oxygen, nitrate, ammonium, phosphate, silicate, iron_free,
     nano_carbon, diat_carbon, nano_chl, diat_chl, nano_iron, diat_iron, diat_silica,
     micro_zoo, meso_zoo, dissolved_org, small_part, big_part, small_iron, big_iron,
     big_silica, calcite) = [functools.partial(get, t) for t in range(NTR)]
    p_am = pos(ammonium())
    nitrogen = pos(nitrate()) + p_am
    limit_nitro = nitrogen / (0.5 + nitrogen)
    p_ph = pos(phosphate())
    p_fe = pos(iron_free())
    p_si = pos(silicate())
    nutr_nano = jnp.minimum(jnp.minimum(limit_nitro, p_ph / (0.3 + p_ph)), p_fe / (0.2 + p_fe))
    nutr_diat = jnp.minimum(nutr_nano, p_si / (1.0 + p_si))
    nc = nano_carbon()
    dc = diat_carbon()
    wp = warm * par
    prod_nano = 0.1 * wp / (par + 0.5) * nutr_nano * nc
    prod_diat = 0.12 * wp / (par + 1.0) * nutr_diat * dc
    share = (p_am + 0.01) / (nitrogen + 0.02)
    mi = micro_zoo()
    me = meso_zoo()
    graze_nano = 0.08 * warm * mi / (1.0 + pos(nc))
    graze_diat = 0.06 * warm * me / (1.0 + pos(dc))
    loss_nano = graze_nano + 0.02
    loss_diat = graze_diat + 0.02
    eaten_nano = graze_nano * nc
    eaten_diat = graze_diat * dc
    death_micro = 0.03 * mi * pos(mi)
    death_meso = 0.03 * me * pos(me)
    do = dissolved_org()
    sp = small_part()
    bp = big_part()
    remin_doc = 0.03 * warm * do
    remin_poc = 0.02 * warm * sp
    remin_goc = 0.01 * warm * bp
    am = ammonium()
    nitrify = 0.05 * am
    cal = calcite()
    melt_cal = 0.01 * cal
    uptake = prod_nano + prod_diat
    remin = remin_doc + remin_poc + remin_goc
    calcify = 0.02 * prod_nano
    shell = melt_cal - calcify
    put(0, carbon_dis() + remin - uptake + shell)
    su = share * uptake
    fresh = uptake - su
    put(1, alkalinity() + 2.0 * shell + 0.16 * (fresh - nitrify))
    put(2, oxygen() + 1.3 * (uptake - remin) - 0.32 * nitrify)
    put(3, nitrate() + 0.16 * (nitrify - fresh))
    put(4, am + 0.16 * (remin - su - nitrify))
    put(5, phosphate() + 0.01 * (remin - uptake))
    bsi = big_silica()
    melt_si = 0.02 * bsi
    put(6, silicate() + melt_si - 0.15 * prod_diat)
    sfe = small_iron()
    bfe = big_iron()
    melt_sfe = 0.02 * sfe
    melt_bfe = 0.01 * bfe
    put(7, iron_free() + melt_sfe + melt_bfe - 0.005 * uptake)
    put(8, nc + prod_nano - loss_nano * nc)
    put(9, dc + prod_diat - loss_diat * dc)
    x = nano_chl()
    put(10, x + 0.03 * prod_nano - loss_nano * x)
    x = diat_chl()
    put(11, x + 0.03 * prod_diat - loss_diat * x)
    x = nano_iron()
    lost = loss_nano * x
    put(12, x + 0.005 * prod_nano - lost)
    put(20, sfe + lost - melt_sfe)
    x = diat_iron()
    lost = loss_diat * x
    put(13, x + 0.005 * prod_diat - lost)
    put(21, bfe + lost - melt_bfe)
    x = diat_silica()
    lost = loss_diat * x
    put(14, x + 0.15 * prod_diat - lost)
    put(22, bsi + lost - melt_si)
    put(15, mi + 0.3 * eaten_nano - death_micro)
    put(16, me + 0.3 * eaten_diat - death_meso)
    put(17, do + 0.3 * eaten_nano + 0.02 * nc - remin_doc)
    put(18, sp + 0.4 * eaten_nano + death_micro - remin_poc)
    put(19, bp + 0.4 * eaten_diat + 0.02 * dc + death_meso - remin_goc)
    put(23, cal - shell)


def tri():
    i = lax.broadcasted_iota(jnp.int32, (LEV, LEV), 0)
    j = lax.broadcasted_iota(jnp.int32, (LEV, LEV), 1)
    return (j < i).astype(jnp.float32)


def depth(absorb):
    return jnp.dot(tri(), absorb, precision=lax.Precision.HIGHEST,
                   preferred_element_type=jnp.float32)


def slot_step(tab, c_ref, phys, rows, west, east, out, coef, par_ref, cross, along, one, two):
    j = pl.program_id(0)
    w_odd = tab[j, 0] % 2
    e_odd = tab[j, 1] % 2
    lane = lanes()
    col = lane % SIDE
    at_w = col == 0
    at_e = col == SIDE - 1
    low = lane < 16
    high = lane >= 112
    H = (slice(0, 128), slice(128, 256))
    edge = jnp.concatenate([phys[0, 200:224, 0:128], phys[0, 200:224, 128:256]], axis=0)
    sel_r = lax.broadcasted_iota(jnp.int32, (128, 256), 0)
    sel_c = lax.broadcasted_iota(jnp.int32, (128, 256), 1)
    sel = ((sel_c == SIDE * sel_r) & (sel_r < SIDE)).astype(jnp.float32)
    edge_lane = jnp.where(low, edge, 0.0)
    edge_w = jnp.dot(edge_lane, sel, precision=lax.Precision.HIGHEST,
                     preferred_element_type=jnp.float32)
    edge_s = roll(edge, 112)
    fn_up = roll(phys[0, 48:96, H[0]], 16)
    level = lax.broadcasted_iota(jnp.int32, (LEV, 128), 0)
    for h in range(2):
        fe = phys[0, 0:48, H[h]]
        fn = phys[0, 48:96, H[h]]
        fw = jnp.where(at_w, edge_w[:, H[h]], roll(fe, 1))
        if h == 0:
            fs = jnp.where(low, edge_s, fn_up)
        else:
            fs = jnp.where(low, fn_up, roll(fn, 16))
        ow = DIFF * phys[0, 192:193, H[h]]
        oe = DIFF * phys[0, 193:194, H[h]]
        os = DIFF * phys[0, 194:195, H[h]]
        on = DIFF * phys[0, 195:196, H[h]]
        coef[0, :, H[h]] = (1.0 - (ow + oe + os + on)) - pos(fe) + jnp.minimum(fw, 0.0) - pos(fn) + jnp.minimum(fs, 0.0)
        coef[1, :, H[h]] = oe - jnp.minimum(fe, 0.0)
        coef[2, :, H[h]] = ow + pos(fw)
        coef[3, :, H[h]] = on - jnp.minimum(fn, 0.0)
        coef[4, :, H[h]] = os + pos(fs)
        below = jnp.where(level < LEV - 1, phys[0, 144:192, H[h]], 0.0)
        coef[5, :, H[h]] = below

    wide = lax.broadcasted_iota(jnp.int32, (HALF, 128), 1)
    flat = (wide // SIDE) % 2 == 0
    for p in range(2):
        hp = slice(p * HALF, (p + 1) * HALF)
        upper = rows[0, p, 1, :, :]
        under = roll(rows[0, p, 0, :, :], 32)
        cross[0, hp, :] = jnp.where(flat, upper, under)
        cross[1, hp, :] = jnp.where(flat, under, upper)
        for h in range(2):
            along[hp, H[h]] = jnp.where(wide % 2 == 0, roll(west[0, hp, H[h]], 128 - 15 - w_odd),
                                        roll(east[0, hp, H[h]], 15 - e_odd))

    def where(g, m):
        return pl.ds(pl.multiple_of((3 * g + m) * LEV, LEV), LEV)

    def turn_to(g, m, around):
        hm = slice(m * LEV, (m + 1) * LEV)
        a = c_ref[0, where(g, m), H[0]]
        b = c_ref[0, where(g, m), H[1]]
        ends = roll(cross[lax.rem(g, 2), hm, :], 112 - 16 * g)
        an, bn = roll(a, 112), roll(b, 112)
        as_, bs = roll(a, 16), roll(b, 16)
        around[m, 0, :, H[0]] = jnp.where(high, bn, an)
        around[m, 0, :, H[1]] = jnp.where(high, ends, bn)
        around[m, 1, :, H[0]] = jnp.where(low, ends, as_)
        around[m, 1, :, H[1]] = jnp.where(low, as_, bs)
        for h, v in enumerate((a, b)):
            sides = roll(along[hm, H[h]], lax.rem(128 - 2 * g, 128))
            around[m, 2, :, H[h]] = jnp.where(at_w, sides, roll(v, 1))
            around[m, 3, :, H[h]] = jnp.where(at_e, sides, roll(v, 127))

    def move(g, m, around):
        for h in range(2):
            v = c_ref[0, where(g, m), H[h]]
            moved = (coef[0, :, H[h]] * v + coef[1, :, H[h]] * around[m, 3, :, H[h]]
                     + coef[2, :, H[h]] * around[m, 2, :, H[h]]
                     + coef[3, :, H[h]] * around[m, 0, :, H[h]] + coef[4, :, H[h]] * around[m, 1, :, H[h]])
            flux = coef[5, :, H[h]] * (pltpu.roll(moved, LEV - 1, 0) - moved)
            out[0, where(g, m), H[h]] = moved + flux - pltpu.roll(flux, 1, 0)

    for m in range(3):
        turn_to(0, m, one)

    def pair(i, carry):
        for now, then, g in ((one, two, 2 * i), (two, one, 2 * i + 1)):
            for m in range(3):
                move(g, m, now)
                turn_to(jnp.minimum(g + 1, 7), m, then)
        return carry

    lax.fori_loop(0, 4, pair, 0)
    absorb = 0.04 + 0.02 * (pos(out[0, 480:528, :]) + pos(out[0, 528:576, :]))
    above = depth(absorb)
    par_ref[...] = phys[0, 196:197, :] * jnp.exp(-(above + 0.5 * absorb))
    for h in range(2):
        wet = jnp.broadcast_to(phys[0, 197:198, H[h]], (8, 128))

        def chunk(i, carry):
            l0 = pl.multiple_of(i * 8, 8)

            def get(t):
                return out[0, pl.ds(pl.multiple_of(t * LEV + l0, 8), 8), H[h]]

            held = [get(t) for t in range(NTR)]

            def put(t, v):
                out[0, pl.ds(pl.multiple_of(t * LEV + l0, 8), 8), H[h]] = v * wet

            warm = jnp.exp(0.0639 * phys[0, pl.ds(pl.multiple_of(96 + l0, 8), 8), H[h]])
            par = par_ref[pl.ds(l0, 8), H[h]]
            react(lambda t: held[t], put, par, warm)
            return carry

        lax.fori_loop(0, LEV // 8, chunk, 0)


def first_kernel(tab, c_ref, phys, rows, west, east, out, rows_out, w_out, e_out, coef, par_ref, cross, along, one, two):
    j = pl.program_id(0)
    odd = j % 2

    @pl.when(tab[j, 2] == 1)
    def _():
        slot_step(tab, c_ref, phys, rows, west, east, out, coef, par_ref, cross, along, one, two)

    @pl.when(tab[j, 2] == 0)
    def _():
        out[...] = jnp.zeros_like(out)

    clear_first(odd, w_out, e_out)
    pack_edges(out, rows_out, w_out, e_out, odd)


def last_kernel(tab, c_ref, phys, rows, west, east, out, light_out, coef, par_ref, cross, along, one, two):
    j = pl.program_id(0)

    @pl.when(tab[j, 2] == 1)
    def _():
        slot_step(tab, c_ref, phys, rows, west, east, out, coef, par_ref, cross, along, one, two)
        absorb = 0.04 + 0.02 * (pos(out[0, 480:528, :]) + pos(out[0, 528:576, :]))
        above = depth(absorb)
        light_out[0] = jnp.exp(-above) - jnp.exp(-(above + absorb))

    @pl.when(tab[j, 2] == 0)
    def _():
        out[...] = jnp.zeros_like(out)
        light_out[...] = jnp.zeros_like(light_out)


def step(last, tab, current, phys, rows, came_west, came_east):
    edge_spec = pl.BlockSpec((1, ROWS3, CELLS), lambda j, tab: (j // 2, 0, 0))
    edge_shape = jax.ShapeDtypeStruct((4, ROWS3, CELLS), jnp.float32)
    if last:
        outs = [pl.BlockSpec((1, LEV, CELLS), lambda j, tab: (tab[j, 5], 0, 0))]
        shapes = [jax.ShapeDtypeStruct((16, LEV, CELLS), jnp.float32)]
    else:
        outs = [pl.BlockSpec((1, 2, 2, HALF, 128), lambda j, tab: (tab[j, 4], 0, 0, 0, 0)), edge_spec, edge_spec]
        shapes = [jax.ShapeDtypeStruct((8, 2, 2, HALF, 128), jnp.float32), edge_shape, edge_shape]
    return pl.pallas_call(
        last_kernel if last else first_kernel,
        grid_spec=pltpu.PrefetchScalarGridSpec(
            num_scalar_prefetch=1,
            grid=(SLOTS,),
            in_specs=[
                pl.BlockSpec((1, NTR * LEV, CELLS), lambda j, tab: (j, 0, 0)),
                pl.BlockSpec((1, PHYS, CELLS), lambda j, tab: (tab[j, 8], 0, 0)),
                pl.BlockSpec((1, 2, 2, HALF, 128), lambda j, tab: (tab[j, 3], 0, 0, 0, 0)),
                pl.BlockSpec((1, ROWS3, CELLS), lambda j, tab: (tab[j, 0] // 2, 0, 0)),
                pl.BlockSpec((1, ROWS3, CELLS), lambda j, tab: (tab[j, 1] // 2, 0, 0)),
            ],
            out_specs=[pl.BlockSpec((1, NTR * LEV, CELLS), lambda j, tab: (j, 0, 0))] + outs,
            scratch_shapes=[VM((6, LEV, CELLS), jnp.float32), VM((LEV, CELLS), jnp.float32),
                            VM((2, ROWS3, 128), jnp.float32), VM((ROWS3, CELLS), jnp.float32),
                            VM((3, 4, LEV, CELLS), jnp.float32), VM((3, 4, LEV, CELLS), jnp.float32)],
        ),
        out_shape=[jax.ShapeDtypeStruct((SLOTS, NTR * LEV, CELLS), jnp.float32)] + shapes,
        cost_estimate=pl.CostEstimate(flops=10**8, bytes_accessed=25 * 10**6, transcendentals=10**6),
        name="last_step" if last else "first_step",
    )(tab, current, phys, rows, came_west, came_east)


def spread_matrix(shape, lhs_wide, dtype=jnp.bfloat16):
    i = lax.broadcasted_iota(jnp.int32, shape, 0)
    j = lax.broadcasted_iota(jnp.int32, shape, 1)
    return (i // 3 == j if lhs_wide else i == j // 3).astype(dtype)


def coarse_kernel(phys, mix, flags, y_ref, col_ref, every_ref, third_ref):
    step = pl.program_id(0)

    @pl.when(step == 0)
    def _():
        i = lax.broadcasted_iota(jnp.int32, (384, 128), 0)
        j = lax.broadcasted_iota(jnp.int32, (384, 128), 1)
        every_ref[...] = (i // 3 == j).astype(jnp.bfloat16)
        third_ref[...] = (i == 3 * j + 2).astype(jnp.bfloat16)
        col_ref[...] = jnp.zeros_like(col_ref)

    def dot(a, b):
        return jnp.dot(a, b, preferred_element_type=jnp.float32)

    u = jnp.concatenate([phys[f, 0:48, :] for f in range(6)], axis=0)
    vt = jnp.concatenate([phys[2, 48:96, :], phys[5, 48:96, :]] + [phys[f, 96:144, :] for f in range(6)], axis=0)
    east = dot(u, third_ref[...])
    rest = dot(vt, every_ref[...])

    def part(x, n):
        return x[48 * n:48 * n + 48]

    for c in range(2):
        e = (part(east, 3 * c) + part(east, 3 * c + 1) + part(east, 3 * c + 2)) / 3.0 * flags[c, 1:2, :]
        y_ref[c, 0:48, :] = e
        y_ref[c, 48:96, :] = part(rest, c) / 3.0 * flags[c, 3:4, :]
        y_ref[c, 96:144, :] = (part(rest, 3 * c + 2) + part(rest, 3 * c + 3) + part(rest, 3 * c + 4)) / 9.0
        y_ref[c, 144:192, :] = mix[c].astype(jnp.float32)
        y_ref[c, 192:200, :] = flags[c]
        r = 2 * step + c
        col_ref[...] = jnp.where(lanes() == r, roll(e, r + 1), col_ref[...])


def coarse(phys_t, mix_t, flags):
    return pl.pallas_call(
        coarse_kernel,
        grid=(SIDE // 2,),
        in_specs=[
            pl.BlockSpec((6, 144, 384), lambda r: (r, 0, 0)),
            pl.BlockSpec((2, LEV, 128), lambda r: (r, 0, 0)),
            pl.BlockSpec((2, 8, 128), lambda r: (r, 0, 0)),
        ],
        out_specs=[
            pl.BlockSpec((2, PHYS, 128), lambda r: (r, 0, 0)),
            pl.BlockSpec((LEV, 128), lambda r: (0, 0)),
        ],
        out_shape=[
            jax.ShapeDtypeStruct((SIDE, PHYS, 128), jnp.float32),
            jax.ShapeDtypeStruct((LEV, 128), jnp.float32),
        ],
        scratch_shapes=[VM((384, 128), jnp.bfloat16), VM((384, 128), jnp.bfloat16)],
        cost_estimate=pl.CostEstimate(flops=10**9, bytes_accessed=8 * 10**6, transcendentals=0),
        name="coarse",
    )(phys_t, mix_t, flags)


def package_kernel(tab, y_ref, col_ref, row_ref, out, faces):
    step = pl.program_id(0)
    group = lax.broadcasted_iota(jnp.int32, (8, 128), 1) // SIDE

    def chunk(i, carry):
        at = pl.ds(pl.multiple_of(8 * i, 8), 8)
        for h in range(2):
            hs = slice(128 * h, 128 * h + 128)
            vals = [y_ref[8 * h + g, at, :] for g in range(8)]
            for d in (1, 2, 4):
                lower = (group // d) % 2 == 0
                for g in range(8):
                    if g & d:
                        continue
                    a, b = vals[g], vals[g + d]
                    vals[g] = jnp.where(lower, a, roll(b, 16 * d))
                    vals[g + d] = jnp.where(lower, roll(a, 128 - 16 * d), b)
            for k in range(TILE):
                out[tab[k, 7], at, hs] = vals[k]

            @pl.when(step < 2)
            def _():
                for k in range(TILE):
                    faces[k, pl.ds(pl.multiple_of(32 * step + 8 * i, 8), 8), hs] = vals[k]
        return carry

    lax.fori_loop(0, jnp.where(step == 6, 1, 4), chunk, 0)

    @pl.when(step == 6)
    def _():
        i = lax.broadcasted_iota(jnp.int32, (256, 128), 0)
        j = lax.broadcasted_iota(jnp.int32, (256, 128), 1)
        last = (i == SIDE * j + SIDE - 1).astype(jnp.float32)
        low = lanes() < SIDE
        for k in range(TILE):
            if k:
                west = jnp.dot(faces[k - 1, 0:48, :], last, precision=lax.Precision.HIGHEST,
                               preferred_element_type=jnp.float32)
            else:
                west = col_ref[...]
            edge = jnp.where(low, west, roll(row_ref[...], (16 - 16 * k) % 128))
            out[tab[k, 7], 8:32, 0:128] = edge[0:24]
            out[tab[k, 7], 8:32, 128:256] = edge[24:48]


def package(tab, y, col, row):
    return pl.pallas_call(
        package_kernel,
        grid_spec=pltpu.PrefetchScalarGridSpec(
            num_scalar_prefetch=1,
            grid=(7,),
            in_specs=[
                pl.BlockSpec((SIDE, 32, 128), lambda i, tab: (0, i, 0)),
                pl.BlockSpec((LEV, 128), lambda i, tab: (0, 0)),
                pl.BlockSpec((LEV, 128), lambda i, tab: (0, 0)),
            ],
            out_specs=pl.BlockSpec((8, 32, CELLS), lambda i, tab: (0, i, 0)),
            scratch_shapes=[VM((TILE, 64, CELLS), jnp.float32)],
        ),
        out_shape=jax.ShapeDtypeStruct((8, PHYS, CELLS), jnp.float32),
        cost_estimate=pl.CostEstimate(flops=10**7, bytes_accessed=4 * 10**6, transcendentals=0),
        name="package",
    )(tab, y, col, row)


MESH = pl.DeviceIdType.MESH


def remote(src, dst, send, recv, where):
    return pltpu.make_async_remote_copy(src_ref=src, dst_ref=dst, send_sem=send, recv_sem=recv,
                                        device_id=where, device_id_type=MESH)


PARTS = 7
PART = PHYS // PARTS
ORDER = (0, 5, 10, 15, 4, 1, 8, 2, 12, 3, 6, 9, 7, 13, 11, 14)


def each(first, last, fn):
    def body(d, carry):
        fn(d)
        return carry

    lax.fori_loop(first, last, body, 0)


def halo_kernel(first, *refs):
    if first:
        tab, up_ref, phys, rows_ref, phys_out, got_s, got_n, pick, turn = refs[:9]
        mid = refs[9:9 + PARTS]
        (up_send, up_recv, dn_send, dn_recv, z_send, z_recv, y_send, y_recv, own, rest, home) = refs[9 + PARTS:]
    else:
        (tab, up_ref, w_ref, e_ref, rows_ref, from_w, from_e, got_s, got_n, pick,
         up_send, up_recv, dn_send, dn_recv, we_send, we_recv, home) = refs
    lat, lon = lax.axis_index("lat"), lax.axis_index("lon")
    bands, count = lax.axis_size("lat"), lax.axis_size("lon")
    sides = (lax.rem(lat + 1, bands), lax.rem(lat + bands - 1, bands))
    row, place = lon // 4, lax.rem(lon, 4)
    got = (got_s, got_n)
    barrier = pltpu.get_barrier_semaphore()

    def ahead(d):
        return lax.rem(row + d // 4, 4) * 4 + lax.rem(place + d % 4, 4)

    def behind(d):
        return lax.rem(row + 4 - d // 4, 4) * 4 + lax.rem(place + 4 - d % 4, 4)

    def greet(d):
        peer = lax.rem(lon + d, count)
        for side in sides:
            pl.semaphore_signal(barrier, inc=1, device_id=(side, peer), device_id_type=MESH)

    each(0, count, greet)
    each(1, count, lambda d: pl.semaphore_signal(
        barrier, inc=1, device_id=(lat, lax.rem(lon + d, count)), device_id_type=MESH))
    pl.semaphore_wait(barrier, 3 * count - 1)

    def up(n, d):
        peer = ahead(d)
        return remote(up_ref.at[peer, 1 - n], got[n].at[lon], up_send.at[n, d], up_recv.at[n, d], (sides[n], peer))

    def up_from(n, d):
        peer = behind(d)
        return remote(up_ref.at[peer, 1 - n], got[n].at[peer], up_send.at[n, d], up_recv.at[n, d], (sides[1 - n], peer))

    def down(n, d):
        peer = ahead(d)
        return remote(pick.at[n, peer], rows_ref.at[lon, n], dn_send.at[n, d], dn_recv.at[n, d], (lat, peer))

    def down_from(n, d):
        peer = behind(d)
        return remote(pick.at[n, peer], rows_ref.at[peer, n], dn_send.at[n, d], dn_recv.at[n, d], (lat, peer))

    def piece(p):
        return pl.ds(p * PART, PART)

    def by_z(p, d):
        z = lax.rem(place + d, 4)
        return remote(phys.at[z, :, piece(p)], mid[p].at[place], z_send.at[p, d], z_recv.at[p, d], (lat, 4 * row + z))

    def from_z(p, d):
        z = lax.rem(place + 4 - d, 4)
        return remote(phys.at[z, :, piece(p)], mid[p].at[z], z_send.at[p, d], z_recv.at[p, d], (lat, 4 * row + z))

    def by_y(p, d):
        y = lax.rem(row + d, 4)
        return remote(turn.at[y, :, piece(p)], phys_out.at[row, :, piece(p)], y_send.at[p, d], y_recv.at[p, d], (lat, 4 * y + place))

    def from_y(p, d):
        y = lax.rem(row + 4 - d, 4)
        return remote(turn.at[y, :, piece(p)], phys_out.at[y, :, piece(p)], y_send.at[p, d], y_recv.at[p, d], (lat, 4 * y + place))

    def at_home(n):
        return pltpu.make_async_copy(pick.at[n, lon], rows_ref.at[lon, n], home.at[n])

    def remain(p):
        return pltpu.make_async_copy(turn.at[row, :, piece(p)], phys_out.at[row, :, piece(p)], rest.at[p])

    def lift(n):
        for d in ORDER:
            up(n, d).start()

    def descend(n):
        for d in ORDER:
            up_from(n, d).wait_recv()

        def choose(o):
            value = got[n][tab[o, 2 * n]]
            pick[n, o] = jnp.where(tab[o, 2 * n + 1] > 0, value, 0.0)

        each(0, count, choose)
        keep = at_home(n)
        keep.start()
        for d in ORDER[1:]:
            down(n, d).start()

    def stay(p):
        return pltpu.make_async_copy(phys.at[place, :, piece(p)], mid[p].at[place], own.at[p])

    def send_z(p):
        for d in (2, 1, 3):
            by_z(p, d).start()
        stay(p).start()

    def send_y(p):
        for d in (1, 2, 3):
            from_z(p, d).wait_recv()
        stay(p).wait()

        def sort(q):
            turn[q // 2, lax.rem(q, 2), piece(p)] = mid[p][tab[q, 4] // 2, lax.rem(tab[q, 4], 2)]

        each(0, 8, sort)
        for d in (2, 1, 3):
            by_y(p, d).start()
        remain(p).start()

    if first:
        send_z(0)
        send_z(1)
        lift(0)
        send_z(2)
        send_z(3)
        lift(1)
        for p in range(4, PARTS):
            send_z(p)
        send_y(0)
        send_y(1)
        descend(0)
        send_y(2)
        send_y(3)
        descend(1)
        for p in range(4, PARTS):
            send_y(p)
    else:
        to_e = remote(e_ref, from_w, we_send.at[0], we_recv.at[0], (lat, lax.rem(lon + 1, count)))
        to_w = remote(w_ref, from_e, we_send.at[1], we_recv.at[1], (lat, lax.rem(lon + count - 1, count)))
        lift(0)
        lift(1)
        descend(0)
        to_e.start()
        to_w.start()
        descend(1)
    for n in range(2):
        at_home(n).wait()
        for d in ORDER[1:]:
            down_from(n, d).wait_recv()
    for n in range(2):
        for d in ORDER:
            up(n, d).wait_send()
        for d in ORDER[1:]:
            down(n, d).wait_send()
    if first:
        for p in range(PARTS):
            for d in (1, 2, 3):
                from_y(p, d).wait_recv()
                by_z(p, d).wait_send()
                by_y(p, d).wait_send()
            remain(p).wait()
    else:
        to_e.wait()
        to_w.wait()


def halo(first, tab, rows, *rest):
    anywhere = pl.BlockSpec(memory_space=pl.ANY)
    edge = jax.ShapeDtypeStruct((4, ROWS3, CELLS), jnp.float32)
    dma = pltpu.SemaphoreType.DMA
    sent = pltpu.VMEM((4, 2, PHYS, CELLS), jnp.float32)
    out = [jax.ShapeDtypeStruct((16, 2, HALF, 128), jnp.float32)]
    scratch = [VM((16, HALF, 128), jnp.float32), VM((16, HALF, 128), jnp.float32),
               VM((2, 16, HALF, 128), jnp.float32)]
    sems = [dma((2, 16)), dma((2, 16)), dma((2, 16)), dma((2, 16))]
    if first:
        in_specs, out_specs = [anywhere], [anywhere, anywhere]
        out.append(jax.ShapeDtypeStruct((4, 2, PHYS, CELLS), jnp.float32))
        scratch += [sent] + [VM((4, 2, PART, CELLS), jnp.float32)] * PARTS
        scratch += sems + [dma((PARTS, 4))] * 4 + [dma((PARTS,)), dma((PARTS,)), dma((2,))]
        rest = [rest[0].reshape(4, 2, PHYS, CELLS)]
    else:
        in_specs, out_specs = [anywhere] * 2, [anywhere] * 3
        out += [edge, edge]
        scratch += sems + [dma((2,)), dma((2,)), dma((2,))]
    rows, *more = pl.pallas_call(
        functools.partial(halo_kernel, first),
        in_specs=[pl.BlockSpec(memory_space=pltpu.SMEM), anywhere] + in_specs,
        out_specs=out_specs,
        out_shape=out,
        scratch_shapes=scratch,
        compiler_params=pltpu.CompilerParams(collective_id=1 if first else 2, has_side_effects=True),
        cost_estimate=pl.CostEstimate(flops=10**6, bytes_accessed=10**8, transcendentals=0),
        name="halo_phys" if first else "halo",
    )(tab, rows.reshape(16, 2, HALF, 128), *rest)
    return [rows.reshape(8, 2, 2, HALF, 128)] + more


def heat_kernel(tab, got, wet, light, out, fine):
    lane = lanes()
    group = lane // SIDE
    for r in range(SIDE):
        half = slice(128 * (r // 8), 128 * (r // 8) + 128)
        acc = jnp.zeros((LEV, 128), jnp.float32)
        for k in range(TILE):
            acc = jnp.where(group == k, roll(got[tab[k, 6], :, half], (16 * k - 16 * (r % 8)) % 128), acc)
        acc = jnp.where(wet[r:r + 1, :] > 0.0, acc, 0.0)
        for a in range(3):
            fine[pl.ds(3 * r + a, LEV, stride=LEV), :] = acc
    spread = spread_matrix((128, 384), False)
    stacked = jnp.concatenate([spread] * 3, axis=0)

    def levels(i, carry):
        x = fine[pl.ds(pl.multiple_of(i * 8 * LEV, 8 * LEV), 8 * LEV), :]
        high = x.astype(jnp.bfloat16)
        rest = x - high.astype(jnp.float32)
        mid = rest.astype(jnp.bfloat16)
        low = (rest - mid.astype(jnp.float32)).astype(jnp.bfloat16)
        wide = jnp.dot(jnp.concatenate([high, mid, low], axis=1), stacked,
                       preferred_element_type=jnp.float32)
        for l in range(8):
            out[8 * i + l] = (light[...] * wide[l * LEV:l * LEV + LEV]).astype(jnp.bfloat16)
        return carry

    lax.fori_loop(0, LEV // 8, levels, 0)


def heat(tab, got, wet, light):
    return pl.pallas_call(
        heat_kernel,
        in_specs=[pl.BlockSpec(memory_space=pltpu.SMEM)] + [pl.BlockSpec(memory_space=VM)] * 3,
        out_specs=pl.BlockSpec(memory_space=VM),
        out_shape=jax.ShapeDtypeStruct((LEV, 48, 384), jnp.bfloat16),
        scratch_shapes=[VM((LEV * LEV, 128), jnp.float32)],
        cost_estimate=pl.CostEstimate(flops=10**9, bytes_accessed=3 * 10**6, transcendentals=0),
        name="heat",
    )(tab, got, wet, light)


def prep_kernel(base, south, north, west, east, light, flags, tab, meet, sums):
    lat, lon = lax.axis_index("lat"), lax.axis_index("lon")
    wet = base[0:16, :]
    lane = lax.broadcasted_iota(jnp.int32, (SIDE, 128), 1)
    line = lax.broadcasted_iota(jnp.int32, (SIDE, 128), 0)
    wet_e = jnp.where(lane == 127, roll(east[0:16, :], 127), roll(wet, 127))
    wet_w = jnp.where(lane == 0, roll(west[0:16, :], 1), roll(wet, 1))
    inner_n = (lat < lax.axis_size("lat") - 1).astype(jnp.float32)
    inner_s = (lat > 0).astype(jnp.float32)
    wet_n = jnp.where(line == 15, inner_n * north[0:1, :], pltpu.roll(wet, 15, 0))
    wet_s = jnp.where(line == 0, inner_s * south[15:16, :], pltpu.roll(wet, 1, 0))
    sums[...] = jnp.dot(light[...], spread_matrix((384, 128), True, jnp.float32),
                        precision=lax.Precision.HIGHEST, preferred_element_type=jnp.float32)
    mean = sums[pl.ds(0, 16, stride=3), :] + sums[pl.ds(1, 16, stride=3), :] + sums[pl.ds(2, 16, stride=3), :]
    values = (wet * wet_w, wet * wet_e, wet * wet_s, wet * wet_n, mean / 9.0, wet,
              jnp.zeros_like(wet), jnp.zeros_like(wet))
    for i, v in enumerate(values):
        flags[pl.ds(i, 16, stride=8), :] = v

    def ints(ref):
        return ref[16:17, :].astype(jnp.int32)

    def owner_of(code):
        return lax.shift_right_arithmetic(code, 3) & 15

    def f32(x):
        return x.astype(jnp.float32)

    def wide(x, n):
        return jnp.broadcast_to(x, (n, 128))

    band = ints(base)
    big_i = lax.broadcasted_iota(jnp.int32, (128, 128), 0)
    big_j = lax.broadcasted_iota(jnp.int32, (128, 128), 1)
    down = jnp.sum(jnp.where(big_i == big_j, f32(wide(band, 128)), 0.0), axis=1, keepdims=True).astype(jnp.int32)
    down = jnp.broadcast_to(down, (128, 128))
    own_i, own_j = owner_of(down), owner_of(wide(band, 128))
    before = (big_i < big_j) & (down >= 0)
    near = jnp.sum(f32(before & (big_i // 8 == big_j // 8) & ((own_i & 3) == (own_j & 3))), axis=0, keepdims=True)
    far = jnp.sum(f32(before & (big_i // 32 == big_j // 32) & (own_i == own_j)), axis=0, keepdims=True)
    ids = lax.broadcasted_iota(jnp.int32, (1, 128), 1)
    own = owner_of(band)
    wet_b = band >= 0

    def total(mask, value):
        n = mask.shape[0]
        return jnp.sum(jnp.where(mask, wide(f32(value), n), 0.0), axis=1, keepdims=True)

    slot = lax.broadcasted_iota(jnp.int32, (8, 128), 0)
    ids8 = wide(ids, 8)
    band8 = wide(band, 8)
    hit = band8 == (lat * 16 + lon) * SLOTS + slot
    full = total(hit, jnp.ones_like(band))
    pair = total(hit, ids // 16)
    got_at = total(hit, ids // 32 * 2) + total(hit, far)
    west_code = total(hit, roll(band, 1))
    east_code = total(hit, roll(band, 127))

    def slot_of(code):
        code = code.astype(jnp.int32)
        return f32(jnp.where(code >= 0, code & 7, 0))

    w_slot, e_slot = slot_of(west_code), slot_of(east_code)
    some = jnp.broadcast_to(ids8 // 16 == slot, (8, 128))
    band_hit = wide(f32(jnp.max(f32(hit), axis=0, keepdims=True)), 8) > 0.0
    first_of = lax.broadcasted_iota(jnp.int32, (8, 1), 0).astype(jnp.float32)
    pair_used = total(some & band_hit, jnp.ones_like(band))
    pair_spare = jnp.min(jnp.where(pair_used > 0.0, 99.0, first_of), axis=0, keepdims=True)
    my_tile = ids // TILE == lon
    tile_mask = (ids8 // TILE == lon) & (ids8 - TILE * lon == slot)
    t_wet = total(tile_mask & (band8 >= 0), jnp.ones_like(band))
    t_own = total(tile_mask & (band8 >= 0), own)
    z_key = (own & 3) * 2 + near.astype(jnp.int32)
    z_at = total(tile_mask & (band8 >= 0), z_key)
    z_used = total(wide(my_tile & wet_b, 8) & (wide(z_key, 8) == slot), jnp.ones_like(band))
    z_spare = jnp.min(jnp.where(z_used > 0.0, 99.0, first_of), axis=0, keepdims=True)
    z_at = jnp.where(t_wet > 0.0, z_at, jnp.minimum(z_spare, 7.0))
    t_first = lax.broadcasted_iota(jnp.int32, (16, 1), 0).astype(jnp.float32)
    row16 = lax.broadcasted_iota(jnp.int32, (16, 128), 0)
    in_tile = wide(my_tile & wet_b, 16)
    to_me = jnp.max(f32(hit), axis=0, keepdims=True)
    src_used = total((wide(ids // TILE, 16) == row16) & (wide(to_me, 16) > 0.0), jnp.ones_like(band))
    src_spare = jnp.min(jnp.where(src_used > 0.0, 99.0, t_first), axis=0, keepdims=True)
    src = total(hit, ids // TILE)
    fields = (w_slot, e_slot, full, pair, jnp.where(full > 0.0, pair, jnp.minimum(pair_spare, 7.0)),
              jnp.where(full > 0.0, src, src_spare), t_own, z_at, got_at)
    acc = jnp.zeros((8, 128), jnp.float32)
    for i, v in enumerate(fields):
        acc = jnp.where(ids8 == i, v, acc)
    tab[...] = acc.astype(jnp.int32)
    ids16 = wide(ids, 16)
    here = (ids16 // 16 == lon // 2) & wide(wet_b, 16) & (wide(own, 16) == row16)
    acc = jnp.zeros((16, 128), jnp.float32)
    for i, other in enumerate((ints(south), ints(north))):
        both = here & (wide(other, 16) >= 0)
        acc = jnp.where(ids16 == 2 * i, total(both, owner_of(other)), acc)
        acc = jnp.where(ids16 == 2 * i + 1, total(both, jnp.ones_like(band)), acc)
    mine = wet_b & (ids // 32 == lon // 4) & ((own & 3) == lax.rem(lon, 4))
    y_key = lax.shift_right_arithmetic(own, 2) * 2 + far.astype(jnp.int32)
    turn = wide(mine, 16) & (wide(y_key, 16) == row16)
    acc = jnp.where(ids16 == 4, total(turn, (ids // 8 & 3) * 2 + near.astype(jnp.int32)), acc)
    meet[...] = acc.astype(jnp.int32)


def prep(base, south, north, west, east, light):
    flags, tab, meet = pl.pallas_call(
        prep_kernel,
        in_specs=[pl.BlockSpec(memory_space=VM)] * 6,
        out_specs=[pl.BlockSpec(memory_space=VM)] * 3,
        out_shape=[jax.ShapeDtypeStruct((128, 128), jnp.float32),
                   jax.ShapeDtypeStruct((8, 128), jnp.int32),
                   jax.ShapeDtypeStruct((16, 128), jnp.int32)],
        scratch_shapes=[VM((48, 128), jnp.float32)],
        cost_estimate=pl.CostEstimate(flops=10**7, bytes_accessed=10**5, transcendentals=0),
        name="prep",
    )(base, south, north, west, east, light)
    return flags.reshape(SIDE, 8, 128), tab, meet


def shift(x, axis, by):
    n = lax.axis_size(axis)
    return lax.ppermute(x, axis, [(i, (i + by) % n) for i in range(n)])


def swap(x):
    return lax.all_to_all(x, "lon", split_axis=0, concat_axis=0, tiled=True)


def on_device(tracers, phys_fine, mix_coarse, surf_light, land_mask, owner_map):
    wet = land_mask.astype(jnp.float32)
    base = jnp.concatenate([wet, owner_map.astype(jnp.float32)], axis=0)
    flags, tab, meet = prep(base, shift(base, "lat", 1), shift(base, "lat", -1),
                            shift(base, "lon", 1), shift(base, "lon", -1), surf_light)
    y, col = coarse(jnp.swapaxes(phys_fine, 1, 2), jnp.swapaxes(mix_coarse, 1, 2), flags)
    tab, y, col = lax.optimization_barrier((tab, y, col))
    west_col = shift(col, "lon", 1)
    south_row = shift(y[SIDE - 1, 48:96], "lat", 1)
    rows_out, w_out, e_out = pack(tab, tracers)
    came_west = shift(e_out, "lon", 1)
    came_east = shift(w_out, "lon", -1)
    y, rows_out = lax.optimization_barrier((y, rows_out))
    packed = package(tab, y, west_col, south_row)
    rows, phys = halo(True, meet, rows_out, packed)
    phys = phys.reshape(8, PHYS, CELLS)
    current, rows_out, w_out, e_out = step(False, tab, tracers, phys, rows, came_west, came_east)
    rows, came_west, came_east = halo(False, meet, rows_out, w_out, e_out)
    current, light_part = step(True, tab, current, phys, rows, came_west, came_east)
    return current, heat(tab, swap(light_part), wet, surf_light)


def solution(mesh):
    in_specs = (
        P(("lat", "lon"), None, None),
        P("lat", "lon", None),
        P("lat", "lon", None),
        P("lat", "lon"),
        P("lat", "lon"),
        P("lat", None),
    )
    out_specs = (P(("lat", "lon"), None, None), P(None, "lat", "lon"))
    return jax.shard_map(
        on_device, mesh=mesh, in_specs=in_specs, out_specs=out_specs, check_vma=False
    )
```

```python
import functools

import jax
import jax.numpy as jnp
from jax import lax
from jax.experimental import pallas as pl
from jax.experimental.pallas import tpu as pltpu
from jax.sharding import PartitionSpec as P

NTR = 24
LEV = 48
SIDE = 16
CELLS = 256
SLOTS = 8
TILE = 8
PHYS = 224
DIFF = 0.08
VM = pltpu.VMEM
ROWS3 = 3 * LEV
HALF = ROWS3 // 2


def pos(v):
    return jnp.maximum(v, 0.0)


def lanes():
    return lax.broadcasted_iota(jnp.int32, (LEV, 128), 1)


def roll(x, shift):
    return pltpu.roll(x, shift, 1)


def pack_edges(c_ref, rows_ref, w_ref, e_ref, odd):
    lane = lanes()
    group = lane // SIDE
    col = lane % SIDE
    low = lane < SIDE
    for m in range(3):
        blank = jnp.zeros((LEV, 128), jnp.float32)
        ends = [blank, blank]
        both = [blank, blank]
        for g in range(8):
            t = 3 * g + m
            a = c_ref[0, t * LEV:(t + 1) * LEV, 0:128]
            b = c_ref[0, t * LEV:(t + 1) * LEV, 128:256]
            end = jnp.where(low, a, b)
            ends[g % 2] = jnp.where((group == g) | (group == (g + 7) % 8), roll(end, 16 * g) if g else end, ends[g % 2])
            here = (col == 2 * g) | (col == (2 * g + 15) % 16)
            for h, v in enumerate((a, b)):
                both[h] = jnp.where(here, roll(v, 2 * g) if g else v, both[h])
        flat = group % 2 == 0
        put_rows(rows_ref, 0, m, jnp.where(flat, ends[0], ends[1]))
        put_rows(rows_ref, 1, m, jnp.where(flat, ends[1], ends[0]))
        at = slice(m * LEV, (m + 1) * LEV)
        mine = (lane % 2) == odd
        for h in range(2):
            hs = slice(h * 128, (h + 1) * 128)
            turned = roll(both[h], odd)
            w_ref[0, at, hs] = jnp.where(mine, turned, w_ref[0, at, hs])
            e_ref[0, at, hs] = jnp.where(mine, e_ref[0, at, hs], turned)


def put_rows(rows_ref, d, m, x):
    lo = m * LEV
    if lo < HALF:
        n = min(LEV, HALF - lo)
        rows_ref[0, 0, d, lo:lo + n, :] = x[:n]
        if n < LEV:
            rows_ref[0, 1, d, 0:LEV - n, :] = x[n:]
    else:
        rows_ref[0, 1, d, lo - HALF:lo - HALF + LEV, :] = x


def clear_first(odd, *refs):
    @pl.when(odd == 0)
    def _():
        for ref in refs:
            ref[...] = jnp.zeros_like(ref)


def pack_kernel(tab, c_ref, rows_ref, w_ref, e_ref):
    p = pl.program_id(0)
    lane = lanes()
    group = lane // SIDE
    col = lane % SIDE
    even = lane % 2 == 0
    low = lane < SIDE
    flat = group % 2 == 0
    for m in range(3):
        at = slice(m * LEV, (m + 1) * LEV)
        blank = jnp.zeros((LEV, 128), jnp.float32)
        both = [[blank, blank], [blank, blank]]
        for i in range(2):
            ends = [blank, blank]
            for g in range(8):
                t = 3 * g + m
                a = c_ref[i, t * LEV:(t + 1) * LEV, 0:128]
                b = c_ref[i, t * LEV:(t + 1) * LEV, 128:256]
                end = jnp.where(low, a, b)
                ends[g % 2] = jnp.where((group == g) | (group == (g + 7) % 8), roll(end, 16 * g) if g else end, ends[g % 2])
                here = (col == 2 * g) | (col == (2 * g + 15) % 16)
                for h, v in enumerate((a, b)):
                    both[i][h] = jnp.where(here, roll(v, 2 * g) if g else v, both[i][h])
            view = rows_ref.at[pl.ds(tab[2 * p + i, 4], 1)]
            put_rows(view, 0, m, jnp.where(flat, ends[0], ends[1]))
            put_rows(view, 1, m, jnp.where(flat, ends[1], ends[0]))
        for h in range(2):
            hs = slice(h * 128, (h + 1) * 128)
            other = roll(both[1][h], 1)
            w_ref[0, at, hs] = jnp.where(even, both[0][h], other)
            e_ref[0, at, hs] = jnp.where(even, other, both[0][h])


def pack(tab, tracers):
    return pl.pallas_call(
        pack_kernel,
        grid_spec=pltpu.PrefetchScalarGridSpec(
            num_scalar_prefetch=1,
            grid=(SLOTS // 2,),
            in_specs=[pl.BlockSpec((2, NTR * LEV, CELLS), lambda j, tab: (j, 0, 0))],
            out_specs=[
                pl.BlockSpec((8, 2, 2, HALF, 128), lambda j, tab: (0, 0, 0, 0, 0)),
                pl.BlockSpec((1, ROWS3, CELLS), lambda j, tab: (j, 0, 0)),
                pl.BlockSpec((1, ROWS3, CELLS), lambda j, tab: (j, 0, 0)),
            ],
        ),
        out_shape=[
            jax.ShapeDtypeStruct((8, 2, 2, HALF, 128), jnp.float32),
            jax.ShapeDtypeStruct((4, ROWS3, CELLS), jnp.float32),
            jax.ShapeDtypeStruct((4, ROWS3, CELLS), jnp.float32),
        ],
        cost_estimate=pl.CostEstimate(flops=10**7, bytes_accessed=12 * 10**6, transcendentals=0),
        name="pack",
    )(tab, tracers)


def react(get, put, par, warm):
    (carbon_dis, alkalinity, oxygen, nitrate, ammonium, phosphate, silicate, iron_free,
     nano_carbon, diat_carbon, nano_chl, diat_chl, nano_iron, diat_iron, diat_silica,
     micro_zoo, meso_zoo, dissolved_org, small_part, big_part, small_iron, big_iron,
     big_silica, calcite) = [functools.partial(get, t) for t in range(NTR)]
    p_am = pos(ammonium())
    nitrogen = pos(nitrate()) + p_am
    limit_nitro = nitrogen / (0.5 + nitrogen)
    p_ph = pos(phosphate())
    p_fe = pos(iron_free())
    p_si = pos(silicate())
    nutr_nano = jnp.minimum(jnp.minimum(limit_nitro, p_ph / (0.3 + p_ph)), p_fe / (0.2 + p_fe))
    nutr_diat = jnp.minimum(nutr_nano, p_si / (1.0 + p_si))
    nc = nano_carbon()
    dc = diat_carbon()
    wp = warm * par
    prod_nano = 0.1 * wp / (par + 0.5) * nutr_nano * nc
    prod_diat = 0.12 * wp / (par + 1.0) * nutr_diat * dc
    share = (p_am + 0.01) / (nitrogen + 0.02)
    mi = micro_zoo()
    me = meso_zoo()
    graze_nano = 0.08 * warm * mi / (1.0 + pos(nc))
    graze_diat = 0.06 * warm * me / (1.0 + pos(dc))
    loss_nano = graze_nano + 0.02
    loss_diat = graze_diat + 0.02
    eaten_nano = graze_nano * nc
    eaten_diat = graze_diat * dc
    death_micro = 0.03 * mi * pos(mi)
    death_meso = 0.03 * me * pos(me)
    do = dissolved_org()
    sp = small_part()
    bp = big_part()
    remin_doc = 0.03 * warm * do
    remin_poc = 0.02 * warm * sp
    remin_goc = 0.01 * warm * bp
    am = ammonium()
    nitrify = 0.05 * am
    cal = calcite()
    melt_cal = 0.01 * cal
    uptake = prod_nano + prod_diat
    remin = remin_doc + remin_poc + remin_goc
    calcify = 0.02 * prod_nano
    shell = melt_cal - calcify
    put(0, carbon_dis() + remin - uptake + shell)
    su = share * uptake
    fresh = uptake - su
    put(1, alkalinity() + 2.0 * shell + 0.16 * (fresh - nitrify))
    put(2, oxygen() + 1.3 * (uptake - remin) - 0.32 * nitrify)
    put(3, nitrate() + 0.16 * (nitrify - fresh))
    put(4, am + 0.16 * (remin - su - nitrify))
    put(5, phosphate() + 0.01 * (remin - uptake))
    bsi = big_silica()
    melt_si = 0.02 * bsi
    put(6, silicate() + melt_si - 0.15 * prod_diat)
    sfe = small_iron()
    bfe = big_iron()
    melt_sfe = 0.02 * sfe
    melt_bfe = 0.01 * bfe
    put(7, iron_free() + melt_sfe + melt_bfe - 0.005 * uptake)
    put(8, nc + prod_nano - loss_nano * nc)
    put(9, dc + prod_diat - loss_diat * dc)
    x = nano_chl()
    put(10, x + 0.03 * prod_nano - loss_nano * x)
    x = diat_chl()
    put(11, x + 0.03 * prod_diat - loss_diat * x)
    x = nano_iron()
    lost = loss_nano * x
    put(12, x + 0.005 * prod_nano - lost)
    put(20, sfe + lost - melt_sfe)
    x = diat_iron()
    lost = loss_diat * x
    put(13, x + 0.005 * prod_diat - lost)
    put(21, bfe + lost - melt_bfe)
    x = diat_silica()
    lost = loss_diat * x
    put(14, x + 0.15 * prod_diat - lost)
    put(22, bsi + lost - melt_si)
    put(15, mi + 0.3 * eaten_nano - death_micro)
    put(16, me + 0.3 * eaten_diat - death_meso)
    put(17, do + 0.3 * eaten_nano + 0.02 * nc - remin_doc)
    put(18, sp + 0.4 * eaten_nano + death_micro - remin_poc)
    put(19, bp + 0.4 * eaten_diat + 0.02 * dc + death_meso - remin_goc)
    put(23, cal - shell)


def tri():
    i = lax.broadcasted_iota(jnp.int32, (LEV, LEV), 0)
    j = lax.broadcasted_iota(jnp.int32, (LEV, LEV), 1)
    return (j < i).astype(jnp.float32)


def depth(absorb):
    return jnp.dot(tri(), absorb, precision=lax.Precision.HIGHEST,
                   preferred_element_type=jnp.float32)


def slot_step(tab, c_ref, phys, rows, west, east, out, coef, par_ref, cross, along, one, two):
    j = pl.program_id(0)
    w_odd = tab[j, 0] % 2
    e_odd = tab[j, 1] % 2
    lane = lanes()
    col = lane % SIDE
    at_w = col == 0
    at_e = col == SIDE - 1
    low = lane < 16
    high = lane >= 112
    H = (slice(0, 128), slice(128, 256))
    edge = jnp.concatenate([phys[0, 200:224, 0:128], phys[0, 200:224, 128:256]], axis=0)
    sel_r = lax.broadcasted_iota(jnp.int32, (128, 256), 0)
    sel_c = lax.broadcasted_iota(jnp.int32, (128, 256), 1)
    sel = ((sel_c == SIDE * sel_r) & (sel_r < SIDE)).astype(jnp.float32)
    edge_lane = jnp.where(low, edge, 0.0)
    edge_w = jnp.dot(edge_lane, sel, precision=lax.Precision.HIGHEST,
                     preferred_element_type=jnp.float32)
    edge_s = roll(edge, 112)
    fn_up = roll(phys[0, 48:96, H[0]], 16)
    level = lax.broadcasted_iota(jnp.int32, (LEV, 128), 0)
    for h in range(2):
        fe = phys[0, 0:48, H[h]]
        fn = phys[0, 48:96, H[h]]
        fw = jnp.where(at_w, edge_w[:, H[h]], roll(fe, 1))
        if h == 0:
            fs = jnp.where(low, edge_s, fn_up)
        else:
            fs = jnp.where(low, fn_up, roll(fn, 16))
        ow = DIFF * phys[0, 192:193, H[h]]
        oe = DIFF * phys[0, 193:194, H[h]]
        os = DIFF * phys[0, 194:195, H[h]]
        on = DIFF * phys[0, 195:196, H[h]]
        coef[0, :, H[h]] = (1.0 - (ow + oe + os + on)) - pos(fe) + jnp.minimum(fw, 0.0) - pos(fn) + jnp.minimum(fs, 0.0)
        coef[1, :, H[h]] = oe - jnp.minimum(fe, 0.0)
        coef[2, :, H[h]] = ow + pos(fw)
        coef[3, :, H[h]] = on - jnp.minimum(fn, 0.0)
        coef[4, :, H[h]] = os + pos(fs)
        below = jnp.where(level < LEV - 1, phys[0, 144:192, H[h]], 0.0)
        coef[5, :, H[h]] = below

    wide = lax.broadcasted_iota(jnp.int32, (HALF, 128), 1)
    flat = (wide // SIDE) % 2 == 0
    for p in range(2):
        hp = slice(p * HALF, (p + 1) * HALF)
        upper = rows[0, p, 1, :, :]
        under = roll(rows[0, p, 0, :, :], 32)
        cross[0, hp, :] = jnp.where(flat, upper, under)
        cross[1, hp, :] = jnp.where(flat, under, upper)
        for h in range(2):
            along[hp, H[h]] = jnp.where(wide % 2 == 0, roll(west[0, hp, H[h]], 128 - 15 - w_odd),
                                        roll(east[0, hp, H[h]], 15 - e_odd))

    def where(g, m):
        return pl.ds(pl.multiple_of((3 * g + m) * LEV, LEV), LEV)

    def turn_to(g, m, around):
        hm = slice(m * LEV, (m + 1) * LEV)
        a = c_ref[0, where(g, m), H[0]]
        b = c_ref[0, where(g, m), H[1]]
        ends = roll(cross[lax.rem(g, 2), hm, :], 112 - 16 * g)
        an, bn = roll(a, 112), roll(b, 112)
        as_, bs = roll(a, 16), roll(b, 16)
        around[m, 0, :, H[0]] = jnp.where(high, bn, an)
        around[m, 0, :, H[1]] = jnp.where(high, ends, bn)
        around[m, 1, :, H[0]] = jnp.where(low, ends, as_)
        around[m, 1, :, H[1]] = jnp.where(low, as_, bs)
        for h, v in enumerate((a, b)):
            sides = roll(along[hm, H[h]], lax.rem(128 - 2 * g, 128))
            around[m, 2, :, H[h]] = jnp.where(at_w, sides, roll(v, 1))
            around[m, 3, :, H[h]] = jnp.where(at_e, sides, roll(v, 127))

    def move(g, m, around):
        for h in range(2):
            v = c_ref[0, where(g, m), H[h]]
            moved = (coef[0, :, H[h]] * v + coef[1, :, H[h]] * around[m, 3, :, H[h]]
                     + coef[2, :, H[h]] * around[m, 2, :, H[h]]
                     + coef[3, :, H[h]] * around[m, 0, :, H[h]] + coef[4, :, H[h]] * around[m, 1, :, H[h]])
            flux = coef[5, :, H[h]] * (pltpu.roll(moved, LEV - 1, 0) - moved)
            out[0, where(g, m), H[h]] = moved + flux - pltpu.roll(flux, 1, 0)

    for m in range(3):
        turn_to(0, m, one)

    def pair(i, carry):
        for now, then, g in ((one, two, 2 * i), (two, one, 2 * i + 1)):
            for m in range(3):
                move(g, m, now)
                turn_to(jnp.minimum(g + 1, 7), m, then)
        return carry

    lax.fori_loop(0, 4, pair, 0)
    absorb = 0.04 + 0.02 * (pos(out[0, 480:528, :]) + pos(out[0, 528:576, :]))
    above = depth(absorb)
    par_ref[...] = phys[0, 196:197, :] * jnp.exp(-(above + 0.5 * absorb))
    for h in range(2):
        wet = jnp.broadcast_to(phys[0, 197:198, H[h]], (8, 128))

        def chunk(i, carry):
            l0 = pl.multiple_of(i * 8, 8)

            def get(t):
                return out[0, pl.ds(pl.multiple_of(t * LEV + l0, 8), 8), H[h]]

            held = [get(t) for t in range(NTR)]

            def put(t, v):
                out[0, pl.ds(pl.multiple_of(t * LEV + l0, 8), 8), H[h]] = v * wet

            warm = jnp.exp(0.0639 * phys[0, pl.ds(pl.multiple_of(96 + l0, 8), 8), H[h]])
            par = par_ref[pl.ds(l0, 8), H[h]]
            react(lambda t: held[t], put, par, warm)
            return carry

        lax.fori_loop(0, LEV // 8, chunk, 0)


def first_kernel(tab, c_ref, phys, rows, west, east, out, rows_out, w_out, e_out, coef, par_ref, cross, along, one, two):
    j = pl.program_id(0)
    odd = j % 2

    @pl.when(tab[j, 2] == 1)
    def _():
        slot_step(tab, c_ref, phys, rows, west, east, out, coef, par_ref, cross, along, one, two)

    @pl.when(tab[j, 2] == 0)
    def _():
        out[...] = jnp.zeros_like(out)

    clear_first(odd, w_out, e_out)
    pack_edges(out, rows_out, w_out, e_out, odd)


def last_kernel(tab, c_ref, phys, rows, west, east, out, light_out, coef, par_ref, cross, along, one, two):
    j = pl.program_id(0)

    @pl.when(tab[j, 2] == 1)
    def _():
        slot_step(tab, c_ref, phys, rows, west, east, out, coef, par_ref, cross, along, one, two)
        absorb = 0.04 + 0.02 * (pos(out[0, 480:528, :]) + pos(out[0, 528:576, :]))
        above = depth(absorb)
        light_out[0] = jnp.exp(-above) - jnp.exp(-(above + absorb))

    @pl.when(tab[j, 2] == 0)
    def _():
        out[...] = jnp.zeros_like(out)
        light_out[...] = jnp.zeros_like(light_out)


def step(last, tab, current, phys, rows, came_west, came_east):
    edge_spec = pl.BlockSpec((1, ROWS3, CELLS), lambda j, tab: (j // 2, 0, 0))
    edge_shape = jax.ShapeDtypeStruct((4, ROWS3, CELLS), jnp.float32)
    if last:
        outs = [pl.BlockSpec((1, LEV, CELLS), lambda j, tab: (tab[j, 5], 0, 0))]
        shapes = [jax.ShapeDtypeStruct((16, LEV, CELLS), jnp.float32)]
    else:
        outs = [pl.BlockSpec((1, 2, 2, HALF, 128), lambda j, tab: (tab[j, 4], 0, 0, 0, 0)), edge_spec, edge_spec]
        shapes = [jax.ShapeDtypeStruct((8, 2, 2, HALF, 128), jnp.float32), edge_shape, edge_shape]
    return pl.pallas_call(
        last_kernel if last else first_kernel,
        grid_spec=pltpu.PrefetchScalarGridSpec(
            num_scalar_prefetch=1,
            grid=(SLOTS,),
            in_specs=[
                pl.BlockSpec((1, NTR * LEV, CELLS), lambda j, tab: (j, 0, 0)),
                pl.BlockSpec((1, PHYS, CELLS), lambda j, tab: (tab[j, 8], 0, 0)),
                pl.BlockSpec((1, 2, 2, HALF, 128), lambda j, tab: (tab[j, 3], 0, 0, 0, 0)),
                pl.BlockSpec((1, ROWS3, CELLS), lambda j, tab: (tab[j, 0] // 2, 0, 0)),
                pl.BlockSpec((1, ROWS3, CELLS), lambda j, tab: (tab[j, 1] // 2, 0, 0)),
            ],
            out_specs=[pl.BlockSpec((1, NTR * LEV, CELLS), lambda j, tab: (j, 0, 0))] + outs,
            scratch_shapes=[VM((6, LEV, CELLS), jnp.float32), VM((LEV, CELLS), jnp.float32),
                            VM((2, ROWS3, 128), jnp.float32), VM((ROWS3, CELLS), jnp.float32),
                            VM((3, 4, LEV, CELLS), jnp.float32), VM((3, 4, LEV, CELLS), jnp.float32)],
        ),
        out_shape=[jax.ShapeDtypeStruct((SLOTS, NTR * LEV, CELLS), jnp.float32)] + shapes,
        cost_estimate=pl.CostEstimate(flops=10**8, bytes_accessed=25 * 10**6, transcendentals=10**6),
        name="last_step" if last else "first_step",
    )(tab, current, phys, rows, came_west, came_east)


def spread_matrix(shape, lhs_wide, dtype=jnp.bfloat16):
    i = lax.broadcasted_iota(jnp.int32, shape, 0)
    j = lax.broadcasted_iota(jnp.int32, shape, 1)
    return (i // 3 == j if lhs_wide else i == j // 3).astype(dtype)


def coarse_kernel(phys, mix, flags, y_ref, col_ref, every_ref, third_ref):
    step = pl.program_id(0)

    @pl.when(step == 0)
    def _():
        i = lax.broadcasted_iota(jnp.int32, (384, 128), 0)
        j = lax.broadcasted_iota(jnp.int32, (384, 128), 1)
        every_ref[...] = (i // 3 == j).astype(jnp.bfloat16)
        third_ref[...] = (i == 3 * j + 2).astype(jnp.bfloat16)
        col_ref[...] = jnp.zeros_like(col_ref)

    def dot(a, b):
        return jnp.dot(a, b, preferred_element_type=jnp.float32)

    u = jnp.concatenate([phys[f, 0:48, :] for f in range(6)], axis=0)
    vt = jnp.concatenate([phys[2, 48:96, :], phys[5, 48:96, :]] + [phys[f, 96:144, :] for f in range(6)], axis=0)
    east = dot(u, third_ref[...])
    rest = dot(vt, every_ref[...])

    def part(x, n):
        return x[48 * n:48 * n + 48]

    for c in range(2):
        e = (part(east, 3 * c) + part(east, 3 * c + 1) + part(east, 3 * c + 2)) / 3.0 * flags[c, 1:2, :]
        y_ref[c, 0:48, :] = e
        y_ref[c, 48:96, :] = part(rest, c) / 3.0 * flags[c, 3:4, :]
        y_ref[c, 96:144, :] = (part(rest, 3 * c + 2) + part(rest, 3 * c + 3) + part(rest, 3 * c + 4)) / 9.0
        y_ref[c, 144:192, :] = mix[c].astype(jnp.float32)
        y_ref[c, 192:200, :] = flags[c]
        r = 2 * step + c
        col_ref[...] = jnp.where(lanes() == r, roll(e, r + 1), col_ref[...])


def coarse(phys_t, mix_t, flags):
    return pl.pallas_call(
        coarse_kernel,
        grid=(SIDE // 2,),
        in_specs=[
            pl.BlockSpec((6, 144, 384), lambda r: (r, 0, 0)),
            pl.BlockSpec((2, LEV, 128), lambda r: (r, 0, 0)),
            pl.BlockSpec((2, 8, 128), lambda r: (r, 0, 0)),
        ],
        out_specs=[
            pl.BlockSpec((2, 200, 128), lambda r: (r, 0, 0)),
            pl.BlockSpec((LEV, 128), lambda r: (0, 0)),
        ],
        out_shape=[
            jax.ShapeDtypeStruct((SIDE, 200, 128), jnp.float32),
            jax.ShapeDtypeStruct((LEV, 128), jnp.float32),
        ],
        scratch_shapes=[VM((384, 128), jnp.bfloat16), VM((384, 128), jnp.bfloat16)],
        cost_estimate=pl.CostEstimate(flops=10**9, bytes_accessed=8 * 10**6, transcendentals=0),
        name="coarse",
    )(phys_t, mix_t, flags)


def package_kernel(tab, y_ref, col_ref, row_ref, out):
    group = lax.broadcasted_iota(jnp.int32, (8, 128), 1) // SIDE
    places = [tab[k, 7] for k in range(TILE)]

    def chunk(i, carry):
        at = pl.ds(pl.multiple_of(8 * i, 8), 8)
        for h in range(2):
            vals = [y_ref[8 * h + g, at, :] for g in range(8)]
            for d in (1, 2, 4):
                lower = (group // d) % 2 == 0
                for g in range(8):
                    if g & d:
                        continue
                    a, b = vals[g], vals[g + d]
                    vals[g] = jnp.where(lower, a, roll(b, 16 * d))
                    vals[g + d] = jnp.where(lower, roll(a, 128 - 16 * d), b)
            for k in range(TILE):
                out[places[k], at, 128 * h:128 * h + 128] = vals[k]
        return carry

    def chunks(i, carry):
        for c in range(5):
            chunk(5 * i + c, carry)
        return carry

    lax.fori_loop(0, 5, chunks, 0)
    i = lax.broadcasted_iota(jnp.int32, (256, 128), 0)
    j = lax.broadcasted_iota(jnp.int32, (256, 128), 1)
    last = (i == SIDE * j + SIDE - 1).astype(jnp.float32)
    low = lanes() < SIDE
    for k in range(TILE):
        if k:
            west = jnp.dot(out[tab[k - 1, 7], 0:48, :], last, precision=lax.Precision.HIGHEST,
                           preferred_element_type=jnp.float32)
        else:
            west = col_ref[...]
        edge = jnp.where(low, west, roll(row_ref[...], (16 - 16 * k) % 128))
        out[tab[k, 7], 200:224, 0:128] = edge[0:24]
        out[tab[k, 7], 200:224, 128:256] = edge[24:48]


def package(tab, y, col, row):
    return pl.pallas_call(
        package_kernel,
        in_specs=[pl.BlockSpec(memory_space=pltpu.SMEM)] + [pl.BlockSpec(memory_space=VM)] * 3,
        out_specs=pl.BlockSpec(memory_space=VM),
        out_shape=jax.ShapeDtypeStruct((8, PHYS, CELLS), jnp.float32),
        cost_estimate=pl.CostEstimate(flops=10**7, bytes_accessed=4 * 10**6, transcendentals=0),
        name="package",
    )(tab, y, col, row)


MESH = pl.DeviceIdType.MESH


def remote(src, dst, send, recv, where):
    return pltpu.make_async_remote_copy(src_ref=src, dst_ref=dst, send_sem=send, recv_sem=recv,
                                        device_id=where, device_id_type=MESH)


PARTS = 7
PART = PHYS // PARTS
ORDER = (0, 5, 10, 15, 4, 1, 8, 2, 12, 3, 6, 9, 7, 13, 11, 14)


def each(first, last, fn):
    def body(d, carry):
        fn(d)
        return carry

    lax.fori_loop(first, last, body, 0)


def halo_kernel(first, *refs):
    if first:
        tab, up_ref, phys, rows_ref, phys_out, got_s, got_n, pick, turn = refs[:9]
        mid = refs[9:9 + PARTS]
        (up_send, up_recv, dn_send, dn_recv, z_send, z_recv, y_send, y_recv, own, rest, home) = refs[9 + PARTS:]
    else:
        (tab, up_ref, w_ref, e_ref, rows_ref, from_w, from_e, got_s, got_n, pick,
         up_send, up_recv, dn_send, dn_recv, we_send, we_recv, home) = refs
    lat, lon = lax.axis_index("lat"), lax.axis_index("lon")
    bands, count = lax.axis_size("lat"), lax.axis_size("lon")
    sides = (lax.rem(lat + 1, bands), lax.rem(lat + bands - 1, bands))
    row, place = lon // 4, lax.rem(lon, 4)
    got = (got_s, got_n)
    barrier = pltpu.get_barrier_semaphore()

    def ahead(d):
        return lax.rem(row + d // 4, 4) * 4 + lax.rem(place + d % 4, 4)

    def behind(d):
        return lax.rem(row + 4 - d // 4, 4) * 4 + lax.rem(place + 4 - d % 4, 4)

    def greet(d):
        peer = lax.rem(lon + d, count)
        for side in sides:
            pl.semaphore_signal(barrier, inc=1, device_id=(side, peer), device_id_type=MESH)

    each(0, count, greet)
    each(1, count, lambda d: pl.semaphore_signal(
        barrier, inc=1, device_id=(lat, lax.rem(lon + d, count)), device_id_type=MESH))
    pl.semaphore_wait(barrier, 3 * count - 1)

    def up(n, d):
        peer = ahead(d)
        return remote(up_ref.at[peer, 1 - n], got[n].at[lon], up_send.at[n, d], up_recv.at[n, d], (sides[n], peer))

    def up_from(n, d):
        peer = behind(d)
        return remote(up_ref.at[peer, 1 - n], got[n].at[peer], up_send.at[n, d], up_recv.at[n, d], (sides[1 - n], peer))

    def down(n, d):
        peer = ahead(d)
        return remote(pick.at[n, peer], rows_ref.at[lon, n], dn_send.at[n, d], dn_recv.at[n, d], (lat, peer))

    def down_from(n, d):
        peer = behind(d)
        return remote(pick.at[n, peer], rows_ref.at[peer, n], dn_send.at[n, d], dn_recv.at[n, d], (lat, peer))

    def piece(p):
        return pl.ds(p * PART, PART)

    def by_z(p, d):
        z = lax.rem(place + d, 4)
        return remote(phys.at[z, :, piece(p)], mid[p].at[place], z_send.at[p, d], z_recv.at[p, d], (lat, 4 * row + z))

    def from_z(p, d):
        z = lax.rem(place + 4 - d, 4)
        return remote(phys.at[z, :, piece(p)], mid[p].at[z], z_send.at[p, d], z_recv.at[p, d], (lat, 4 * row + z))

    def by_y(p, d):
        y = lax.rem(row + d, 4)
        return remote(turn.at[y, :, piece(p)], phys_out.at[row, :, piece(p)], y_send.at[p, d], y_recv.at[p, d], (lat, 4 * y + place))

    def from_y(p, d):
        y = lax.rem(row + 4 - d, 4)
        return remote(turn.at[y, :, piece(p)], phys_out.at[y, :, piece(p)], y_send.at[p, d], y_recv.at[p, d], (lat, 4 * y + place))

    def at_home(n):
        return pltpu.make_async_copy(pick.at[n, lon], rows_ref.at[lon, n], home.at[n])

    def remain(p):
        return pltpu.make_async_copy(turn.at[row, :, piece(p)], phys_out.at[row, :, piece(p)], rest.at[p])

    def lift(n):
        for d in ORDER:
            up(n, d).start()

    def descend(n):
        for d in ORDER:
            up_from(n, d).wait_recv()

        def choose(o):
            value = got[n][tab[o, 2 * n]]
            pick[n, o] = jnp.where(tab[o, 2 * n + 1] > 0, value, 0.0)

        each(0, count, choose)
        keep = at_home(n)
        keep.start()
        for d in ORDER[1:]:
            down(n, d).start()

    def stay(p):
        return pltpu.make_async_copy(phys.at[place, :, piece(p)], mid[p].at[place], own.at[p])

    def send_z(p):
        for d in (2, 1, 3):
            by_z(p, d).start()
        stay(p).start()

    def send_y(p):
        for d in (1, 2, 3):
            from_z(p, d).wait_recv()
        stay(p).wait()

        def sort(q):
            turn[q // 2, lax.rem(q, 2), piece(p)] = mid[p][tab[q, 4] // 2, lax.rem(tab[q, 4], 2)]

        each(0, 8, sort)
        for d in (2, 1, 3):
            by_y(p, d).start()
        remain(p).start()

    if first:
        send_z(0)
        send_z(1)
        lift(0)
        send_z(2)
        send_z(3)
        lift(1)
        for p in range(4, PARTS):
            send_z(p)
        send_y(0)
        send_y(1)
        descend(0)
        send_y(2)
        send_y(3)
        descend(1)
        for p in range(4, PARTS):
            send_y(p)
    else:
        to_e = remote(e_ref, from_w, we_send.at[0], we_recv.at[0], (lat, lax.rem(lon + 1, count)))
        to_w = remote(w_ref, from_e, we_send.at[1], we_recv.at[1], (lat, lax.rem(lon + count - 1, count)))
        lift(0)
        lift(1)
        descend(0)
        to_e.start()
        to_w.start()
        descend(1)
    for n in range(2):
        at_home(n).wait()
        for d in ORDER[1:]:
            down_from(n, d).wait_recv()
    for n in range(2):
        for d in ORDER:
            up(n, d).wait_send()
        for d in ORDER[1:]:
            down(n, d).wait_send()
    if first:
        for p in range(PARTS):
            for d in (1, 2, 3):
                from_y(p, d).wait_recv()
                by_z(p, d).wait_send()
                by_y(p, d).wait_send()
            remain(p).wait()
    else:
        to_e.wait()
        to_w.wait()


def halo(first, tab, rows, *rest):
    anywhere = pl.BlockSpec(memory_space=pl.ANY)
    edge = jax.ShapeDtypeStruct((4, ROWS3, CELLS), jnp.float32)
    dma = pltpu.SemaphoreType.DMA
    sent = pltpu.VMEM((4, 2, PHYS, CELLS), jnp.float32)
    out = [jax.ShapeDtypeStruct((16, 2, HALF, 128), jnp.float32)]
    scratch = [VM((16, HALF, 128), jnp.float32), VM((16, HALF, 128), jnp.float32),
               VM((2, 16, HALF, 128), jnp.float32)]
    sems = [dma((2, 16)), dma((2, 16)), dma((2, 16)), dma((2, 16))]
    if first:
        in_specs, out_specs = [anywhere], [anywhere, anywhere]
        out.append(jax.ShapeDtypeStruct((4, 2, PHYS, CELLS), jnp.float32))
        scratch += [sent] + [VM((4, 2, PART, CELLS), jnp.float32)] * PARTS
        scratch += sems + [dma((PARTS, 4))] * 4 + [dma((PARTS,)), dma((PARTS,)), dma((2,))]
        rest = [rest[0].reshape(4, 2, PHYS, CELLS)]
    else:
        in_specs, out_specs = [anywhere] * 2, [anywhere] * 3
        out += [edge, edge]
        scratch += sems + [dma((2,)), dma((2,)), dma((2,))]
    rows, *more = pl.pallas_call(
        functools.partial(halo_kernel, first),
        in_specs=[pl.BlockSpec(memory_space=pltpu.SMEM), anywhere] + in_specs,
        out_specs=out_specs,
        out_shape=out,
        scratch_shapes=scratch,
        compiler_params=pltpu.CompilerParams(collective_id=1 if first else 2, has_side_effects=True),
        cost_estimate=pl.CostEstimate(flops=10**6, bytes_accessed=10**8, transcendentals=0),
        name="halo_phys" if first else "halo",
    )(tab, rows.reshape(16, 2, HALF, 128), *rest)
    return [rows.reshape(8, 2, 2, HALF, 128)] + more


def heat_kernel(tab, got, wet, light, out, fine):
    lane = lanes()
    group = lane // SIDE
    for r in range(SIDE):
        half = slice(128 * (r // 8), 128 * (r // 8) + 128)
        acc = jnp.zeros((LEV, 128), jnp.float32)
        for k in range(TILE):
            acc = jnp.where(group == k, roll(got[tab[k, 6], :, half], (16 * k - 16 * (r % 8)) % 128), acc)
        acc = jnp.where(wet[r:r + 1, :] > 0.0, acc, 0.0)
        for a in range(3):
            fine[pl.ds(3 * r + a, LEV, stride=LEV), :] = acc
    spread = spread_matrix((128, 384), False)
    stacked = jnp.concatenate([spread] * 3, axis=0)

    def levels(i, carry):
        x = fine[pl.ds(pl.multiple_of(i * 8 * LEV, 8 * LEV), 8 * LEV), :]
        high = x.astype(jnp.bfloat16)
        rest = x - high.astype(jnp.float32)
        mid = rest.astype(jnp.bfloat16)
        low = (rest - mid.astype(jnp.float32)).astype(jnp.bfloat16)
        wide = jnp.dot(jnp.concatenate([high, mid, low], axis=1), stacked,
                       preferred_element_type=jnp.float32)
        for l in range(8):
            out[8 * i + l] = (light[...] * wide[l * LEV:l * LEV + LEV]).astype(jnp.bfloat16)
        return carry

    lax.fori_loop(0, LEV // 8, levels, 0)


def heat(tab, got, wet, light):
    return pl.pallas_call(
        heat_kernel,
        in_specs=[pl.BlockSpec(memory_space=pltpu.SMEM)] + [pl.BlockSpec(memory_space=VM)] * 3,
        out_specs=pl.BlockSpec(memory_space=VM),
        out_shape=jax.ShapeDtypeStruct((LEV, 48, 384), jnp.bfloat16),
        scratch_shapes=[VM((LEV * LEV, 128), jnp.float32)],
        cost_estimate=pl.CostEstimate(flops=10**9, bytes_accessed=3 * 10**6, transcendentals=0),
        name="heat",
    )(tab, got, wet, light)


def prep_kernel(base, south, north, west, east, light, flags, tab, meet, sums):
    lat, lon = lax.axis_index("lat"), lax.axis_index("lon")
    wet = base[0:16, :]
    lane = lax.broadcasted_iota(jnp.int32, (SIDE, 128), 1)
    line = lax.broadcasted_iota(jnp.int32, (SIDE, 128), 0)
    wet_e = jnp.where(lane == 127, roll(east[0:16, :], 127), roll(wet, 127))
    wet_w = jnp.where(lane == 0, roll(west[0:16, :], 1), roll(wet, 1))
    inner_n = (lat < lax.axis_size("lat") - 1).astype(jnp.float32)
    inner_s = (lat > 0).astype(jnp.float32)
    wet_n = jnp.where(line == 15, inner_n * north[0:1, :], pltpu.roll(wet, 15, 0))
    wet_s = jnp.where(line == 0, inner_s * south[15:16, :], pltpu.roll(wet, 1, 0))
    sums[...] = jnp.dot(light[...], spread_matrix((384, 128), True, jnp.float32),
                        precision=lax.Precision.HIGHEST, preferred_element_type=jnp.float32)
    mean = sums[pl.ds(0, 16, stride=3), :] + sums[pl.ds(1, 16, stride=3), :] + sums[pl.ds(2, 16, stride=3), :]
    values = (wet * wet_w, wet * wet_e, wet * wet_s, wet * wet_n, mean / 9.0, wet,
              jnp.zeros_like(wet), jnp.zeros_like(wet))
    for i, v in enumerate(values):
        flags[pl.ds(i, 16, stride=8), :] = v

    def ints(ref):
        return ref[16:17, :].astype(jnp.int32)

    def owner_of(code):
        return lax.shift_right_arithmetic(code, 3) & 15

    def f32(x):
        return x.astype(jnp.float32)

    def wide(x, n):
        return jnp.broadcast_to(x, (n, 128))

    band = ints(base)
    big_i = lax.broadcasted_iota(jnp.int32, (128, 128), 0)
    big_j = lax.broadcasted_iota(jnp.int32, (128, 128), 1)
    down = jnp.sum(jnp.where(big_i == big_j, f32(wide(band, 128)), 0.0), axis=1, keepdims=True).astype(jnp.int32)
    down = jnp.broadcast_to(down, (128, 128))
    own_i, own_j = owner_of(down), owner_of(wide(band, 128))
    before = (big_i < big_j) & (down >= 0)
    near = jnp.sum(f32(before & (big_i // 8 == big_j // 8) & ((own_i & 3) == (own_j & 3))), axis=0, keepdims=True)
    far = jnp.sum(f32(before & (big_i // 32 == big_j // 32) & (own_i == own_j)), axis=0, keepdims=True)
    ids = lax.broadcasted_iota(jnp.int32, (1, 128), 1)
    own = owner_of(band)
    wet_b = band >= 0

    def total(mask, value):
        n = mask.shape[0]
        return jnp.sum(jnp.where(mask, wide(f32(value), n), 0.0), axis=1, keepdims=True)

    slot = lax.broadcasted_iota(jnp.int32, (8, 128), 0)
    ids8 = wide(ids, 8)
    band8 = wide(band, 8)
    hit = band8 == (lat * 16 + lon) * SLOTS + slot
    full = total(hit, jnp.ones_like(band))
    pair = total(hit, ids // 16)
    got_at = total(hit, ids // 32 * 2) + total(hit, far)
    west_code = total(hit, roll(band, 1))
    east_code = total(hit, roll(band, 127))

    def slot_of(code):
        code = code.astype(jnp.int32)
        return f32(jnp.where(code >= 0, code & 7, 0))

    w_slot, e_slot = slot_of(west_code), slot_of(east_code)
    some = jnp.broadcast_to(ids8 // 16 == slot, (8, 128))
    band_hit = wide(f32(jnp.max(f32(hit), axis=0, keepdims=True)), 8) > 0.0
    first_of = lax.broadcasted_iota(jnp.int32, (8, 1), 0).astype(jnp.float32)
    pair_used = total(some & band_hit, jnp.ones_like(band))
    pair_spare = jnp.min(jnp.where(pair_used > 0.0, 99.0, first_of), axis=0, keepdims=True)
    my_tile = ids // TILE == lon
    tile_mask = (ids8 // TILE == lon) & (ids8 - TILE * lon == slot)
    t_wet = total(tile_mask & (band8 >= 0), jnp.ones_like(band))
    t_own = total(tile_mask & (band8 >= 0), own)
    z_key = (own & 3) * 2 + near.astype(jnp.int32)
    z_at = total(tile_mask & (band8 >= 0), z_key)
    z_used = total(wide(my_tile & wet_b, 8) & (wide(z_key, 8) == slot), jnp.ones_like(band))
    z_spare = jnp.min(jnp.where(z_used > 0.0, 99.0, first_of), axis=0, keepdims=True)
    z_at = jnp.where(t_wet > 0.0, z_at, jnp.minimum(z_spare, 7.0))
    t_first = lax.broadcasted_iota(jnp.int32, (16, 1), 0).astype(jnp.float32)
    row16 = lax.broadcasted_iota(jnp.int32, (16, 128), 0)
    in_tile = wide(my_tile & wet_b, 16)
    to_me = jnp.max(f32(hit), axis=0, keepdims=True)
    src_used = total((wide(ids // TILE, 16) == row16) & (wide(to_me, 16) > 0.0), jnp.ones_like(band))
    src_spare = jnp.min(jnp.where(src_used > 0.0, 99.0, t_first), axis=0, keepdims=True)
    src = total(hit, ids // TILE)
    fields = (w_slot, e_slot, full, pair, jnp.where(full > 0.0, pair, jnp.minimum(pair_spare, 7.0)),
              jnp.where(full > 0.0, src, src_spare), t_own, z_at, got_at)
    acc = jnp.zeros((8, 128), jnp.float32)
    for i, v in enumerate(fields):
        acc = jnp.where(ids8 == i, v, acc)
    tab[...] = acc.astype(jnp.int32)
    ids16 = wide(ids, 16)
    here = (ids16 // 16 == lon // 2) & wide(wet_b, 16) & (wide(own, 16) == row16)
    acc = jnp.zeros((16, 128), jnp.float32)
    for i, other in enumerate((ints(south), ints(north))):
        both = here & (wide(other, 16) >= 0)
        acc = jnp.where(ids16 == 2 * i, total(both, owner_of(other)), acc)
        acc = jnp.where(ids16 == 2 * i + 1, total(both, jnp.ones_like(band)), acc)
    mine = wet_b & (ids // 32 == lon // 4) & ((own & 3) == lax.rem(lon, 4))
    y_key = lax.shift_right_arithmetic(own, 2) * 2 + far.astype(jnp.int32)
    turn = wide(mine, 16) & (wide(y_key, 16) == row16)
    acc = jnp.where(ids16 == 4, total(turn, (ids // 8 & 3) * 2 + near.astype(jnp.int32)), acc)
    meet[...] = acc.astype(jnp.int32)


def prep(base, south, north, west, east, light):
    flags, tab, meet = pl.pallas_call(
        prep_kernel,
        in_specs=[pl.BlockSpec(memory_space=VM)] * 6,
        out_specs=[pl.BlockSpec(memory_space=VM)] * 3,
        out_shape=[jax.ShapeDtypeStruct((128, 128), jnp.float32),
                   jax.ShapeDtypeStruct((8, 128), jnp.int32),
                   jax.ShapeDtypeStruct((16, 128), jnp.int32)],
        scratch_shapes=[VM((48, 128), jnp.float32)],
        cost_estimate=pl.CostEstimate(flops=10**7, bytes_accessed=10**5, transcendentals=0),
        name="prep",
    )(base, south, north, west, east, light)
    return flags.reshape(SIDE, 8, 128), tab, meet


def shift(x, axis, by):
    n = lax.axis_size(axis)
    return lax.ppermute(x, axis, [(i, (i + by) % n) for i in range(n)])


def swap(x):
    return lax.all_to_all(x, "lon", split_axis=0, concat_axis=0, tiled=True)


def on_device(tracers, phys_fine, mix_coarse, surf_light, land_mask, owner_map):
    wet = land_mask.astype(jnp.float32)
    base = jnp.concatenate([wet, owner_map.astype(jnp.float32)], axis=0)
    flags, tab, meet = prep(base, shift(base, "lat", 1), shift(base, "lat", -1),
                            shift(base, "lon", 1), shift(base, "lon", -1), surf_light)
    y, col = coarse(jnp.swapaxes(phys_fine, 1, 2), jnp.swapaxes(mix_coarse, 1, 2), flags)
    tab, y, col = lax.optimization_barrier((tab, y, col))
    west_col = shift(col, "lon", 1)
    south_row = shift(y[SIDE - 1, 48:96], "lat", 1)
    rows_out, w_out, e_out = pack(tab, tracers)
    came_west = shift(e_out, "lon", 1)
    came_east = shift(w_out, "lon", -1)
    y, rows_out = lax.optimization_barrier((y, rows_out))
    packed = package(tab, y, west_col, south_row)
    rows, phys = halo(True, meet, rows_out, packed)
    phys = phys.reshape(8, PHYS, CELLS)
    current, rows_out, w_out, e_out = step(False, tab, tracers, phys, rows, came_west, came_east)
    rows, came_west, came_east = halo(False, meet, rows_out, w_out, e_out)
    current, light_part = step(True, tab, current, phys, rows, came_west, came_east)
    return current, heat(tab, swap(light_part), wet, surf_light)


def solution(mesh):
    in_specs = (
        P(("lat", "lon"), None, None),
        P("lat", "lon", None),
        P("lat", "lon", None),
        P("lat", "lon"),
        P("lat", "lon"),
        P("lat", None),
    )
    out_specs = (P(("lat", "lon"), None, None), P(None, "lat", "lon"))
    return jax.shard_map(
        on_device, mesh=mesh, in_specs=in_specs, out_specs=out_specs, check_vma=False
    )
```

```python
import functools

import jax
import jax.numpy as jnp
from jax import lax
from jax.experimental import pallas as pl
from jax.experimental.pallas import tpu as pltpu
from jax.sharding import PartitionSpec as P

NTR = 24
LEV = 48
SIDE = 16
CELLS = 256
SLOTS = 8
TILE = 8
PHYS = 224
DIFF = 0.08
VM = pltpu.VMEM
ROWS3 = 3 * LEV
HALF = ROWS3 // 2


def pos(v):
    return jnp.maximum(v, 0.0)


def lanes():
    return lax.broadcasted_iota(jnp.int32, (LEV, 128), 1)


def roll(x, shift):
    return pltpu.roll(x, shift, 1)


def pack_edges(c_ref, rows_ref, w_ref, e_ref, odd):
    lane = lanes()
    group = lane // SIDE
    col = lane % SIDE
    low = lane < SIDE
    for m in range(3):
        blank = jnp.zeros((LEV, 128), jnp.float32)
        ends = [blank, blank]
        both = [blank, blank]
        for g in range(8):
            t = 3 * g + m
            a = c_ref[0, t * LEV:(t + 1) * LEV, 0:128]
            b = c_ref[0, t * LEV:(t + 1) * LEV, 128:256]
            end = jnp.where(low, a, b)
            ends[g % 2] = jnp.where((group == g) | (group == (g + 7) % 8), roll(end, 16 * g) if g else end, ends[g % 2])
            here = (col == 2 * g) | (col == (2 * g + 15) % 16)
            for h, v in enumerate((a, b)):
                both[h] = jnp.where(here, roll(v, 2 * g) if g else v, both[h])
        flat = group % 2 == 0
        put_rows(rows_ref, 0, m, jnp.where(flat, ends[0], ends[1]))
        put_rows(rows_ref, 1, m, jnp.where(flat, ends[1], ends[0]))
        at = slice(m * LEV, (m + 1) * LEV)
        mine = (lane % 2) == odd
        for h in range(2):
            hs = slice(h * 128, (h + 1) * 128)
            turned = roll(both[h], odd)
            w_ref[0, at, hs] = jnp.where(mine, turned, w_ref[0, at, hs])
            e_ref[0, at, hs] = jnp.where(mine, e_ref[0, at, hs], turned)


def put_rows(rows_ref, d, m, x):
    lo = m * LEV
    if lo < HALF:
        n = min(LEV, HALF - lo)
        rows_ref[0, 0, d, lo:lo + n, :] = x[:n]
        if n < LEV:
            rows_ref[0, 1, d, 0:LEV - n, :] = x[n:]
    else:
        rows_ref[0, 1, d, lo - HALF:lo - HALF + LEV, :] = x


def clear_first(odd, *refs):
    @pl.when(odd == 0)
    def _():
        for ref in refs:
            ref[...] = jnp.zeros_like(ref)


def pack_kernel(tab, c_ref, rows_ref, w_ref, e_ref):
    p = pl.program_id(0)
    lane = lanes()
    group = lane // SIDE
    col = lane % SIDE
    even = lane % 2 == 0
    low = lane < SIDE
    flat = group % 2 == 0
    for m in range(3):
        at = slice(m * LEV, (m + 1) * LEV)
        blank = jnp.zeros((LEV, 128), jnp.float32)
        both = [[blank, blank], [blank, blank]]
        for i in range(2):
            ends = [blank, blank]
            for g in range(8):
                t = 3 * g + m
                a = c_ref[i, t * LEV:(t + 1) * LEV, 0:128]
                b = c_ref[i, t * LEV:(t + 1) * LEV, 128:256]
                end = jnp.where(low, a, b)
                ends[g % 2] = jnp.where((group == g) | (group == (g + 7) % 8), roll(end, 16 * g) if g else end, ends[g % 2])
                here = (col == 2 * g) | (col == (2 * g + 15) % 16)
                for h, v in enumerate((a, b)):
                    both[i][h] = jnp.where(here, roll(v, 2 * g) if g else v, both[i][h])
            view = rows_ref.at[pl.ds(tab[2 * p + i, 4], 1)]
            put_rows(view, 0, m, jnp.where(flat, ends[0], ends[1]))
            put_rows(view, 1, m, jnp.where(flat, ends[1], ends[0]))
        for h in range(2):
            hs = slice(h * 128, (h + 1) * 128)
            other = roll(both[1][h], 1)
            w_ref[0, at, hs] = jnp.where(even, both[0][h], other)
            e_ref[0, at, hs] = jnp.where(even, other, both[0][h])


def pack(tab, tracers):
    return pl.pallas_call(
        pack_kernel,
        grid_spec=pltpu.PrefetchScalarGridSpec(
            num_scalar_prefetch=1,
            grid=(SLOTS // 2,),
            in_specs=[pl.BlockSpec((2, NTR * LEV, CELLS), lambda j, tab: (j, 0, 0))],
            out_specs=[
                pl.BlockSpec((8, 2, 2, HALF, 128), lambda j, tab: (0, 0, 0, 0, 0)),
                pl.BlockSpec((1, ROWS3, CELLS), lambda j, tab: (j, 0, 0)),
                pl.BlockSpec((1, ROWS3, CELLS), lambda j, tab: (j, 0, 0)),
            ],
        ),
        out_shape=[
            jax.ShapeDtypeStruct((8, 2, 2, HALF, 128), jnp.float32),
            jax.ShapeDtypeStruct((4, ROWS3, CELLS), jnp.float32),
            jax.ShapeDtypeStruct((4, ROWS3, CELLS), jnp.float32),
        ],
        cost_estimate=pl.CostEstimate(flops=10**7, bytes_accessed=12 * 10**6, transcendentals=0),
        name="pack",
    )(tab, tracers)


def react(get, put, par, warm):
    (carbon_dis, alkalinity, oxygen, nitrate, ammonium, phosphate, silicate, iron_free,
     nano_carbon, diat_carbon, nano_chl, diat_chl, nano_iron, diat_iron, diat_silica,
     micro_zoo, meso_zoo, dissolved_org, small_part, big_part, small_iron, big_iron,
     big_silica, calcite) = [functools.partial(get, t) for t in range(NTR)]
    p_am = pos(ammonium())
    nitrogen = pos(nitrate()) + p_am
    limit_nitro = nitrogen / (0.5 + nitrogen)
    p_ph = pos(phosphate())
    p_fe = pos(iron_free())
    p_si = pos(silicate())
    nutr_nano = jnp.minimum(jnp.minimum(limit_nitro, p_ph / (0.3 + p_ph)), p_fe / (0.2 + p_fe))
    nutr_diat = jnp.minimum(nutr_nano, p_si / (1.0 + p_si))
    nc = nano_carbon()
    dc = diat_carbon()
    wp = warm * par
    prod_nano = 0.1 * wp / (par + 0.5) * nutr_nano * nc
    prod_diat = 0.12 * wp / (par + 1.0) * nutr_diat * dc
    share = (p_am + 0.01) / (nitrogen + 0.02)
    mi = micro_zoo()
    me = meso_zoo()
    graze_nano = 0.08 * warm * mi / (1.0 + pos(nc))
    graze_diat = 0.06 * warm * me / (1.0 + pos(dc))
    loss_nano = graze_nano + 0.02
    loss_diat = graze_diat + 0.02
    eaten_nano = graze_nano * nc
    eaten_diat = graze_diat * dc
    death_micro = 0.03 * mi * pos(mi)
    death_meso = 0.03 * me * pos(me)
    do = dissolved_org()
    sp = small_part()
    bp = big_part()
    remin_doc = 0.03 * warm * do
    remin_poc = 0.02 * warm * sp
    remin_goc = 0.01 * warm * bp
    am = ammonium()
    nitrify = 0.05 * am
    cal = calcite()
    melt_cal = 0.01 * cal
    uptake = prod_nano + prod_diat
    remin = remin_doc + remin_poc + remin_goc
    calcify = 0.02 * prod_nano
    shell = melt_cal - calcify
    put(0, carbon_dis() + remin - uptake + shell)
    su = share * uptake
    fresh = uptake - su
    put(1, alkalinity() + 2.0 * shell + 0.16 * (fresh - nitrify))
    put(2, oxygen() + 1.3 * (uptake - remin) - 0.32 * nitrify)
    put(3, nitrate() + 0.16 * (nitrify - fresh))
    put(4, am + 0.16 * (remin - su - nitrify))
    put(5, phosphate() + 0.01 * (remin - uptake))
    bsi = big_silica()
    melt_si = 0.02 * bsi
    put(6, silicate() + melt_si - 0.15 * prod_diat)
    sfe = small_iron()
    bfe = big_iron()
    melt_sfe = 0.02 * sfe
    melt_bfe = 0.01 * bfe
    put(7, iron_free() + melt_sfe + melt_bfe - 0.005 * uptake)
    put(8, nc + prod_nano - loss_nano * nc)
    put(9, dc + prod_diat - loss_diat * dc)
    x = nano_chl()
    put(10, x + 0.03 * prod_nano - loss_nano * x)
    x = diat_chl()
    put(11, x + 0.03 * prod_diat - loss_diat * x)
    x = nano_iron()
    lost = loss_nano * x
    put(12, x + 0.005 * prod_nano - lost)
    put(20, sfe + lost - melt_sfe)
    x = diat_iron()
    lost = loss_diat * x
    put(13, x + 0.005 * prod_diat - lost)
    put(21, bfe + lost - melt_bfe)
    x = diat_silica()
    lost = loss_diat * x
    put(14, x + 0.15 * prod_diat - lost)
    put(22, bsi + lost - melt_si)
    put(15, mi + 0.3 * eaten_nano - death_micro)
    put(16, me + 0.3 * eaten_diat - death_meso)
    put(17, do + 0.3 * eaten_nano + 0.02 * nc - remin_doc)
    put(18, sp + 0.4 * eaten_nano + death_micro - remin_poc)
    put(19, bp + 0.4 * eaten_diat + 0.02 * dc + death_meso - remin_goc)
    put(23, cal - shell)


def tri():
    i = lax.broadcasted_iota(jnp.int32, (LEV, LEV), 0)
    j = lax.broadcasted_iota(jnp.int32, (LEV, LEV), 1)
    return (j < i).astype(jnp.float32)


def depth(absorb):
    return jnp.dot(tri(), absorb, precision=lax.Precision.HIGHEST,
                   preferred_element_type=jnp.float32)


def slot_step(tab, c_ref, phys, rows, west, east, out, coef, par_ref, cross, along, one, two):
    j = pl.program_id(0)
    w_odd = tab[j, 0] % 2
    e_odd = tab[j, 1] % 2
    lane = lanes()
    col = lane % SIDE
    at_w = col == 0
    at_e = col == SIDE - 1
    low = lane < 16
    high = lane >= 112
    H = (slice(0, 128), slice(128, 256))
    edge = jnp.concatenate([phys[0, 200:224, 0:128], phys[0, 200:224, 128:256]], axis=0)
    sel_r = lax.broadcasted_iota(jnp.int32, (128, 256), 0)
    sel_c = lax.broadcasted_iota(jnp.int32, (128, 256), 1)
    sel = ((sel_c == SIDE * sel_r) & (sel_r < SIDE)).astype(jnp.float32)
    edge_lane = jnp.where(low, edge, 0.0)
    edge_w = jnp.dot(edge_lane, sel, precision=lax.Precision.HIGHEST,
                     preferred_element_type=jnp.float32)
    edge_s = roll(edge, 112)
    fn_up = roll(phys[0, 48:96, H[0]], 16)
    level = lax.broadcasted_iota(jnp.int32, (LEV, 128), 0)
    for h in range(2):
        fe = phys[0, 0:48, H[h]]
        fn = phys[0, 48:96, H[h]]
        fw = jnp.where(at_w, edge_w[:, H[h]], roll(fe, 1))
        if h == 0:
            fs = jnp.where(low, edge_s, fn_up)
        else:
            fs = jnp.where(low, fn_up, roll(fn, 16))
        ow = DIFF * phys[0, 192:193, H[h]]
        oe = DIFF * phys[0, 193:194, H[h]]
        os = DIFF * phys[0, 194:195, H[h]]
        on = DIFF * phys[0, 195:196, H[h]]
        coef[0, :, H[h]] = (1.0 - (ow + oe + os + on)) - pos(fe) + jnp.minimum(fw, 0.0) - pos(fn) + jnp.minimum(fs, 0.0)
        coef[1, :, H[h]] = oe - jnp.minimum(fe, 0.0)
        coef[2, :, H[h]] = ow + pos(fw)
        coef[3, :, H[h]] = on - jnp.minimum(fn, 0.0)
        coef[4, :, H[h]] = os + pos(fs)
        below = jnp.where(level < LEV - 1, phys[0, 144:192, H[h]], 0.0)
        coef[5, :, H[h]] = below

    wide = lax.broadcasted_iota(jnp.int32, (HALF, 128), 1)
    flat = (wide // SIDE) % 2 == 0
    for p in range(2):
        hp = slice(p * HALF, (p + 1) * HALF)
        upper = rows[0, p, 1, :, :]
        under = roll(rows[0, p, 0, :, :], 32)
        cross[0, hp, :] = jnp.where(flat, upper, under)
        cross[1, hp, :] = jnp.where(flat, under, upper)
        for h in range(2):
            along[hp, H[h]] = jnp.where(wide % 2 == 0, roll(west[0, hp, H[h]], 128 - 15 - w_odd),
                                        roll(east[0, hp, H[h]], 15 - e_odd))

    def where(g, m):
        return pl.ds(pl.multiple_of((3 * g + m) * LEV, LEV), LEV)

    def turn_to(g, m, around):
        hm = slice(m * LEV, (m + 1) * LEV)
        a = c_ref[0, where(g, m), H[0]]
        b = c_ref[0, where(g, m), H[1]]
        ends = roll(cross[lax.rem(g, 2), hm, :], 112 - 16 * g)
        an, bn = roll(a, 112), roll(b, 112)
        as_, bs = roll(a, 16), roll(b, 16)
        around[m, 0, :, H[0]] = jnp.where(high, bn, an)
        around[m, 0, :, H[1]] = jnp.where(high, ends, bn)
        around[m, 1, :, H[0]] = jnp.where(low, ends, as_)
        around[m, 1, :, H[1]] = jnp.where(low, as_, bs)
        for h, v in enumerate((a, b)):
            sides = roll(along[hm, H[h]], lax.rem(128 - 2 * g, 128))
            around[m, 2, :, H[h]] = jnp.where(at_w, sides, roll(v, 1))
            around[m, 3, :, H[h]] = jnp.where(at_e, sides, roll(v, 127))

    def move(g, m, around):
        for h in range(2):
            v = c_ref[0, where(g, m), H[h]]
            moved = (coef[0, :, H[h]] * v + coef[1, :, H[h]] * around[m, 3, :, H[h]]
                     + coef[2, :, H[h]] * around[m, 2, :, H[h]]
                     + coef[3, :, H[h]] * around[m, 0, :, H[h]] + coef[4, :, H[h]] * around[m, 1, :, H[h]])
            flux = coef[5, :, H[h]] * (pltpu.roll(moved, LEV - 1, 0) - moved)
            out[0, where(g, m), H[h]] = moved + flux - pltpu.roll(flux, 1, 0)

    for m in range(3):
        turn_to(0, m, one)

    def pair(i, carry):
        for now, then, g in ((one, two, 2 * i), (two, one, 2 * i + 1)):
            for m in range(3):
                move(g, m, now)
                turn_to(jnp.minimum(g + 1, 7), m, then)
        return carry

    lax.fori_loop(0, 4, pair, 0)
    absorb = 0.04 + 0.02 * (pos(out[0, 480:528, :]) + pos(out[0, 528:576, :]))
    above = depth(absorb)
    par_ref[...] = phys[0, 196:197, :] * jnp.exp(-(above + 0.5 * absorb))
    wets = [jnp.broadcast_to(phys[0, 197:198, H[h]], (8, 128)) for h in range(2)]

    def chunk(i, carry):
        l0 = pl.multiple_of(i * 8, 8)
        for h in range(2):

            def get(t, h=h):
                return out[0, pl.ds(pl.multiple_of(t * LEV + l0, 8), 8), H[h]]

            def put(t, v, h=h):
                out[0, pl.ds(pl.multiple_of(t * LEV + l0, 8), 8), H[h]] = v * wets[h]

            held = [get(t) for t in range(NTR)]
            warm = jnp.exp(0.0639 * phys[0, pl.ds(pl.multiple_of(96 + l0, 8), 8), H[h]])
            par = par_ref[pl.ds(l0, 8), H[h]]
            react(lambda t, held=held: held[t], put, par, warm)
        return carry

    lax.fori_loop(0, LEV // 8, chunk, 0)


def first_kernel(tab, c_ref, phys, rows, west, east, out, rows_out, w_out, e_out, coef, par_ref, cross, along, one, two):
    j = pl.program_id(0)
    odd = j % 2

    @pl.when(tab[j, 2] == 1)
    def _():
        slot_step(tab, c_ref, phys, rows, west, east, out, coef, par_ref, cross, along, one, two)

    @pl.when(tab[j, 2] == 0)
    def _():
        out[...] = jnp.zeros_like(out)

    clear_first(odd, w_out, e_out)
    pack_edges(out, rows_out, w_out, e_out, odd)


def last_kernel(tab, c_ref, phys, rows, west, east, out, light_out, coef, par_ref, cross, along, one, two):
    j = pl.program_id(0)

    @pl.when(tab[j, 2] == 1)
    def _():
        slot_step(tab, c_ref, phys, rows, west, east, out, coef, par_ref, cross, along, one, two)
        absorb = 0.04 + 0.02 * (pos(out[0, 480:528, :]) + pos(out[0, 528:576, :]))
        above = depth(absorb)
        light_out[0] = jnp.exp(-above) - jnp.exp(-(above + absorb))

    @pl.when(tab[j, 2] == 0)
    def _():
        out[...] = jnp.zeros_like(out)
        light_out[...] = jnp.zeros_like(light_out)


def step(last, tab, current, phys, rows, came_west, came_east):
    edge_spec = pl.BlockSpec((1, ROWS3, CELLS), lambda j, tab: (j // 2, 0, 0))
    edge_shape = jax.ShapeDtypeStruct((4, ROWS3, CELLS), jnp.float32)
    if last:
        outs = [pl.BlockSpec((1, LEV, CELLS), lambda j, tab: (tab[j, 5], 0, 0))]
        shapes = [jax.ShapeDtypeStruct((16, LEV, CELLS), jnp.float32)]
    else:
        outs = [pl.BlockSpec((1, 2, 2, HALF, 128), lambda j, tab: (tab[j, 4], 0, 0, 0, 0)), edge_spec, edge_spec]
        shapes = [jax.ShapeDtypeStruct((8, 2, 2, HALF, 128), jnp.float32), edge_shape, edge_shape]
    return pl.pallas_call(
        last_kernel if last else first_kernel,
        grid_spec=pltpu.PrefetchScalarGridSpec(
            num_scalar_prefetch=1,
            grid=(SLOTS,),
            in_specs=[
                pl.BlockSpec((1, NTR * LEV, CELLS), lambda j, tab: (j, 0, 0)),
                pl.BlockSpec((1, PHYS, CELLS), lambda j, tab: (tab[j, 8], 0, 0)),
                pl.BlockSpec((1, 2, 2, HALF, 128), lambda j, tab: (tab[j, 3], 0, 0, 0, 0)),
                pl.BlockSpec((1, ROWS3, CELLS), lambda j, tab: (tab[j, 0] // 2, 0, 0)),
                pl.BlockSpec((1, ROWS3, CELLS), lambda j, tab: (tab[j, 1] // 2, 0, 0)),
            ],
            out_specs=[pl.BlockSpec((1, NTR * LEV, CELLS), lambda j, tab: (j, 0, 0))] + outs,
            scratch_shapes=[VM((6, LEV, CELLS), jnp.float32), VM((LEV, CELLS), jnp.float32),
                            VM((2, ROWS3, 128), jnp.float32), VM((ROWS3, CELLS), jnp.float32),
                            VM((3, 4, LEV, CELLS), jnp.float32), VM((3, 4, LEV, CELLS), jnp.float32)],
        ),
        out_shape=[jax.ShapeDtypeStruct((SLOTS, NTR * LEV, CELLS), jnp.float32)] + shapes,
        cost_estimate=pl.CostEstimate(flops=10**8, bytes_accessed=25 * 10**6, transcendentals=10**6),
        name="last_step" if last else "first_step",
    )(tab, current, phys, rows, came_west, came_east)


def spread_matrix(shape, lhs_wide, dtype=jnp.bfloat16):
    i = lax.broadcasted_iota(jnp.int32, shape, 0)
    j = lax.broadcasted_iota(jnp.int32, shape, 1)
    return (i // 3 == j if lhs_wide else i == j // 3).astype(dtype)


def coarse_kernel(phys, mix, flags, y_ref, col_ref, every_ref, third_ref):
    step = pl.program_id(0)

    @pl.when(step == 0)
    def _():
        i = lax.broadcasted_iota(jnp.int32, (384, 128), 0)
        j = lax.broadcasted_iota(jnp.int32, (384, 128), 1)
        every_ref[...] = (i // 3 == j).astype(jnp.bfloat16)
        third_ref[...] = (i == 3 * j + 2).astype(jnp.bfloat16)
        col_ref[...] = jnp.zeros_like(col_ref)

    def dot(a, b):
        return jnp.dot(a, b, preferred_element_type=jnp.float32)

    u = jnp.concatenate([phys[f, 0:48, :] for f in range(6)], axis=0)
    vt = jnp.concatenate([phys[2, 48:96, :], phys[5, 48:96, :]] + [phys[f, 96:144, :] for f in range(6)], axis=0)
    east = dot(u, third_ref[...])
    rest = dot(vt, every_ref[...])

    def part(x, n):
        return x[48 * n:48 * n + 48]

    for c in range(2):
        e = (part(east, 3 * c) + part(east, 3 * c + 1) + part(east, 3 * c + 2)) / 3.0 * flags[c, 1:2, :]
        y_ref[c, 0:48, :] = e
        y_ref[c, 48:96, :] = part(rest, c) / 3.0 * flags[c, 3:4, :]
        y_ref[c, 96:144, :] = (part(rest, 3 * c + 2) + part(rest, 3 * c + 3) + part(rest, 3 * c + 4)) / 9.0
        y_ref[c, 144:192, :] = mix[c].astype(jnp.float32)
        y_ref[c, 192:200, :] = flags[c]
        r = 2 * step + c
        col_ref[...] = jnp.where(lanes() == r, roll(e, r + 1), col_ref[...])


def coarse(phys_t, mix_t, flags):
    return pl.pallas_call(
        coarse_kernel,
        grid=(SIDE // 2,),
        in_specs=[
            pl.BlockSpec((6, 144, 384), lambda r: (r, 0, 0)),
            pl.BlockSpec((2, LEV, 128), lambda r: (r, 0, 0)),
            pl.BlockSpec((2, 8, 128), lambda r: (r, 0, 0)),
        ],
        out_specs=[
            pl.BlockSpec((2, 200, 128), lambda r: (r, 0, 0)),
            pl.BlockSpec((LEV, 128), lambda r: (0, 0)),
        ],
        out_shape=[
            jax.ShapeDtypeStruct((SIDE, 200, 128), jnp.float32),
            jax.ShapeDtypeStruct((LEV, 128), jnp.float32),
        ],
        scratch_shapes=[VM((384, 128), jnp.bfloat16), VM((384, 128), jnp.bfloat16)],
        cost_estimate=pl.CostEstimate(flops=10**9, bytes_accessed=8 * 10**6, transcendentals=0),
        name="coarse",
    )(phys_t, mix_t, flags)


def package_kernel(tab, y_ref, col_ref, row_ref, out):
    group = lax.broadcasted_iota(jnp.int32, (8, 128), 1) // SIDE
    places = [tab[k, 7] for k in range(TILE)]

    def chunk(i, carry):
        at = pl.ds(pl.multiple_of(8 * i, 8), 8)
        for h in range(2):
            vals = [y_ref[8 * h + g, at, :] for g in range(8)]
            for d in (1, 2, 4):
                lower = (group // d) % 2 == 0
                for g in range(8):
                    if g & d:
                        continue
                    a, b = vals[g], vals[g + d]
                    vals[g] = jnp.where(lower, a, roll(b, 16 * d))
                    vals[g + d] = jnp.where(lower, roll(a, 128 - 16 * d), b)
            for k in range(TILE):
                out[places[k], at, 128 * h:128 * h + 128] = vals[k]
        return carry

    def chunks(i, carry):
        for c in range(5):
            chunk(5 * i + c, carry)
        return carry

    lax.fori_loop(0, 5, chunks, 0)
    i = lax.broadcasted_iota(jnp.int32, (256, 128), 0)
    j = lax.broadcasted_iota(jnp.int32, (256, 128), 1)
    last = (i == SIDE * j + SIDE - 1).astype(jnp.float32)
    low = lanes() < SIDE
    for k in range(TILE):
        if k:
            west = jnp.dot(out[tab[k - 1, 7], 0:48, :], last, precision=lax.Precision.HIGHEST,
                           preferred_element_type=jnp.float32)
        else:
            west = col_ref[...]
        edge = jnp.where(low, west, roll(row_ref[...], (16 - 16 * k) % 128))
        out[tab[k, 7], 200:224, 0:128] = edge[0:24]
        out[tab[k, 7], 200:224, 128:256] = edge[24:48]


def package(tab, y, col, row):
    return pl.pallas_call(
        package_kernel,
        in_specs=[pl.BlockSpec(memory_space=pltpu.SMEM)] + [pl.BlockSpec(memory_space=VM)] * 3,
        out_specs=pl.BlockSpec(memory_space=VM),
        out_shape=jax.ShapeDtypeStruct((8, PHYS, CELLS), jnp.float32),
        cost_estimate=pl.CostEstimate(flops=10**7, bytes_accessed=4 * 10**6, transcendentals=0),
        name="package",
    )(tab, y, col, row)


MESH = pl.DeviceIdType.MESH


def remote(src, dst, send, recv, where):
    return pltpu.make_async_remote_copy(src_ref=src, dst_ref=dst, send_sem=send, recv_sem=recv,
                                        device_id=where, device_id_type=MESH)


PARTS = 7
PART = PHYS // PARTS
ORDER = (0, 5, 10, 15, 4, 1, 8, 2, 12, 3, 6, 9, 7, 13, 11, 14)


def each(first, last, fn):
    def body(d, carry):
        fn(d)
        return carry

    lax.fori_loop(first, last, body, 0)


def halo_kernel(first, *refs):
    if first:
        tab, up_ref, phys, rows_ref, phys_out, got_s, got_n, pick, turn = refs[:9]
        mid = refs[9:9 + PARTS]
        (up_send, up_recv, dn_send, dn_recv, z_send, z_recv, y_send, y_recv, own, rest, home) = refs[9 + PARTS:]
    else:
        (tab, up_ref, w_ref, e_ref, rows_ref, from_w, from_e, got_s, got_n, pick,
         up_send, up_recv, dn_send, dn_recv, we_send, we_recv, home) = refs
    lat, lon = lax.axis_index("lat"), lax.axis_index("lon")
    bands, count = lax.axis_size("lat"), lax.axis_size("lon")
    sides = (lax.rem(lat + 1, bands), lax.rem(lat + bands - 1, bands))
    row, place = lon // 4, lax.rem(lon, 4)
    got = (got_s, got_n)
    barrier = pltpu.get_barrier_semaphore()

    def ahead(d):
        return lax.rem(row + d // 4, 4) * 4 + lax.rem(place + d % 4, 4)

    def behind(d):
        return lax.rem(row + 4 - d // 4, 4) * 4 + lax.rem(place + 4 - d % 4, 4)

    def greet(d):
        peer = lax.rem(lon + d, count)
        for side in sides:
            pl.semaphore_signal(barrier, inc=1, device_id=(side, peer), device_id_type=MESH)

    each(0, count, greet)
    each(1, count, lambda d: pl.semaphore_signal(
        barrier, inc=1, device_id=(lat, lax.rem(lon + d, count)), device_id_type=MESH))
    pl.semaphore_wait(barrier, 3 * count - 1)

    def up(n, d):
        peer = ahead(d)
        return remote(up_ref.at[peer, 1 - n], got[n].at[lon], up_send.at[n, d], up_recv.at[n, d], (sides[n], peer))

    def up_from(n, d):
        peer = behind(d)
        return remote(up_ref.at[peer, 1 - n], got[n].at[peer], up_send.at[n, d], up_recv.at[n, d], (sides[1 - n], peer))

    def down(n, d):
        peer = ahead(d)
        return remote(pick.at[n, peer], rows_ref.at[lon, n], dn_send.at[n, d], dn_recv.at[n, d], (lat, peer))

    def down_from(n, d):
        peer = behind(d)
        return remote(pick.at[n, peer], rows_ref.at[peer, n], dn_send.at[n, d], dn_recv.at[n, d], (lat, peer))

    def piece(p):
        return pl.ds(p * PART, PART)

    def by_z(p, d):
        z = lax.rem(place + d, 4)
        return remote(phys.at[z, :, piece(p)], mid[p].at[place], z_send.at[p, d], z_recv.at[p, d], (lat, 4 * row + z))

    def from_z(p, d):
        z = lax.rem(place + 4 - d, 4)
        return remote(phys.at[z, :, piece(p)], mid[p].at[z], z_send.at[p, d], z_recv.at[p, d], (lat, 4 * row + z))

    def by_y(p, d):
        y = lax.rem(row + d, 4)
        return remote(turn.at[y, :, piece(p)], phys_out.at[row, :, piece(p)], y_send.at[p, d], y_recv.at[p, d], (lat, 4 * y + place))

    def from_y(p, d):
        y = lax.rem(row + 4 - d, 4)
        return remote(turn.at[y, :, piece(p)], phys_out.at[y, :, piece(p)], y_send.at[p, d], y_recv.at[p, d], (lat, 4 * y + place))

    def at_home(n):
        return pltpu.make_async_copy(pick.at[n, lon], rows_ref.at[lon, n], home.at[n])

    def remain(p):
        return pltpu.make_async_copy(turn.at[row, :, piece(p)], phys_out.at[row, :, piece(p)], rest.at[p])

    def lift(n):
        for d in ORDER:
            up(n, d).start()

    def descend(n):
        for d in ORDER:
            up_from(n, d).wait_recv()

        def choose(o):
            value = got[n][tab[o, 2 * n]]
            pick[n, o] = jnp.where(tab[o, 2 * n + 1] > 0, value, 0.0)

        each(0, count, choose)
        keep = at_home(n)
        keep.start()
        for d in ORDER[1:]:
            down(n, d).start()

    def stay(p):
        return pltpu.make_async_copy(phys.at[place, :, piece(p)], mid[p].at[place], own.at[p])

    def send_z(p):
        for d in (2, 1, 3):
            by_z(p, d).start()
        stay(p).start()

    def send_y(p):
        for d in (1, 2, 3):
            from_z(p, d).wait_recv()
        stay(p).wait()

        def sort(q):
            turn[q // 2, lax.rem(q, 2), piece(p)] = mid[p][tab[q, 4] // 2, lax.rem(tab[q, 4], 2)]

        each(0, 8, sort)
        for d in (2, 1, 3):
            by_y(p, d).start()
        remain(p).start()

    if first:
        send_z(0)
        send_z(1)
        lift(0)
        send_z(2)
        send_z(3)
        lift(1)
        for p in range(4, PARTS):
            send_z(p)
        send_y(0)
        send_y(1)
        descend(0)
        send_y(2)
        send_y(3)
        descend(1)
        for p in range(4, PARTS):
            send_y(p)
    else:
        to_e = remote(e_ref, from_w, we_send.at[0], we_recv.at[0], (lat, lax.rem(lon + 1, count)))
        to_w = remote(w_ref, from_e, we_send.at[1], we_recv.at[1], (lat, lax.rem(lon + count - 1, count)))
        lift(0)
        lift(1)
        descend(0)
        to_e.start()
        to_w.start()
        descend(1)
    for n in range(2):
        at_home(n).wait()
        for d in ORDER[1:]:
            down_from(n, d).wait_recv()
    for n in range(2):
        for d in ORDER:
            up(n, d).wait_send()
        for d in ORDER[1:]:
            down(n, d).wait_send()
    if first:
        for p in range(PARTS):
            for d in (1, 2, 3):
                from_y(p, d).wait_recv()
                by_z(p, d).wait_send()
                by_y(p, d).wait_send()
            remain(p).wait()
    else:
        to_e.wait()
        to_w.wait()


def halo(first, tab, rows, *rest):
    anywhere = pl.BlockSpec(memory_space=pl.ANY)
    edge = jax.ShapeDtypeStruct((4, ROWS3, CELLS), jnp.float32)
    dma = pltpu.SemaphoreType.DMA
    sent = pltpu.VMEM((4, 2, PHYS, CELLS), jnp.float32)
    out = [jax.ShapeDtypeStruct((16, 2, HALF, 128), jnp.float32)]
    scratch = [VM((16, HALF, 128), jnp.float32), VM((16, HALF, 128), jnp.float32),
               VM((2, 16, HALF, 128), jnp.float32)]
    sems = [dma((2, 16)), dma((2, 16)), dma((2, 16)), dma((2, 16))]
    if first:
        in_specs, out_specs = [anywhere], [anywhere, anywhere]
        out.append(jax.ShapeDtypeStruct((4, 2, PHYS, CELLS), jnp.float32))
        scratch += [sent] + [VM((4, 2, PART, CELLS), jnp.float32)] * PARTS
        scratch += sems + [dma((PARTS, 4))] * 4 + [dma((PARTS,)), dma((PARTS,)), dma((2,))]
        rest = [rest[0].reshape(4, 2, PHYS, CELLS)]
    else:
        in_specs, out_specs = [anywhere] * 2, [anywhere] * 3
        out += [edge, edge]
        scratch += sems + [dma((2,)), dma((2,)), dma((2,))]
    rows, *more = pl.pallas_call(
        functools.partial(halo_kernel, first),
        in_specs=[pl.BlockSpec(memory_space=pltpu.SMEM), anywhere] + in_specs,
        out_specs=out_specs,
        out_shape=out,
        scratch_shapes=scratch,
        compiler_params=pltpu.CompilerParams(collective_id=1 if first else 2, has_side_effects=True),
        cost_estimate=pl.CostEstimate(flops=10**6, bytes_accessed=10**8, transcendentals=0),
        name="halo_phys" if first else "halo",
    )(tab, rows.reshape(16, 2, HALF, 128), *rest)
    return [rows.reshape(8, 2, 2, HALF, 128)] + more


def heat_kernel(tab, got, wet, light, out, fine):
    lane = lanes()
    group = lane // SIDE
    for r in range(SIDE):
        half = slice(128 * (r // 8), 128 * (r // 8) + 128)
        acc = jnp.zeros((LEV, 128), jnp.float32)
        for k in range(TILE):
            acc = jnp.where(group == k, roll(got[tab[k, 6], :, half], (16 * k - 16 * (r % 8)) % 128), acc)
        acc = jnp.where(wet[r:r + 1, :] > 0.0, acc, 0.0)
        for a in range(3):
            fine[pl.ds(3 * r + a, LEV, stride=LEV), :] = acc
    spread = spread_matrix((128, 384), False)
    stacked = jnp.concatenate([spread] * 3, axis=0)

    def levels(i, carry):
        x = fine[pl.ds(pl.multiple_of(i * 8 * LEV, 8 * LEV), 8 * LEV), :]
        high = x.astype(jnp.bfloat16)
        rest = x - high.astype(jnp.float32)
        mid = rest.astype(jnp.bfloat16)
        low = (rest - mid.astype(jnp.float32)).astype(jnp.bfloat16)
        wide = jnp.dot(jnp.concatenate([high, mid, low], axis=1), stacked,
                       preferred_element_type=jnp.float32)
        for l in range(8):
            out[8 * i + l] = (light[...] * wide[l * LEV:l * LEV + LEV]).astype(jnp.bfloat16)
        return carry

    lax.fori_loop(0, LEV // 8, levels, 0)


def heat(tab, got, wet, light):
    return pl.pallas_call(
        heat_kernel,
        in_specs=[pl.BlockSpec(memory_space=pltpu.SMEM)] + [pl.BlockSpec(memory_space=VM)] * 3,
        out_specs=pl.BlockSpec(memory_space=VM),
        out_shape=jax.ShapeDtypeStruct((LEV, 48, 384), jnp.bfloat16),
        scratch_shapes=[VM((LEV * LEV, 128), jnp.float32)],
        cost_estimate=pl.CostEstimate(flops=10**9, bytes_accessed=3 * 10**6, transcendentals=0),
        name="heat",
    )(tab, got, wet, light)


def prep_kernel(base, south, north, west, east, light, flags, tab, meet, sums):
    lat, lon = lax.axis_index("lat"), lax.axis_index("lon")
    wet = base[0:16, :]
    lane = lax.broadcasted_iota(jnp.int32, (SIDE, 128), 1)
    line = lax.broadcasted_iota(jnp.int32, (SIDE, 128), 0)
    wet_e = jnp.where(lane == 127, roll(east[0:16, :], 127), roll(wet, 127))
    wet_w = jnp.where(lane == 0, roll(west[0:16, :], 1), roll(wet, 1))
    inner_n = (lat < lax.axis_size("lat") - 1).astype(jnp.float32)
    inner_s = (lat > 0).astype(jnp.float32)
    wet_n = jnp.where(line == 15, inner_n * north[0:1, :], pltpu.roll(wet, 15, 0))
    wet_s = jnp.where(line == 0, inner_s * south[15:16, :], pltpu.roll(wet, 1, 0))
    sums[...] = jnp.dot(light[...], spread_matrix((384, 128), True, jnp.float32),
                        precision=lax.Precision.HIGHEST, preferred_element_type=jnp.float32)
    mean = sums[pl.ds(0, 16, stride=3), :] + sums[pl.ds(1, 16, stride=3), :] + sums[pl.ds(2, 16, stride=3), :]
    values = (wet * wet_w, wet * wet_e, wet * wet_s, wet * wet_n, mean / 9.0, wet,
              jnp.zeros_like(wet), jnp.zeros_like(wet))
    for i, v in enumerate(values):
        flags[pl.ds(i, 16, stride=8), :] = v

    def ints(ref):
        return ref[16:17, :].astype(jnp.int32)

    def owner_of(code):
        return lax.shift_right_arithmetic(code, 3) & 15

    def f32(x):
        return x.astype(jnp.float32)

    def wide(x, n):
        return jnp.broadcast_to(x, (n, 128))

    band = ints(base)
    big_i = lax.broadcasted_iota(jnp.int32, (128, 128), 0)
    big_j = lax.broadcasted_iota(jnp.int32, (128, 128), 1)
    down = jnp.sum(jnp.where(big_i == big_j, f32(wide(band, 128)), 0.0), axis=1, keepdims=True).astype(jnp.int32)
    down = jnp.broadcast_to(down, (128, 128))
    own_i, own_j = owner_of(down), owner_of(wide(band, 128))
    before = (big_i < big_j) & (down >= 0)
    near = jnp.sum(f32(before & (big_i // 8 == big_j // 8) & ((own_i & 3) == (own_j & 3))), axis=0, keepdims=True)
    far = jnp.sum(f32(before & (big_i // 32 == big_j // 32) & (own_i == own_j)), axis=0, keepdims=True)
    ids = lax.broadcasted_iota(jnp.int32, (1, 128), 1)
    own = owner_of(band)
    wet_b = band >= 0

    def total(mask, value):
        n = mask.shape[0]
        return jnp.sum(jnp.where(mask, wide(f32(value), n), 0.0), axis=1, keepdims=True)

    slot = lax.broadcasted_iota(jnp.int32, (8, 128), 0)
    ids8 = wide(ids, 8)
    band8 = wide(band, 8)
    hit = band8 == (lat * 16 + lon) * SLOTS + slot
    full = total(hit, jnp.ones_like(band))
    pair = total(hit, ids // 16)
    got_at = total(hit, ids // 32 * 2) + total(hit, far)
    west_code = total(hit, roll(band, 1))
    east_code = total(hit, roll(band, 127))

    def slot_of(code):
        code = code.astype(jnp.int32)
        return f32(jnp.where(code >= 0, code & 7, 0))

    w_slot, e_slot = slot_of(west_code), slot_of(east_code)
    some = jnp.broadcast_to(ids8 // 16 == slot, (8, 128))
    band_hit = wide(f32(jnp.max(f32(hit), axis=0, keepdims=True)), 8) > 0.0
    first_of = lax.broadcasted_iota(jnp.int32, (8, 1), 0).astype(jnp.float32)
    pair_used = total(some & band_hit, jnp.ones_like(band))
    pair_spare = jnp.min(jnp.where(pair_used > 0.0, 99.0, first_of), axis=0, keepdims=True)
    my_tile = ids // TILE == lon
    tile_mask = (ids8 // TILE == lon) & (ids8 - TILE * lon == slot)
    t_wet = total(tile_mask & (band8 >= 0), jnp.ones_like(band))
    t_own = total(tile_mask & (band8 >= 0), own)
    z_key = (own & 3) * 2 + near.astype(jnp.int32)
    z_at = total(tile_mask & (band8 >= 0), z_key)
    z_used = total(wide(my_tile & wet_b, 8) & (wide(z_key, 8) == slot), jnp.ones_like(band))
    z_spare = jnp.min(jnp.where(z_used > 0.0, 99.0, first_of), axis=0, keepdims=True)
    z_at = jnp.where(t_wet > 0.0, z_at, jnp.minimum(z_spare, 7.0))
    t_first = lax.broadcasted_iota(jnp.int32, (16, 1), 0).astype(jnp.float32)
    row16 = lax.broadcasted_iota(jnp.int32, (16, 128), 0)
    in_tile = wide(my_tile & wet_b, 16)
    to_me = jnp.max(f32(hit), axis=0, keepdims=True)
    src_used = total((wide(ids // TILE, 16) == row16) & (wide(to_me, 16) > 0.0), jnp.ones_like(band))
    src_spare = jnp.min(jnp.where(src_used > 0.0, 99.0, t_first), axis=0, keepdims=True)
    src = total(hit, ids // TILE)
    fields = (w_slot, e_slot, full, pair, jnp.where(full > 0.0, pair, jnp.minimum(pair_spare, 7.0)),
              jnp.where(full > 0.0, src, src_spare), t_own, z_at, got_at)
    acc = jnp.zeros((8, 128), jnp.float32)
    for i, v in enumerate(fields):
        acc = jnp.where(ids8 == i, v, acc)
    tab[...] = acc.astype(jnp.int32)
    ids16 = wide(ids, 16)
    here = (ids16 // 16 == lon // 2) & wide(wet_b, 16) & (wide(own, 16) == row16)
    acc = jnp.zeros((16, 128), jnp.float32)
    for i, other in enumerate((ints(south), ints(north))):
        both = here & (wide(other, 16) >= 0)
        acc = jnp.where(ids16 == 2 * i, total(both, owner_of(other)), acc)
        acc = jnp.where(ids16 == 2 * i + 1, total(both, jnp.ones_like(band)), acc)
    mine = wet_b & (ids // 32 == lon // 4) & ((own & 3) == lax.rem(lon, 4))
    y_key = lax.shift_right_arithmetic(own, 2) * 2 + far.astype(jnp.int32)
    turn = wide(mine, 16) & (wide(y_key, 16) == row16)
    acc = jnp.where(ids16 == 4, total(turn, (ids // 8 & 3) * 2 + near.astype(jnp.int32)), acc)
    meet[...] = acc.astype(jnp.int32)


def prep(base, south, north, west, east, light):
    flags, tab, meet = pl.pallas_call(
        prep_kernel,
        in_specs=[pl.BlockSpec(memory_space=VM)] * 6,
        out_specs=[pl.BlockSpec(memory_space=VM)] * 3,
        out_shape=[jax.ShapeDtypeStruct((128, 128), jnp.float32),
                   jax.ShapeDtypeStruct((8, 128), jnp.int32),
                   jax.ShapeDtypeStruct((16, 128), jnp.int32)],
        scratch_shapes=[VM((48, 128), jnp.float32)],
        cost_estimate=pl.CostEstimate(flops=10**7, bytes_accessed=10**5, transcendentals=0),
        name="prep",
    )(base, south, north, west, east, light)
    return flags.reshape(SIDE, 8, 128), tab, meet


def shift(x, axis, by):
    n = lax.axis_size(axis)
    return lax.ppermute(x, axis, [(i, (i + by) % n) for i in range(n)])


def swap(x):
    return lax.all_to_all(x, "lon", split_axis=0, concat_axis=0, tiled=True)


def on_device(tracers, phys_fine, mix_coarse, surf_light, land_mask, owner_map):
    wet = land_mask.astype(jnp.float32)
    base = jnp.concatenate([wet, owner_map.astype(jnp.float32)], axis=0)
    flags, tab, meet = prep(base, shift(base, "lat", 1), shift(base, "lat", -1),
                            shift(base, "lon", 1), shift(base, "lon", -1), surf_light)
    y, col = coarse(jnp.swapaxes(phys_fine, 1, 2), jnp.swapaxes(mix_coarse, 1, 2), flags)
    tab, y, col = lax.optimization_barrier((tab, y, col))
    west_col = shift(col, "lon", 1)
    south_row = shift(y[SIDE - 1, 48:96], "lat", 1)
    rows_out, w_out, e_out = pack(tab, tracers)
    came_west = shift(e_out, "lon", 1)
    came_east = shift(w_out, "lon", -1)
    y, rows_out = lax.optimization_barrier((y, rows_out))
    packed = package(tab, y, west_col, south_row)
    rows, phys = halo(True, meet, rows_out, packed)
    phys = phys.reshape(8, PHYS, CELLS)
    current, rows_out, w_out, e_out = step(False, tab, tracers, phys, rows, came_west, came_east)
    rows, came_west, came_east = halo(False, meet, rows_out, w_out, e_out)
    current, light_part = step(True, tab, current, phys, rows, came_west, came_east)
    return current, heat(tab, swap(light_part), wet, surf_light)


def solution(mesh):
    in_specs = (
        P(("lat", "lon"), None, None),
        P("lat", "lon", None),
        P("lat", "lon", None),
        P("lat", "lon"),
        P("lat", "lon"),
        P("lat", None),
    )
    out_specs = (P(("lat", "lon"), None, None), P(None, "lat", "lon"))
    return jax.shard_map(
        on_device, mesh=mesh, in_specs=in_specs, out_specs=out_specs, check_vma=False
    )
```
